32 devices in a mesh: member: 2 (over x), patch: 16 (over z, y, core).
Axes of the slice: x: 2, y: 2, z: 4, core: 2. Of those that a mesh axis runs over, the one named last changes fastest.
Arguments:
- log_rate: float32 [65536, 128], P(('member', 'patch')), parts along dimension 0, may hold values from -3 to 3
- log_state: float32 [65536, 128], P(('member', 'patch')), parts along dimension 0, may hold values from -3 to 3
- near_blocks: bfloat16 [512, 12, 128, 128], P(('member', 'patch')), parts along dimension 0, may hold values from -0.15625 to 0.15625
- near_columns: int32 [512, 12], P(('member', 'patch')), parts along dimension 0, may hold values from 0 to 255, as said below
- far_basis: bfloat16 [8, 32, 32768], P('member', None, 'patch'), parts along dimension 0, may hold values from -0.0625 to 0.0625
- far_coupling: bfloat16 [8, 32, 32768], P('member', None, 'patch'), parts along dimension 0, may hold values from -0.5 to 0.5
- self_stiffness: float32 [65536], P(('member', 'patch')), parts along dimension 0, may hold values from 1 to 3
- plate_rate: float32 [65536], P(('member', 'patch')), parts along dimension 0, may hold values from 0.5 to 2
- direct_effect: float32 [65536], P(('member', 'patch')), parts along dimension 0, may hold values from 0.3 to 1
- evolution_effect: float32 [65536], P(('member', 'patch')), parts along dimension 0, may hold values from 0.5 to 1.5
- triangle_area: float32 [65536], P(('member', 'patch')), parts along dimension 0, may hold values from 0.5 to 10.5
Outputs:
- new_log_rate: float32 [65536, 128], P(('member', 'patch')), parts along dimension 0
- new_log_state: float32 [65536, 128], P(('member', 'patch')), parts along dimension 0
- error_norm: float32 [256], P('member'), parts along dimension 0
The draws below stay inside these ranges and needn't reach their ends.
There are 2 independent parts, one for each index of `member`. The reference program is written for one: setup_inputs(seed, part) draws one part's arguments, and reference() takes and returns one part's arrays. A program takes and returns all parts, laid end to end along the dimension named above; each array names one. Nothing has to cross between parts.
Inputs may be any that keep to these rules, and one draw needn't show every extreme that they name: `near_columns`: row block r's 12 column blocks are distinct, each is (r + o) mod 256 with -6 <= o <= 6, and they include r itself and both blocks at distance 6.
All inputs are finite; a program needn't handle non-finite values.
Results may differ from the reference program's by a relative error of at most 0.0012.
Values may be sent and summed in bfloat16 or wider, within the bound.
No kernel may reach another device: no remote copies, remote signals or barrier semaphores. Data moves between devices by JAX's collectives and lax.ppermute only.
A program may use at most 128 MiB of HBM per device.

```python
import math
import jax
import jax.numpy as jnp
from jax import lax

BS = 128
R = 32
REACH = 6
NEAR = 12
SCEN = 128
NE_DEV = 2048
NBLK = 256
NE = 32768
LEVELS = 4
N_PATCH = 16


def draw_near_columns(key, part):
    spare_count = 2 * REACH - 2
    row_index = jnp.arange(NBLK, dtype=jnp.int32)
    key_pick, key_order = jax.random.split(key)
    candidates = jnp.concatenate([jnp.arange(-REACH + 1, 0, dtype=jnp.int32), jnp.arange(1, REACH, dtype=jnp.int32)])
    scores = jax.random.randint(key_pick, (NBLK, spare_count), 0, 1048576, dtype=jnp.int32) * spare_count + jnp.arange(spare_count, dtype=jnp.int32)[None, :]
    picked = jnp.take(candidates, jnp.argsort(scores, axis=1)[:, :NEAR - 3])
    fixed_part = jnp.broadcast_to(jnp.array([0, -REACH, REACH], dtype=jnp.int32), (NBLK, 3))
    offsets = jnp.concatenate([fixed_part, picked], axis=1)
    order_scores = jax.random.randint(key_order, (NBLK, NEAR), 0, 1048576, dtype=jnp.int32) * NEAR + jnp.arange(NEAR, dtype=jnp.int32)[None, :]
    offsets = jnp.take_along_axis(offsets, jnp.argsort(order_scores, axis=1), axis=1)
    return ((row_index[:, None] + offsets) % NBLK).astype(jnp.int32)


def draw_triangle_area(key, part):
    along = jnp.arange(NE, dtype=jnp.float32) / (NE - 1)
    rough = jnp.exp(jax.random.uniform(key, (NE,), jnp.float32, -0.35, 0.35))
    return (1.0 + 2.0 * along) * rough


def level_of(key, shape, pieces, low, high):
    level = 1.0
    for dim, shards_of in pieces:
        steps = jax.random.uniform(jax.random.fold_in(jax.random.fold_in(key, 6), dim), (shards_of,), jnp.float32, low / len(pieces), high / len(pieces))
        level = level * jnp.repeat(jnp.exp(steps), shape[dim] // shards_of).reshape((-1,) + (1,) * (len(shape) - 1 - dim))
    return level


def scatter_about(own_key, shape, scale, limit, pieces=(), kind=jnp.bfloat16):
    entries = scale * jax.random.normal(own_key, shape, jnp.float32)
    if pieces:
        entries = entries * level_of(own_key, shape, pieces, -0.22, 0.18)
    return jnp.clip(entries, -limit, limit).astype(kind)


def setup_inputs(seed: int = 0, part: int = 0) -> dict:
    splits = jax.random.split(jax.random.key(seed), 12)
    own_keys = jax.random.split(jax.random.fold_in(splits[11], part), 12)
    log_rate = scatter_about(own_keys[0], (NE, SCEN), 0.7, 3.0, ((0, 16),), jnp.float32)
    log_state = scatter_about(own_keys[1], (NE, SCEN), 0.7, 3.0, ((0, 16),), jnp.float32)
    near_blocks = scatter_about(own_keys[2], (NBLK, NEAR, BS, BS), (NEAR * BS) ** -0.5, 0.15625, ((0, 16),))
    near_columns = draw_near_columns(jax.random.fold_in(jax.random.fold_in(splits[11], part), 71), part)
    far_basis = scatter_about(own_keys[4], (LEVELS, R, NE), (4 * NE_DEV) ** -0.5, 0.0625, ((2, 16),))
    far_coupling = scatter_about(own_keys[5], (LEVELS, R, NE), (R * LEVELS) ** -0.5, 0.5, ((2, 16),))
    self_stiffness = jnp.clip(jnp.exp(math.log(3.0) - 1.0986123 * jax.random.uniform(own_keys[6], (NE,), jnp.float32) ** level_of(own_keys[6], (NE,), ((0, 16),), -0.2, 0.2)), 1.0, 3.0)
    plate_rate = jnp.clip(jnp.exp(math.log(2.0) - 1.3862944 * jax.random.uniform(own_keys[7], (NE,), jnp.float32) ** level_of(own_keys[7], (NE,), ((0, 16),), -0.2, 0.2)), 0.5, 2.0)
    direct_effect = jnp.clip(jnp.exp(math.log(1.0) - 1.2039728 * jax.random.uniform(own_keys[8], (NE,), jnp.float32) ** level_of(own_keys[8], (NE,), ((0, 16),), -0.2, 0.2)), 0.3, 1.0)
    evolution_effect = jnp.clip(jnp.exp(math.log(1.5) - 1.0986123 * jax.random.uniform(own_keys[9], (NE,), jnp.float32) ** level_of(own_keys[9], (NE,), ((0, 16),), -0.2, 0.2)), 0.5, 1.5)
    triangle_area = draw_triangle_area(jax.random.fold_in(jax.random.fold_in(splits[11], part), 71), part)
    return dict(log_rate=log_rate, log_state=log_state, near_blocks=near_blocks, near_columns=near_columns, far_basis=far_basis, far_coupling=far_coupling, self_stiffness=self_stiffness, plate_rate=plate_rate, direct_effect=direct_effect, evolution_effect=evolution_effect, triangle_area=triangle_area)


step_size = 0.1
damping = 0.5
error_scale = 0.01

def near_stress(rate_bf, near_blocks, near_columns):
    column_blocks = rate_bf.reshape(NBLK, BS, SCEN)

    def one_block(block_item):
        blocks, columns = block_item
        chosen = column_blocks[columns.astype(jnp.int32)]
        return jnp.einsum('kij,kjb->ib', blocks.astype(jnp.float32), chosen.astype(jnp.float32))
    result_rows = lax.map(one_block, (near_blocks, near_columns))
    return result_rows.reshape(NE, SCEN)

def far_stress(rate_bf, far_basis, far_coupling):
    leaves = rate_bf.reshape(N_PATCH, NE_DEV, SCEN).astype(jnp.float32)
    basis_four = far_basis.reshape(LEVELS, R, N_PATCH, NE_DEV).astype(jnp.float32)
    projected = jnp.einsum('lkci,cib->lckb', basis_four, leaves)
    coupled = []
    for tree_level in range(LEVELS):
        group_span = 2 ** tree_level
        group_sums = projected[tree_level].reshape(N_PATCH // (2 * group_span), 2, group_span, R, SCEN).sum(axis=2)
        sibling = group_sums[:, ::-1].reshape(N_PATCH // group_span, R, SCEN)
        coupled.append(jnp.repeat(sibling, group_span, axis=0))
    coupled = lax.optimization_barrier(jnp.stack(coupled).astype(jnp.bfloat16))
    coupling = far_coupling.reshape(LEVELS, R, N_PATCH, NE_DEV).astype(jnp.float32)
    result_rows = jnp.einsum('lkci,lckb->cib', coupling, coupled.astype(jnp.float32))
    return result_rows.reshape(NE, SCEN)

def section_rates(log_rate, log_state, near_blocks, near_columns, far_basis, far_coupling, self_stiffness, plate_rate, direct_effect, evolution_effect):
    velocity = jnp.exp(log_rate)
    rate_bf = lax.optimization_barrier(velocity.astype(jnp.bfloat16))
    near_term = near_stress(rate_bf, near_blocks, near_columns)
    far_term = far_stress(rate_bf, far_basis, far_coupling)
    stress_rate = self_stiffness[:, None] * (plate_rate[:, None] - velocity) - near_term - far_term
    state_rate = jnp.exp(-log_state) - velocity
    log_rate_rate = (stress_rate - evolution_effect[:, None] * state_rate) / (direct_effect[:, None] + damping * velocity)
    return (log_rate_rate, state_rate)

def reference(log_rate, log_state, near_blocks, near_columns, far_basis, far_coupling, self_stiffness, plate_rate, direct_effect, evolution_effect, triangle_area):
    fixed_args = (near_blocks, near_columns, far_basis, far_coupling, self_stiffness, plate_rate, direct_effect, evolution_effect)
    rate_one, state_one = section_rates(log_rate, log_state, *fixed_args)
    rate_two, state_two = section_rates(log_rate + step_size * rate_one, log_state + step_size * state_one, *fixed_args)
    half_step = 0.5 * step_size
    new_log_rate = log_rate + half_step * (rate_one + rate_two)
    new_log_state = log_state + half_step * (state_one + state_two)
    rate_error = half_step * (rate_two - rate_one) / error_scale
    state_error = half_step * (state_two - state_one) / error_scale
    totals = lax.optimization_barrier(jnp.sum(triangle_area[:, None] * (rate_error * rate_error + state_error * state_error), axis=0))
    area_total = jnp.sum(triangle_area)
    error_norm = jnp.sqrt(totals / area_total + 1e-06)
    return (new_log_rate, new_log_state, error_norm)
```

```python
import functools

import jax
import jax.numpy as jnp
from jax import lax
from jax.experimental import pallas as pl
from jax.experimental.pallas import tpu as pltpu
from jax.sharding import PartitionSpec as P

REACH = 6

step_size = 0.1
damping = 0.5
error_scale = 0.01
half_step = 0.5 * step_size

AXIS = "patch"
F32 = jnp.float32
BF16 = jnp.bfloat16
WHOLE = pl.BlockSpec(memory_space=pltpu.VMEM)
SCALARS = pl.BlockSpec(memory_space=pltpu.SMEM)


def on_chip(*shapes):
    return tuple(pltpu.VMEM(shape, dtype) for shape, dtype in shapes)


def params(limit_mib):
    return pltpu.CompilerParams(vmem_limit_bytes=limit_mib * 1024 * 1024)


def cost(flops, moved, exps=0):
    return pl.CostEstimate(flops=flops, bytes_accessed=moved, transcendentals=exps)


def send_out(me, x, projected, slots, side_a, side_b):
    row_blocks = x.shape[0] - 1
    devices, rank, _ = slots.shape
    odd = lax.rem(me, 2)
    start_a = (1 - odd) * (row_blocks - REACH)
    start_b = odd * (row_blocks - REACH)
    for t in range(REACH):
        side_a[t] = x[start_a + t]
        side_b[t] = x[start_b + t]
    for m in range(devices):
        level = max(m.bit_length() - 1, 0)
        slots[me ^ m] = projected[level * rank : (level + 1) * rank].astype(slots.dtype)


def open_kernel(me_ref, p_ref, basis_ref, x, slots, side_a, side_b):
    row_blocks, size, cols = p_ref.shape
    group = 2 if row_blocks % 2 == 0 else 1
    projected = jnp.zeros((basis_ref.shape[0], cols), F32)
    for r in range(0, row_blocks, group):
        rates = jnp.exp(p_ref[r : r + group]).astype(BF16)
        x[r : r + group] = rates
        projected += jnp.dot(
            basis_ref[:, r * size : (r + group) * size],
            rates.reshape(group * size, cols),
            preferred_element_type=F32,
        )
    x[row_blocks] = jnp.zeros((size, cols), BF16)
    send_out(me_ref[0], x, projected, slots, side_a, side_b)


def local_products(me_ref, columns, x, near, acc, place=None):
    row_blocks, near_count, size, _ = near.shape
    total = row_blocks * me_ref[1]
    first = row_blocks * me_ref[0]

    def row(r, carry):
        picked = []
        for k in range(near_count):
            offset = columns[r, k] - first - r
            offset = jnp.where(offset > REACH, offset - total, offset)
            offset = jnp.where(offset < -REACH, offset + total, offset)
            if place is not None:
                place[r, offset + REACH] = k
            index = r + offset
            inside = jnp.logical_and(index >= 0, index < row_blocks)
            picked.append(x[jnp.where(inside, index, row_blocks)])
        left = jnp.concatenate([near[r, k] for k in range(near_count)], axis=1)
        acc[r] = jnp.dot(left, jnp.concatenate(picked, axis=0), preferred_element_type=F32)
        return carry

    lax.fori_loop(0, row_blocks, row, 0)


def local_kernel(me_ref, columns, x, near, acc):
    local_products(me_ref, columns, x, near, acc)


def edge_rows(row_blocks):
    left = [(r, r) for r in range(min(REACH, row_blocks))]
    right = [(r, r + REACH + 1 - row_blocks) for r in range(max(row_blocks - REACH, 0), row_blocks)]
    return left, right


def first_local_kernel(
    me_ref, columns, x, near, coupling, stiff, plate, direct, evolve, area,
    acc, left_near, right_near, coupling_t, per_row, place,
):
    row_blocks, near_count, size, _ = near.shape
    for r in range(row_blocks):
        for o in range(2 * REACH + 1):
            place[r, o] = -1
    local_products(me_ref, columns, x, near, acc, place)
    left, right = edge_rows(row_blocks)

    def halo_block(r, offset):
        k = place[r, offset + REACH]
        block = near[r, jnp.maximum(k, 0)]
        return jnp.where(k >= 0, block, jnp.zeros_like(block))

    for n, (r, low) in enumerate(left):
        for t in range(low, REACH):
            left_near[n, :, t * size : (t + 1) * size] = halo_block(r, t - REACH - r)
    for n, (r, count) in enumerate(right):
        for t in range(count):
            right_near[n, :, t * size : (t + 1) * size] = halo_block(r, row_blocks + t - r)
    for r in range(row_blocks):
        rows = slice(r * size, (r + 1) * size)
        coupling_t[r] = coupling[:, rows].T
        stacked = jnp.concatenate(
            [v[r : r + 1] for v in (stiff, plate, direct, evolve, area, area, area, area)], axis=0
        )
        per_row[r] = stacked.T


def add_halo(me, got_a, got_b, halo, left_near, right_near, acc):
    row_blocks, size, cols = acc.shape
    odd = lax.rem(me, 2)
    at_a = (1 - odd) * REACH
    at_b = odd * REACH
    for t in range(REACH):
        halo[at_a + t] = got_a[t]
        halo[at_b + t] = got_b[t]
    left, right = edge_rows(row_blocks)
    for n, (r, low) in enumerate(left):
        blocks = halo[low:REACH].reshape((REACH - low) * size, cols)
        acc[r] += jnp.dot(left_near[n, :, low * size :], blocks, preferred_element_type=F32)
    for n, (r, count) in enumerate(right):
        blocks = halo[REACH : REACH + count].reshape(count * size, cols)
        acc[r] += jnp.dot(right_near[n, :, : count * size], blocks, preferred_element_type=F32)


def couple(me, got, levels):
    devices = got.shape[0]
    sums = []
    for level in range(levels):
        total = got[me ^ (1 << level)].astype(F32)
        for m in range((1 << level) + 1, min(2 << level, devices)):
            total += got[me ^ m].astype(F32)
        sums.append(total.astype(BF16))
    return jnp.concatenate(sums, axis=0)


def rates_of(p, s, near_far, rows):
    stiff, plate, direct, evolve = (rows[:, q : q + 1] for q in range(4))
    velocity = jnp.exp(p)
    stress = stiff * (plate - velocity) - near_far
    state = jnp.exp(-s) - velocity
    return (stress - evolve * state) / (direct + damping * velocity), state


def middle_kernel(
    me_ref, acc_in, got_a, got_b, got, left_near, right_near, coupling_t, per_row, p_ref, s_ref, basis_ref,
    rate_one, state_one, x, slots, side_a, side_b, halo, acc, proj, coupled,
):
    row_blocks, size, cols = p_ref.shape
    me = me_ref[0]
    levels = basis_ref.shape[0] // got.shape[1]
    acc[...] = acc_in[...]
    add_halo(me, got_a, got_b, halo, left_near, right_near, acc)
    coupled[...] = couple(me, got, levels)

    def row(r, carry):
        p, s = p_ref[r], s_ref[r]
        near_far = acc[r] + jnp.dot(coupling_t[r], coupled[...], preferred_element_type=F32)
        rate, state = rates_of(p, s, near_far, per_row[r])
        rate_one[r] = rate
        state_one[r] = state
        x[r] = jnp.exp(p + step_size * rate).astype(BF16)
        return carry

    lax.fori_loop(0, row_blocks, row, 0)
    x[row_blocks] = jnp.zeros((size, cols), BF16)
    projected = jnp.zeros((basis_ref.shape[0], cols), F32)
    group = 2 if row_blocks % 2 == 0 else 1
    for r in range(0, row_blocks, group):
        projected += jnp.dot(
            basis_ref[:, r * size : (r + group) * size],
            x[r : r + group].reshape(group * size, cols),
            preferred_element_type=F32,
        )
    send_out(me, x, projected, slots, side_a, side_b)


def close_kernel(
    me_ref, acc_in, got_a, got_b, got, left_near, right_near, coupling_t, per_row, p_ref, s_ref, rate_one, state_one,
    new_p, new_s, parts, halo, acc, coupled,
):
    row_blocks, size, cols = p_ref.shape
    me = me_ref[0]
    levels = coupling_t.shape[2] // got.shape[1]
    acc[...] = acc_in[...]
    add_halo(me, got_a, got_b, halo, left_near, right_near, acc)
    coupled[...] = couple(me, got, levels)

    def row(r, carry):
        errors, areas = carry
        p, s = p_ref[r], s_ref[r]
        rate_a, state_a = rate_one[r], state_one[r]
        rows = per_row[r]
        near_far = acc[r] + jnp.dot(coupling_t[r], coupled[...], preferred_element_type=F32)
        rate_b, state_b = rates_of(p + step_size * rate_a, s + step_size * state_a, near_far, rows)
        new_p[r] = p + half_step * (rate_a + rate_b)
        new_s[r] = s + half_step * (state_a + state_b)
        rate_error = half_step * (rate_b - rate_a) / error_scale
        state_error = half_step * (state_b - state_a) / error_scale
        area = jnp.broadcast_to(rows[:, 4:5], (size, cols))
        weighted = area * (rate_error * rate_error + state_error * state_error)
        errors += jnp.sum(weighted.reshape(size // 8, 8, cols), axis=0)
        areas += jnp.sum(area.reshape(size // 8, 8, cols), axis=0)
        return errors, areas

    zero = jnp.zeros((8, cols), F32)
    errors, areas = lax.fori_loop(0, row_blocks, row, (zero, zero))
    both = jnp.concatenate(
        [jnp.sum(errors, axis=0, keepdims=True), jnp.sum(areas, axis=0, keepdims=True)], axis=0
    )
    for j in range(parts.shape[0]):
        parts[j] = both


def exchange(x, side_a, side_b, slots):
    count = lax.axis_size(AXIS)
    got_a = lax.ppermute(side_a, AXIS, [(i, i ^ 1) for i in range(count)])
    pairs = [(i, (i - 1) % count if i % 2 == 0 else (i + 1) % count) for i in range(count)]
    got_b = lax.ppermute(side_b, AXIS, pairs)
    got = lax.all_to_all(slots, AXIS, 0, 0)
    return got_a, got_b, got


def on_device(
    log_rate,
    log_state,
    near_blocks,
    near_columns,
    far_basis,
    far_coupling,
    self_stiffness,
    plate_rate,
    direct_effect,
    evolution_effect,
    triangle_area,
):
    rows, cols = log_rate.shape
    row_blocks, near_count, size, _ = near_blocks.shape
    levels, rank, _ = far_basis.shape
    devices = lax.axis_size(AXIS)
    me = jnp.stack([lax.axis_index(AXIS), jnp.int32(devices)]).astype(jnp.int32)
    p = log_rate.reshape(row_blocks, size, cols)
    s = log_state.reshape(row_blocks, size, cols)
    basis = far_basis.reshape(levels * rank, rows)
    coupling = far_coupling.reshape(levels * rank, rows)
    vectors = [
        v.reshape(row_blocks, size)
        for v in (self_stiffness, plate_rate, direct_effect, evolution_effect, triangle_area)
    ]
    state = (row_blocks, size, cols)
    outgoing = (
        ((row_blocks + 1, size, cols), BF16),
        ((devices, rank, cols), BF16),
        ((REACH, size, cols), BF16),
        ((REACH, size, cols), BF16),
    )
    near_flops = 2 * rows * near_count * size * cols

    x, slots, side_a, side_b = pl.pallas_call(
        open_kernel,
        out_shape=on_chip(*outgoing),
        in_specs=[SCALARS, WHOLE, WHOLE],
        out_specs=(WHOLE,) * 4,
        compiler_params=params(16),
        name="open",
    )(me, p, basis)

    got_a, got_b, got = exchange(x, side_a, side_b, slots)
    acc, left_near, right_near, coupling_t, per_row = pl.pallas_call(
        first_local_kernel,
        out_shape=on_chip(
            (state, F32),
            ((min(REACH, row_blocks), size, REACH * size), BF16),
            ((min(REACH, row_blocks), size, REACH * size), BF16),
            ((row_blocks, size, levels * rank), BF16),
            ((row_blocks, size, 8), F32),
        ),
        in_specs=[SCALARS, SCALARS] + [WHOLE] * 8,
        out_specs=(WHOLE,) * 5,
        scratch_shapes=[pltpu.SMEM((row_blocks, 2 * REACH + 1), jnp.int32)],
        compiler_params=params(16),
        cost_estimate=cost(near_flops, near_blocks.size * 2),
        name="local_one",
    )(me, near_columns, x, near_blocks, coupling, *vectors)

    rate_one, state_one, x, slots, side_a, side_b = pl.pallas_call(
        middle_kernel,
        out_shape=on_chip((state, F32), (state, F32), *outgoing),
        in_specs=[SCALARS] + [WHOLE] * 11,
        out_specs=(WHOLE,) * 6,
        scratch_shapes=[
            pltpu.VMEM((2 * REACH, size, cols), BF16),
            pltpu.VMEM(state, F32),
            pltpu.VMEM((levels * rank, cols), F32),
            pltpu.VMEM((levels * rank, cols), BF16),
        ],
        compiler_params=params(16),
        name="middle",
    )(me, acc, got_a, got_b, got, left_near, right_near, coupling_t, per_row, p, s, basis)

    got_a, got_b, got = exchange(x, side_a, side_b, slots)
    acc = pl.pallas_call(
        local_kernel,
        out_shape=on_chip((state, F32))[0],
        in_specs=[SCALARS, SCALARS, WHOLE, WHOLE],
        out_specs=WHOLE,
        compiler_params=params(16),
        cost_estimate=cost(near_flops, near_blocks.size * 2),
        name="local_two",
    )(me, near_columns, x, near_blocks)

    new_p, new_s, parts = pl.pallas_call(
        close_kernel,
        out_shape=on_chip((state, F32), (state, F32), ((devices, 2, cols), F32)),
        in_specs=[SCALARS] + [WHOLE] * 12,
        out_specs=(WHOLE,) * 3,
        scratch_shapes=[
            pltpu.VMEM((2 * REACH, size, cols), BF16),
            pltpu.VMEM(state, F32),
            pltpu.VMEM((levels * rank, cols), BF16),
        ],
        compiler_params=params(16),
        name="close",
    )(me, acc, got_a, got_b, got, left_near, right_near, coupling_t, per_row, p, s, rate_one, state_one)

    totals = lax.all_to_all(parts, AXIS, 0, 0).sum(axis=0)
    error_norm = jnp.sqrt(totals[0] / totals[1] + 1e-06)
    return new_p.reshape(rows, cols), new_s.reshape(rows, cols), error_norm


def solution(mesh):
    split = P(("member", "patch"))
    in_specs = (
        P(("member", "patch"), None),
        P(("member", "patch"), None),
        P(("member", "patch"), None, None, None),
        P(("member", "patch"), None),
        P("member", None, "patch"),
        P("member", None, "patch"),
        split,
        split,
        split,
        split,
        split,
    )
    out_specs = (P(("member", "patch"), None), P(("member", "patch"), None), P("member"))
    return jax.shard_map(
        on_device, mesh=mesh, in_specs=in_specs, out_specs=out_specs, check_vma=False
    )
```

```python
import jax
import jax.numpy as jnp
from jax import lax
from jax.experimental import pallas as pl
from jax.experimental.pallas import tpu as pltpu
from jax.sharding import PartitionSpec as P

REACH = 6

step_size = 0.1
damping = 0.5
error_scale = 0.01
half_step = 0.5 * step_size

AXIS = "patch"
F32 = jnp.float32
BF16 = jnp.bfloat16
PLAIN = pl.BlockSpec(memory_space=pltpu.HBM)
LOOSE = pl.BlockSpec(memory_space=pl.ANY)
WHOLE = pl.BlockSpec(memory_space=pltpu.VMEM)
SCALARS = pl.BlockSpec(memory_space=pltpu.SMEM)
SEMS = pltpu.SemaphoreType.DMA


def cost(flops, moved, exps=0):
    return pl.CostEstimate(flops=flops, bytes_accessed=moved, transcendentals=exps)


def like(*shapes):
    return tuple(jax.ShapeDtypeStruct(shape, dtype) for shape, dtype in shapes)


def part(src, dst, sems, c, group):
    at = pl.ds(c * group, group)
    return pltpu.make_async_copy(src.at[at], dst.at[at], sems.at[c])


def edge_rows(row_blocks):
    left = [(r, r) for r in range(min(REACH, row_blocks))]
    right = [(r, r + REACH + 1 - row_blocks) for r in range(max(row_blocks - REACH, 0), row_blocks)]
    return left, right


def edge_list(row_blocks):
    left, right = edge_rows(row_blocks)
    return (
        [(r, t - REACH - r) for r, low in left for t in range(low, REACH)],
        [(r, row_blocks + t - r) for r, count in right for t in range(count)],
    )


def fill_slots(me, projected, slots):
    devices, rank, _ = slots.shape
    for m in range(devices):
        level = max(m.bit_length() - 1, 0)
        slots[me ^ m] = projected[level * rank : (level + 1) * rank].astype(slots.dtype)


def send_copies(me, x, slots, side_a, side_b, slots_out, a_out, b_out, sems):
    row_blocks = x.shape[0] - 1
    odd = lax.rem(me, 2)
    start_a = (1 - odd) * (row_blocks - REACH)
    start_b = odd * (row_blocks - REACH)
    return [
        pltpu.make_async_copy(slots, slots_out, sems.at[0]),
        pltpu.make_async_copy(x.at[pl.ds(start_a, REACH)], a_out, sems.at[1]),
        pltpu.make_async_copy(x.at[pl.ds(start_b, REACH)], b_out, sems.at[2]),
    ]


def open_kernel(
    me_ref, p_in, basis_in, x_out, slots_out, a_out, b_out,
    p, basis, x, slots, p_sems, x_sems, basis_sem, send_sems,
):
    row_blocks, size, cols = p.shape
    chunks = p_sems.shape[0]
    group = row_blocks // chunks
    me = me_ref[0]
    for c in range(chunks):
        part(p_in, p, p_sems, c, group).start()
        if c == 0:
            pltpu.make_async_copy(basis_in, basis, basis_sem).start()
    projected = jnp.zeros((basis.shape[0], cols), F32)
    for c in range(chunks):
        part(p_in, p, p_sems, c, group).wait()
        rows = slice(c * group, (c + 1) * group)
        rates = jnp.exp(p[rows]).astype(BF16)
        x[rows] = rates
        if c == 0:
            pltpu.make_async_copy(basis_in, basis, basis_sem).wait()
        projected += jnp.dot(
            basis[:, c * group * size : (c + 1) * group * size],
            rates.reshape(group * size, cols),
            preferred_element_type=F32,
        )
    x[row_blocks] = jnp.zeros((size, cols), BF16)
    fill_slots(me, projected, slots)
    copies = send_copies(me, x, slots, None, None, slots_out, a_out, b_out, send_sems)
    copies.append(pltpu.make_async_copy(x, x_out, x_sems))
    for copy in copies:
        copy.start()
    for copy in copies:
        copy.wait()


def column_blocks(me_ref, columns, x, r, near_count, row_blocks, place=None):
    total = row_blocks * me_ref[1]
    first = row_blocks * me_ref[0]
    picked = []
    for k in range(near_count):
        offset = columns[r, k] - first - r
        offset = jnp.where(offset > REACH, offset - total, offset)
        offset = jnp.where(offset < -REACH, offset + total, offset)
        if place is not None:
            place[r, offset + REACH] = k
        index = r + offset
        inside = jnp.logical_and(index >= 0, index < row_blocks)
        picked.append(x[jnp.where(inside, index, row_blocks)])
    return jnp.concatenate(picked, axis=0)


def near_product(me_ref, columns, x, near, r, place=None):
    row_blocks, near_count, size, _ = near.shape
    left = jnp.concatenate([near[r, k] for k in range(near_count)], axis=1)
    right = column_blocks(me_ref, columns, x, r, near_count, row_blocks, place)
    return jnp.dot(left, right, preferred_element_type=F32)


def per_row(vectors, r):
    rows = [v[pl.ds(r, 1), :] for v in vectors]
    rows += [rows[0]] * (8 - len(rows))
    stacked = jnp.concatenate(rows, axis=0).T
    return [stacked[:, q : q + 1] for q in range(len(vectors))]


def known_rates(p, s, near_term, vectors, r):
    stiff, plate, direct, evolve = per_row(vectors, r)
    velocity = jnp.exp(p)
    state = jnp.exp(-s) - velocity
    factor = 1.0 / (direct + damping * velocity)
    return (stiff * (plate - velocity) - near_term - evolve * state) * factor, factor, state


def first_local_kernel(
    me_ref, columns, x_in, near_in, p_in, s_in, coupling, stiff, plate, direct, evolve,
    known_out, factor_out, edge_out, coupling_t_out,
    x, near, p, s, known, factor, edge, coupling_t, place,
    x_sem, near_sems, p_sems, s_sems, known_sems, factor_sems, edge_sems, ct_sem,
):
    row_blocks, near_count, size, _ = near.shape
    chunks = near_sems.shape[0]
    group = row_blocks // chunks
    load_x = pltpu.make_async_copy(x_in, x, x_sem)
    load_x.start()

    def loads(c):
        return [
            part(near_in, near, near_sems, c, group),
            part(p_in, p, p_sems, c, group),
            part(s_in, s, s_sems, c, group),
        ]

    def stores(c):
        return [
            part(known, known_out, known_sems, c, group),
            part(factor, factor_out, factor_sems, c, group),
        ]

    for c in range(chunks):
        for copy in loads(c):
            copy.start()
    for r in range(row_blocks):
        for o in range(2 * REACH + 1):
            place[r, o] = -1
    for r in range(row_blocks):
        coupling_t[r] = coupling[:, r * size : (r + 1) * size].T
    store_ct = pltpu.make_async_copy(coupling_t, coupling_t_out, ct_sem)
    store_ct.start()
    load_x.wait()

    def chunk(c, carry):
        for copy in loads(c):
            copy.wait()
        for i in range(group):
            r = c * group + i
            product = near_product(me_ref, columns, x, near, r, place)
            rate, scale, _ = known_rates(p[r], s[r], product, (stiff, plate, direct, evolve), r)
            known[r] = p[r] + step_size * rate
            factor[r] = step_size * scale
        for copy in stores(c):
            copy.start()
        return carry

    lax.fori_loop(0, chunks, chunk, 0)
    n = 0
    store_edges = []
    for side, blocks in enumerate(edge_list(row_blocks)):
        first = n
        for r, offset in blocks:
            k = place[r, offset + REACH]
            block = near[r, jnp.maximum(k, 0)]
            edge[n] = jnp.where(k >= 0, block, jnp.zeros_like(block))
            n += 1
        at = pl.ds(first, n - first)
        store_edges.append(pltpu.make_async_copy(edge.at[at], edge_out.at[at], edge_sems.at[side]))
        store_edges[-1].start()
    lax.fori_loop(0, chunks, lambda c, carry: [copy.wait() for copy in stores(c)] and carry, 0)
    for copy in store_edges + [store_ct]:
        copy.wait()


def second_local_kernel(
    me_ref, columns, x_in, near_in, p_in, s_in, p2_in, stiff, plate, direct, evolve, area,
    known_out, change_out, factor_out, new_s_out, parts,
    x, near, p, s, p2, known, change, factor, new_s,
    x_sem, near_sems, p_sems, s_sems, p2_sems, known_sems, change_sems, factor_sems, new_s_sems,
):
    row_blocks, near_count, size, cols = near.shape
    chunks = near_sems.shape[0]
    group = row_blocks // chunks
    load_x = pltpu.make_async_copy(x_in, x, x_sem)
    load_x.start()

    def loads(c):
        return [
            part(near_in, near, near_sems, c, group),
            part(p_in, p, p_sems, c, group),
            part(s_in, s, s_sems, c, group),
            part(p2_in, p2, p2_sems, c, group),
        ]

    def stores(c):
        return [
            part(known, known_out, known_sems, c, group),
            part(change, change_out, change_sems, c, group),
            part(factor, factor_out, factor_sems, c, group),
            part(new_s, new_s_out, new_s_sems, c, group),
        ]

    for c in range(chunks):
        for copy in loads(c):
            copy.start()
    load_x.wait()

    def chunk(c, carry):
        errors, areas = carry
        for copy in loads(c):
            copy.wait()
        for i in range(group):
            r = c * group + i
            product = near_product(me_ref, columns, x, near, r)
            rate_a = (p2[r] - p[r]) * (1.0 / step_size)
            state_a = jnp.exp(-s[r]) - jnp.exp(p[r])
            rate, scale, state_b = known_rates(
                p2[r], s[r] + step_size * state_a, product, (stiff, plate, direct, evolve), r
            )
            known[r] = p[r] + half_step * (rate_a + rate)
            change[r] = half_step * (rate - rate_a)
            factor[r] = half_step * scale
            new_s[r] = s[r] + half_step * (state_a + state_b)
            state_error = (half_step / error_scale) * (state_b - state_a)
            weight = jnp.broadcast_to(per_row((area,), r)[0], (size, cols))
            weighted = weight * (state_error * state_error)
            errors += jnp.sum(weighted.reshape(size // 8, 8, cols), axis=0)
            areas += jnp.sum(weight.reshape(size // 8, 8, cols), axis=0)
        for copy in stores(c):
            copy.start()
        return errors, areas

    zero = jnp.zeros((8, cols), F32)
    errors, areas = lax.fori_loop(0, chunks, chunk, (zero, zero))
    parts[0] = errors
    parts[1] = areas
    lax.fori_loop(0, chunks, lambda c, carry: [copy.wait() for copy in stores(c)] and carry, 0)


def couple(me, got, levels):
    devices = got.shape[0]
    sums = []
    for level in range(levels):
        total = got[me ^ (1 << level)].astype(F32)
        for m in range((1 << level) + 1, min(2 << level, devices)):
            total += got[me ^ m].astype(F32)
        sums.append(total.astype(BF16))
    return jnp.concatenate(sums, axis=0)


def row_order(row_blocks, chunks):
    group = row_blocks // chunks
    inner = [
        c for c in range(chunks) if c * group >= REACH and (c + 1) * group <= row_blocks - REACH
    ]
    return inner + [c for c in range(chunks) if c not in inner]


def outer_terms(coupled, coupling_t, halo, edge, r):
    row_blocks, size, _ = coupling_t.shape
    left, right = edge_rows(row_blocks)
    lhs, rhs = [coupling_t[r]], [coupled]
    n = 0
    for row, low in left:
        for t in range(low, REACH):
            if row == r:
                lhs.append(edge[n])
                rhs.append(halo[t])
            n += 1
    for row, count in right:
        for t in range(count):
            if row == r:
                lhs.append(edge[n])
                rhs.append(halo[REACH + t])
            n += 1
    return jnp.dot(
        jnp.concatenate(lhs, axis=1), jnp.concatenate(rhs, axis=0), preferred_element_type=F32
    )


def outer_loads(me, a_in, b_in, got_in, edge_in, ct_in, halo, got, edge, coupling_t, sems):
    odd = lax.rem(me, 2)
    return [
        pltpu.make_async_copy(got_in, got, sems.at[0]),
        pltpu.make_async_copy(ct_in, coupling_t, sems.at[1]),
        pltpu.make_async_copy(a_in, halo.at[pl.ds((1 - odd) * REACH, REACH)], sems.at[2]),
        pltpu.make_async_copy(b_in, halo.at[pl.ds(odd * REACH, REACH)], sems.at[3]),
        pltpu.make_async_copy(edge_in, edge, sems.at[4]),
    ]


def middle_kernel(
    me_ref, a_in, b_in, got_in, edge_in, ct_in, basis_in, known_in, factor_in,
    p2_out, x_out, slots_out, a_out, b_out,
    halo, got, edge, coupling_t, basis, known, factor, p2, x, slots,
    outer_sems, basis_sem, known_sems, factor_sems, p2_sems, x_sem, send_sems,
):
    row_blocks, size, cols = known.shape
    chunks = known_sems.shape[0]
    group = row_blocks // chunks
    me = me_ref[0]
    order = row_order(row_blocks, chunks)
    outer = outer_loads(me, a_in, b_in, got_in, edge_in, ct_in, halo, got, edge, coupling_t, outer_sems)

    def loads(c):
        return [part(known_in, known, known_sems, c, group), part(factor_in, factor, factor_sems, c, group)]

    load_basis = pltpu.make_async_copy(basis_in, basis, basis_sem)
    for copy in outer[:2] + loads(order[0]) + outer[2:] + [load_basis]:
        copy.start()
    for c in order[1:]:
        for copy in loads(c):
            copy.start()
    outer[0].wait()
    coupled = couple(me, got, basis.shape[0] // got.shape[1])
    outer[1].wait()
    projected = jnp.zeros((basis.shape[0], cols), F32)
    waited = False
    for n, c in enumerate(order):
        edged = c * group < REACH or (c + 1) * group > row_blocks - REACH
        if edged and not waited:
            for copy in outer[2:]:
                copy.wait()
            waited = True
        for copy in loads(c):
            copy.wait()
        for r in range(c * group, (c + 1) * group):
            terms = outer_terms(coupled, coupling_t, halo, edge, r)
            value = known[r] - factor[r] * terms
            p2[r] = value
            x[r] = jnp.exp(value).astype(BF16)
        part(p2, p2_out, p2_sems, c, group).start()
        if n == 0:
            load_basis.wait()
        projected += jnp.dot(
            basis[:, c * group * size : (c + 1) * group * size],
            x[c * group : (c + 1) * group].reshape(group * size, cols),
            preferred_element_type=F32,
        )
    x[row_blocks] = jnp.zeros((size, cols), BF16)
    fill_slots(me, projected, slots)
    copies = send_copies(me, x, slots, None, None, slots_out, a_out, b_out, send_sems)
    copies.append(pltpu.make_async_copy(x, x_out, x_sem))
    for copy in copies:
        copy.start()
    for copy in copies + [part(p2, p2_out, p2_sems, c, group) for c in range(chunks)]:
        copy.wait()


def close_kernel(
    me_ref, a_in, b_in, got_in, edge_in, ct_in, known_in, change_in, factor_in, area, parts_in,
    new_p_out, parts_out,
    halo, got, edge, coupling_t, known, change, factor, new_p,
    outer_sems, known_sems, change_sems, factor_sems, new_p_sems,
):
    row_blocks, size, cols = known.shape
    chunks = known_sems.shape[0]
    group = row_blocks // chunks
    me = me_ref[0]
    order = row_order(row_blocks, chunks)
    outer = outer_loads(me, a_in, b_in, got_in, edge_in, ct_in, halo, got, edge, coupling_t, outer_sems)

    def loads(c):
        return [
            part(known_in, known, known_sems, c, group),
            part(change_in, change, change_sems, c, group),
            part(factor_in, factor, factor_sems, c, group),
        ]

    for copy in outer[:2] + loads(order[0]) + outer[2:]:
        copy.start()
    for c in order[1:]:
        for copy in loads(c):
            copy.start()
    outer[0].wait()
    coupled = couple(me, got, coupling_t.shape[2] // got.shape[1])
    outer[1].wait()
    errors = parts_in[0]
    waited = False
    for c in order:
        edged = c * group < REACH or (c + 1) * group > row_blocks - REACH
        if edged and not waited:
            for copy in outer[2:]:
                copy.wait()
            waited = True
        for copy in loads(c):
            copy.wait()
        for r in range(c * group, (c + 1) * group):
            outside = factor[r] * outer_terms(coupled, coupling_t, halo, edge, r)
            new_p[r] = known[r] - outside
            rate_error = (1.0 / error_scale) * (change[r] - outside)
            weighted = per_row((area,), r)[0] * (rate_error * rate_error)
            errors += jnp.sum(weighted.reshape(size // 8, 8, cols), axis=0)
        part(new_p, new_p_out, new_p_sems, c, group).start()
    both = jnp.concatenate(
        [jnp.sum(errors, axis=0, keepdims=True), jnp.sum(parts_in[1], axis=0, keepdims=True)], axis=0
    )
    for j in range(parts_out.shape[0]):
        parts_out[j] = both
    for c in range(chunks):
        part(new_p, new_p_out, new_p_sems, c, group).wait()


def exchange(side_a, side_b, slots):
    count = lax.axis_size(AXIS)
    got_a = lax.ppermute(side_a, AXIS, [(i, i ^ 1) for i in range(count)])
    pairs = [(i, (i - 1) % count if i % 2 == 0 else (i + 1) % count) for i in range(count)]
    got_b = lax.ppermute(side_b, AXIS, pairs)
    got = lax.all_to_all(slots, AXIS, 0, 0)
    return got_a, got_b, got


def on_device(
    log_rate,
    log_state,
    near_blocks,
    near_columns,
    far_basis,
    far_coupling,
    self_stiffness,
    plate_rate,
    direct_effect,
    evolution_effect,
    triangle_area,
):
    rows, cols = log_rate.shape
    row_blocks, near_count, size, _ = near_blocks.shape
    levels, rank, _ = far_basis.shape
    devices = lax.axis_size(AXIS)
    me = jnp.stack([lax.axis_index(AXIS), jnp.int32(devices)]).astype(jnp.int32)
    p = log_rate.reshape(row_blocks, size, cols)
    s = log_state.reshape(row_blocks, size, cols)
    basis = far_basis.reshape(levels * rank, rows)
    coupling = far_coupling.reshape(levels * rank, rows)
    stiff, plate, direct, evolve, area = (
        v.reshape(row_blocks, size)
        for v in (self_stiffness, plate_rate, direct_effect, evolution_effect, triangle_area)
    )
    edges = sum(len(blocks) for blocks in edge_list(row_blocks))
    state = ((row_blocks, size, cols), F32)
    x_kind = ((row_blocks + 1, size, cols), BF16)
    slots_kind = ((devices, rank, cols), BF16)
    side_kind = ((REACH, size, cols), BF16)
    edge_kind = ((edges, size, size), BF16)
    ct_kind = ((row_blocks, size, levels * rank), BF16)
    basis_kind = ((levels * rank, rows), BF16)
    near_kind = (near_blocks.shape, BF16)
    halo_kind = ((2 * REACH, size, cols), BF16)
    chunks = 8 if row_blocks % 8 == 0 else row_blocks
    loads = 4 if row_blocks % 4 == 0 else row_blocks
    near_flops = 2 * rows * near_count * size * cols

    def vmem(*kinds):
        return [pltpu.VMEM(shape, dtype) for shape, dtype in kinds]

    x, slots, side_a, side_b = pl.pallas_call(
        open_kernel,
        out_shape=like(x_kind, slots_kind, side_kind, side_kind),
        in_specs=[SCALARS, PLAIN, PLAIN],
        out_specs=(PLAIN,) * 4,
        scratch_shapes=vmem(state, basis_kind, x_kind, slots_kind)
        + [SEMS((loads,)), SEMS(()), SEMS(()), SEMS((3,))],
        name="open",
    )(me, p, basis)

    got_a, got_b, got = exchange(side_a, side_b, slots)
    known, factor, edge, coupling_t = pl.pallas_call(
        first_local_kernel,
        out_shape=like(state, state, edge_kind, ct_kind),
        in_specs=[SCALARS, SCALARS] + [PLAIN] * 4 + [WHOLE] * 5,
        out_specs=(PLAIN,) * 4,
        scratch_shapes=vmem(x_kind, near_kind, state, state, state, state, edge_kind, ct_kind)
        + [pltpu.SMEM((row_blocks, 2 * REACH + 1), jnp.int32), SEMS(())]
        + [SEMS((chunks,))] * 5
        + [SEMS((2,)), SEMS(())],
        cost_estimate=cost(near_flops, near_blocks.size * 2),
        name="local_one",
    )(me, near_columns, x, near_blocks, p, s, coupling, stiff, plate, direct, evolve)

    p2, x, slots, side_a, side_b = pl.pallas_call(
        middle_kernel,
        out_shape=like(state, x_kind, slots_kind, side_kind, side_kind),
        in_specs=[SCALARS] + [LOOSE] * 3 + [PLAIN] * 5,
        out_specs=(PLAIN,) * 5,
        scratch_shapes=vmem(
            halo_kind, slots_kind, edge_kind, ct_kind, basis_kind, state, state, state, x_kind, slots_kind
        )
        + [SEMS((5,)), SEMS(()), SEMS((chunks,)), SEMS((chunks,)), SEMS((chunks,)), SEMS(()), SEMS((3,))],
        name="middle",
    )(me, got_a, got_b, got, edge, coupling_t, basis, known, factor)

    got_a, got_b, got = exchange(side_a, side_b, slots)
    known, change, factor, new_s, parts = pl.pallas_call(
        second_local_kernel,
        out_shape=like(state, state, state, state, ((2, 8, cols), F32)),
        in_specs=[SCALARS, SCALARS] + [PLAIN] * 5 + [WHOLE] * 5,
        out_specs=(PLAIN,) * 4 + (WHOLE,),
        scratch_shapes=vmem(x_kind, near_kind, state, state, state, state, state, state, state)
        + [SEMS(())]
        + [SEMS((chunks,))] * 8,
        cost_estimate=cost(near_flops, near_blocks.size * 2),
        name="local_two",
    )(me, near_columns, x, near_blocks, p, s, p2, stiff, plate, direct, evolve, area)

    new_p, parts = pl.pallas_call(
        close_kernel,
        out_shape=like(state, ((devices, 2, cols), F32)),
        in_specs=[SCALARS] + [LOOSE] * 3 + [PLAIN] * 5 + [WHOLE] * 2,
        out_specs=(PLAIN, WHOLE),
        scratch_shapes=vmem(halo_kind, slots_kind, edge_kind, ct_kind, state, state, state, state)
        + [SEMS((5,))]
        + [SEMS((chunks,))] * 4,
        name="close",
    )(me, got_a, got_b, got, edge, coupling_t, known, change, factor, area, parts)

    totals = lax.all_to_all(parts, AXIS, 0, 0).sum(axis=0)
    error_norm = jnp.sqrt(totals[0] / totals[1] + 1e-06)
    return new_p.reshape(rows, cols), new_s.reshape(rows, cols), error_norm


def solution(mesh):
    split = P(("member", "patch"))
    in_specs = (
        P(("member", "patch"), None),
        P(("member", "patch"), None),
        P(("member", "patch"), None, None, None),
        P(("member", "patch"), None),
        P("member", None, "patch"),
        P("member", None, "patch"),
        split,
        split,
        split,
        split,
        split,
    )
    out_specs = (P(("member", "patch"), None), P(("member", "patch"), None), P("member"))
    return jax.shard_map(
        on_device, mesh=mesh, in_specs=in_specs, out_specs=out_specs, check_vma=False
    )
```

```python
import jax
import jax.numpy as jnp
from jax import lax
from jax.experimental import pallas as pl
from jax.experimental.pallas import tpu as pltpu
from jax.sharding import PartitionSpec as P


REACH = 6

step_size = 0.1
damping = 0.5
error_scale = 0.01
half_step = 0.5 * step_size

AXIS = "patch"
F32 = jnp.float32
BF16 = jnp.bfloat16
PLAIN = pl.BlockSpec(memory_space=pltpu.HBM)
WHOLE = pl.BlockSpec(memory_space=pltpu.VMEM)
SCALARS = pl.BlockSpec(memory_space=pltpu.SMEM)
SEMS = pltpu.SemaphoreType.DMA


def cost(flops, moved, exps=0):
    return pl.CostEstimate(flops=flops, bytes_accessed=moved, transcendentals=exps)


def in_hbm(*shapes):
    return tuple(pltpu.HBM(shape, dtype) for shape, dtype in shapes)


def hbm(*arrays):
    return tuple(pltpu.with_memory_space_constraint(v, pltpu.HBM) for v in arrays)


def like(*shapes):
    return tuple(jax.ShapeDtypeStruct(shape, dtype) for shape, dtype in shapes)


def part(src, dst, sems, c, group):
    at = pl.ds(c * group, group)
    return pltpu.make_async_copy(src.at[at], dst.at[at], sems.at[c])


def edge_rows(row_blocks):
    left = [(r, r) for r in range(min(REACH, row_blocks))]
    right = [(r, r + REACH + 1 - row_blocks) for r in range(max(row_blocks - REACH, 0), row_blocks)]
    return left, right


def edge_list(row_blocks):
    left, right = edge_rows(row_blocks)
    return (
        [(r, t - REACH - r) for r, low in left for t in range(low, REACH)],
        [(r, row_blocks + t - r) for r, count in right for t in range(count)],
    )


def fill_slots(me, projected, slots):
    devices, rank, _ = slots.shape
    for m in range(devices):
        level = max(m.bit_length() - 1, 0)
        slots[me ^ m] = projected[level * rank : (level + 1) * rank].astype(slots.dtype)


def send_copies(me, x, slots, slots_out, a_out, b_out, sems):
    row_blocks = x.shape[0] - 1
    odd = lax.rem(me, 2)
    start_a = (1 - odd) * (row_blocks - REACH)
    start_b = odd * (row_blocks - REACH)
    return [
        pltpu.make_async_copy(slots, slots_out, sems.at[0]),
        pltpu.make_async_copy(x.at[pl.ds(start_a, REACH)], a_out, sems.at[1]),
        pltpu.make_async_copy(x.at[pl.ds(start_b, REACH)], b_out, sems.at[2]),
    ]


def open_kernel(
    p_in, basis_in, stiff, plate, direct, evolve, area,
    x_out, slots_out, a_out, b_out, columns_out,
    p, basis, x, slots, p_sems, x_sems, basis_sem, send_sems,
):
    row_blocks, size, cols = p.shape
    chunks = p_sems.shape[0]
    group = row_blocks // chunks
    me = lax.axis_index(AXIS)
    for c in range(chunks):
        part(p_in, p, p_sems, c, group).start()
        if c == 0:
            pltpu.make_async_copy(basis_in, basis, basis_sem).start()
    vectors = (stiff, plate, direct, evolve, area, area, area, area)
    for r in range(row_blocks):
        columns_out[r] = jnp.concatenate([v[r : r + 1] for v in vectors], axis=0)
    projected = jnp.zeros((basis.shape[0], cols), F32)
    for c in range(chunks):
        part(p_in, p, p_sems, c, group).wait()
        rows = slice(c * group, (c + 1) * group)
        rates = jnp.exp(p[rows]).astype(BF16)
        x[rows] = rates
        if c == 0:
            pltpu.make_async_copy(basis_in, basis, basis_sem).wait()
        projected += jnp.dot(
            basis[:, c * group * size : (c + 1) * group * size],
            rates.reshape(group * size, cols),
            preferred_element_type=F32,
        )
    x[row_blocks] = jnp.zeros((size, cols), BF16)
    fill_slots(me, projected, slots)
    copies = send_copies(me, x, slots, slots_out, a_out, b_out, send_sems)
    copies.append(pltpu.make_async_copy(x, x_out, x_sems))
    for copy in copies:
        copy.start()
    for copy in copies:
        copy.wait()


def find_columns(columns, picked, r, row_blocks, total, first, place=None):
    for k in range(columns.shape[1]):
        offset = columns[r, k] - first - r
        offset = jnp.where(offset > REACH, offset - total, offset)
        offset = jnp.where(offset < -REACH, offset + total, offset)
        if place is not None:
            place[r, offset + REACH] = k
        index = r + offset
        inside = jnp.logical_and(index >= 0, index < row_blocks)
        picked[k] = jnp.where(inside, index, row_blocks)


def near_product(near, x, picked, r):
    near_count = near.shape[1]
    left = jnp.concatenate([near[r, k] for k in range(near_count)], axis=1)
    right = jnp.concatenate([x[picked[k]] for k in range(near_count)], axis=0)
    return jnp.dot(left, right, preferred_element_type=F32)


def two_stage(row_blocks, find, wait_near, wait_rest, product, finish, even, odd, even_at, odd_at, carry):
    def body(i, carry):
        r = 2 * i
        wait_near(r + 1)
        wait_near(r + 2)
        wait_rest(r)
        wait_rest(r + 1)
        odd[...] = product(r + 1, odd_at)
        find(r + 2, even_at)
        carry = finish(r, even[...], carry)
        even[...] = product(r + 2, even_at)
        find(jnp.minimum(r + 3, row_blocks - 1), odd_at)
        return finish(r + 1, odd[...], carry)

    wait_near(0)
    find(0, even_at)
    find(1, odd_at)
    even[...] = product(0, even_at)
    carry = lax.fori_loop(0, row_blocks // 2 - 1, body, carry)
    last = row_blocks - 2
    wait_near(last + 1)
    wait_rest(last)
    wait_rest(last + 1)
    odd[...] = product(last + 1, odd_at)
    carry = finish(last, even[...], carry)
    return finish(last + 1, odd[...], carry)


def known_rates(velocity, state, near_term, rows):
    stiff, plate, direct, evolve = (rows[:, q : q + 1] for q in range(4))
    factor = 1.0 / (direct + damping * velocity)
    return (stiff * (plate - velocity) - near_term - evolve * state) * factor, factor


def first_local_kernel(
    columns, x_in, near_in, p_in, s_in, coupling, vectors,
    known_out, factor_out, edge_out, coupling_t_out,
    x, near, p, s, known, factor, edge, coupling_t, even, odd, even_at, odd_at, place,
    x_sem, near_sems, p_sems, s_sems, known_sems, factor_sems, edge_sems, ct_sem,
):
    row_blocks, _, size, _ = near.shape
    total = row_blocks * lax.axis_size(AXIS)
    first = row_blocks * lax.axis_index(AXIS)
    load_x = pltpu.make_async_copy(x_in, x, x_sem)
    load_x.start()

    def rest(r):
        return [part(p_in, p, p_sems, r, 1), part(s_in, s, s_sems, r, 1)]

    def stores(r):
        return [part(known, known_out, known_sems, r, 1), part(factor, factor_out, factor_sems, r, 1)]

    def start_loads(r, carry):
        for copy in [part(near_in, near, near_sems, r, 1)] + rest(r):
            copy.start()
        return carry

    lax.fori_loop(0, row_blocks, start_loads, 0)
    for r in range(row_blocks):
        for o in range(2 * REACH + 1):
            place[r, o] = -1
    for r in range(row_blocks):
        coupling_t[r] = coupling[:, r * size : (r + 1) * size].T
    store_ct = pltpu.make_async_copy(coupling_t, coupling_t_out, ct_sem)
    store_ct.start()
    load_x.wait()

    def finish(r, product, carry):
        now = p[r]
        velocity = jnp.exp(now)
        state = jnp.exp(-s[r]) - velocity
        rate, scale = known_rates(velocity, state, product, vectors[r].T)
        known[r] = now + step_size * rate
        factor[r] = step_size * scale
        for copy in stores(r):
            copy.start()
        return carry

    two_stage(
        row_blocks,
        lambda r, at: find_columns(columns, at, r, row_blocks, total, first, place),
        lambda r: part(near_in, near, near_sems, r, 1).wait(),
        lambda r: [copy.wait() for copy in rest(r)],
        lambda r, at: near_product(near, x, at, r),
        finish, even, odd, even_at, odd_at, 0,
    )
    n = 0
    store_edges = []
    for side, blocks in enumerate(edge_list(row_blocks)):
        begin = n
        for r, offset in blocks:
            k = place[r, offset + REACH]
            block = near[r, jnp.maximum(k, 0)]
            edge[n] = jnp.where(k >= 0, block, jnp.zeros_like(block))
            n += 1
        at = pl.ds(begin, n - begin)
        store_edges.append(pltpu.make_async_copy(edge.at[at], edge_out.at[at], edge_sems.at[side]))
        store_edges[-1].start()

    def wait_stores(r, carry):
        for copy in stores(r):
            copy.wait()
        return carry

    lax.fori_loop(0, row_blocks, wait_stores, 0)
    for copy in store_edges + [store_ct]:
        copy.wait()


def second_local_kernel(
    columns, x_in, near_in, p_in, s_in, p2_in, vectors,
    change_out, factor_out, new_s_out, parts,
    x, near, p, s, p2, change, factor, new_s, even, odd, even_at, odd_at,
    x_sem, near_sems, p_sems, s_sems, p2_sems, change_sems, factor_sems, new_s_sems,
):
    row_blocks, _, size, cols = near.shape
    total = row_blocks * lax.axis_size(AXIS)
    first = row_blocks * lax.axis_index(AXIS)
    load_x = pltpu.make_async_copy(x_in, x, x_sem)
    load_x.start()

    def rest(r):
        return [part(p_in, p, p_sems, r, 1), part(s_in, s, s_sems, r, 1), part(p2_in, p2, p2_sems, r, 1)]

    def stores(r):
        return [
            part(change, change_out, change_sems, r, 1),
            part(factor, factor_out, factor_sems, r, 1),
            part(new_s, new_s_out, new_s_sems, r, 1),
        ]

    def start_loads(r, carry):
        for copy in [part(near_in, near, near_sems, r, 1)] + rest(r):
            copy.start()
        return carry

    lax.fori_loop(0, row_blocks, start_loads, 0)
    load_x.wait()

    def finish(r, product, carry):
        errors, areas = carry
        before, now, start = p[r], p2[r], s[r]
        rows = vectors[r].T
        state_a = jnp.exp(-start) - jnp.exp(before)
        velocity = jnp.exp(now)
        state_b = jnp.exp(-(start + step_size * state_a)) - velocity
        rate, scale = known_rates(velocity, state_b, product, rows)
        change[r] = half_step * rate - (half_step / step_size) * (now - before)
        factor[r] = half_step * scale
        new_s[r] = start + half_step * (state_a + state_b)
        state_error = (half_step / error_scale) * (state_b - state_a)
        weight = jnp.broadcast_to(rows[:, 4:5], (size, cols))
        weighted = weight * (state_error * state_error)
        errors += jnp.sum(weighted.reshape(size // 8, 8, cols), axis=0)
        areas += jnp.sum(weight.reshape(size // 8, 8, cols), axis=0)
        for copy in stores(r):
            copy.start()
        return errors, areas

    zero = jnp.zeros((8, cols), F32)
    errors, areas = two_stage(
        row_blocks,
        lambda r, at: find_columns(columns, at, r, row_blocks, total, first),
        lambda r: part(near_in, near, near_sems, r, 1).wait(),
        lambda r: [copy.wait() for copy in rest(r)],
        lambda r, at: near_product(near, x, at, r),
        finish, even, odd, even_at, odd_at, (zero, zero),
    )
    parts[0] = errors
    parts[1] = areas

    def wait_stores(r, carry):
        for copy in stores(r):
            copy.wait()
        return carry

    lax.fori_loop(0, row_blocks, wait_stores, 0)


def couple(me, got, levels):
    devices = got.shape[0]
    sums = []
    for level in range(levels):
        total = got[me ^ (1 << level)].astype(F32)
        for m in range((1 << level) + 1, min(2 << level, devices)):
            total += got[me ^ m].astype(F32)
        sums.append(total.astype(BF16))
    return jnp.concatenate(sums, axis=0)


def row_order(row_blocks, chunks):
    group = row_blocks // chunks
    inner = [
        c for c in range(chunks) if c * group >= REACH and (c + 1) * group <= row_blocks - REACH
    ]
    return inner + [c for c in range(chunks) if c not in inner]


def outer_terms(coupled, coupling_t, halo, edge, r):
    row_blocks, _, _ = coupling_t.shape
    left, right = edge_rows(row_blocks)
    lhs, rhs = [coupling_t[r]], [coupled]
    n = 0
    for row, low in left:
        for t in range(low, REACH):
            if row == r:
                lhs.append(edge[n])
                rhs.append(halo[t])
            n += 1
    for row, count in right:
        for t in range(count):
            if row == r:
                lhs.append(edge[n])
                rhs.append(halo[REACH + t])
            n += 1
    return jnp.dot(
        jnp.concatenate(lhs, axis=1), jnp.concatenate(rhs, axis=0), preferred_element_type=F32
    )


def place_halo(me, got_a, got_b, halo):
    odd = lax.rem(me, 2)
    at_a = (1 - odd) * REACH
    at_b = odd * REACH
    for t in range(REACH):
        halo[at_a + t] = got_a[t]
        halo[at_b + t] = got_b[t]


def run_rows(order, loads, outer, row, done, start):
    ahead = 4
    for copy in outer[:1]:
        copy.start()
    for c in order[:ahead]:
        for copy in loads(c):
            copy.start()
        if c == order[0]:
            for copy in outer[1:]:
                copy.start()
    start()
    for n, c in enumerate(order):
        if n == 0:
            outer[0].wait()
        if n == 2:
            for copy in outer[1:]:
                copy.wait()
        for copy in loads(c):
            copy.wait()
        if n + ahead < len(order):
            for copy in loads(order[n + ahead]):
                copy.start()
        row(c)
        done(c)


def middle_kernel(
    got_a, got_b, got, edge_in, ct_in, basis_in, known_in, factor_in,
    p2_out, x_out, slots_out, a_out, b_out,
    halo, edge, coupling_t, basis, known, factor, p2, x, slots, coupled,
    outer_sems, known_sems, factor_sems, p2_sems, x_sem, send_sems,
):
    row_blocks, size, cols = known.shape
    chunks = known_sems.shape[0]
    group = row_blocks // chunks
    me = lax.axis_index(AXIS)
    order = row_order(row_blocks, chunks)
    outer = [
        pltpu.make_async_copy(ct_in, coupling_t, outer_sems.at[0]),
        pltpu.make_async_copy(edge_in, edge, outer_sems.at[1]),
        pltpu.make_async_copy(basis_in, basis, outer_sems.at[2]),
    ]

    def loads(c):
        return [part(known_in, known, known_sems, c, group), part(factor_in, factor, factor_sems, c, group)]

    def start():
        coupled[...] = couple(me, got, basis.shape[0] // got.shape[1])
        place_halo(me, got_a, got_b, halo)
        x[row_blocks] = jnp.zeros((size, cols), BF16)

    def row(c):
        for r in range(c * group, (c + 1) * group):
            value = known[r] - factor[r] * outer_terms(coupled[...], coupling_t, halo, edge, r)
            p2[r] = value
            x[r] = jnp.exp(value).astype(BF16)

    def done(c):
        part(p2, p2_out, p2_sems, c, group).start()

    run_rows(order, loads, outer, row, done, start)
    send = send_copies(me, x, slots, slots_out, a_out, b_out, send_sems)
    send.append(pltpu.make_async_copy(x, x_out, x_sem))
    for copy in send[1:]:
        copy.start()
    total = jnp.dot(
        basis[...], x[:row_blocks].reshape(row_blocks * size, cols), preferred_element_type=F32
    )
    fill_slots(me, total, slots)
    send[0].start()
    for copy in send + [part(p2, p2_out, p2_sems, c, group) for c in range(chunks)]:
        copy.wait()


def close_kernel(
    got_a, got_b, got, edge_in, ct_in, p2_in, change_in, factor_in, vectors, parts_in,
    new_p_out, parts_out,
    halo, edge, coupling_t, p2, change, factor, new_p, coupled,
    outer_sems, p2_sems, change_sems, factor_sems, new_p_sems,
):
    row_blocks, size, cols = change.shape
    chunks = change_sems.shape[0]
    group = row_blocks // chunks
    me = lax.axis_index(AXIS)
    order = row_order(row_blocks, chunks)
    outer = [
        pltpu.make_async_copy(ct_in, coupling_t, outer_sems.at[0]),
        pltpu.make_async_copy(edge_in, edge, outer_sems.at[1]),
    ]

    def loads(c):
        return [
            part(change_in, change, change_sems, c, group),
            part(factor_in, factor, factor_sems, c, group),
            part(p2_in, p2, p2_sems, c, group),
        ]

    def start():
        coupled[...] = couple(me, got, coupling_t.shape[2] // got.shape[1])
        place_halo(me, got_a, got_b, halo)

    errors = [parts_in[0]]

    def row(c):
        for r in range(c * group, (c + 1) * group):
            move = change[r] - factor[r] * outer_terms(coupled[...], coupling_t, halo, edge, r)
            new_p[r] = p2[r] + move
            rate_error = (1.0 / error_scale) * move
            weighted = vectors[r].T[:, 4:5] * (rate_error * rate_error)
            errors[0] += jnp.sum(weighted.reshape(size // 8, 8, cols), axis=0)

    def done(c):
        part(new_p, new_p_out, new_p_sems, c, group).start()

    run_rows(order, loads, outer, row, done, start)
    both = jnp.concatenate(
        [jnp.sum(errors[0], axis=0, keepdims=True), jnp.sum(parts_in[1], axis=0, keepdims=True)], axis=0
    )
    for j in range(parts_out.shape[0]):
        parts_out[j] = both
    for c in range(chunks):
        part(new_p, new_p_out, new_p_sems, c, group).wait()


def exchange(side_a, side_b, slots):
    count = lax.axis_size(AXIS)
    got_a = lax.ppermute(side_a, AXIS, [(i, i ^ 1) for i in range(count)])
    pairs = [(i, (i - 1) % count if i % 2 == 0 else (i + 1) % count) for i in range(count)]
    got_b = lax.ppermute(side_b, AXIS, pairs)
    got = lax.all_to_all(slots, AXIS, 0, 0)
    return got_a, got_b, got


def on_device(
    log_rate,
    log_state,
    near_blocks,
    near_columns,
    far_basis,
    far_coupling,
    self_stiffness,
    plate_rate,
    direct_effect,
    evolution_effect,
    triangle_area,
):
    rows, cols = log_rate.shape
    row_blocks, near_count, size, _ = near_blocks.shape
    levels, rank, _ = far_basis.shape
    devices = lax.axis_size(AXIS)
    p = log_rate.reshape(row_blocks, size, cols)
    s = log_state.reshape(row_blocks, size, cols)
    basis = far_basis.reshape(levels * rank, rows)
    coupling = far_coupling.reshape(levels * rank, rows)
    stiff, plate, direct, evolve, area = (
        v.reshape(row_blocks, size)
        for v in (self_stiffness, plate_rate, direct_effect, evolution_effect, triangle_area)
    )
    edges = sum(len(blocks) for blocks in edge_list(row_blocks))
    state = ((row_blocks, size, cols), F32)
    x_kind = ((row_blocks + 1, size, cols), BF16)
    slots_kind = ((devices, rank, cols), BF16)
    side_kind = ((REACH, size, cols), BF16)
    edge_kind = ((edges, size, size), BF16)
    ct_kind = ((row_blocks, size, levels * rank), BF16)
    basis_kind = ((levels * rank, rows), BF16)
    near_kind = (near_blocks.shape, BF16)
    halo_kind = ((2 * REACH, size, cols), BF16)
    chunks = 8 if row_blocks % 8 == 0 else row_blocks
    loads = 4 if row_blocks % 4 == 0 else row_blocks
    near_flops = 2 * rows * near_count * size * cols

    def vmem(*kinds):
        return [pltpu.VMEM(shape, dtype) for shape, dtype in kinds]

    small = pltpu.CompilerParams(vmem_limit_bytes=40 * 1024 * 1024)
    tiles_kind = ((row_blocks, 8, size), F32)
    coupled_kind = ((levels * rank, cols), BF16)
    product_kind = ((size, cols), F32)
    picked = [pltpu.SMEM((near_count,), jnp.int32)] * 2

    x, slots, side_a, side_b, vectors = pl.pallas_call(
        open_kernel,
        out_shape=in_hbm(x_kind, slots_kind, side_kind, side_kind) + like(tiles_kind),
        in_specs=[PLAIN, PLAIN] + [WHOLE] * 5,
        out_specs=(PLAIN,) * 4 + (WHOLE,),
        scratch_shapes=vmem(state, basis_kind, x_kind, slots_kind)
        + [SEMS((loads,)), SEMS(()), SEMS(()), SEMS((3,))],
        name="open",
    )(*hbm(p, basis), stiff, plate, direct, evolve, area)

    got_a, got_b, got = exchange(side_a, side_b, slots)
    known, factor, edge, coupling_t = pl.pallas_call(
        first_local_kernel,
        out_shape=in_hbm(state, state, edge_kind, ct_kind),
        in_specs=[SCALARS] + [PLAIN] * 4 + [WHOLE] * 2,
        out_specs=(PLAIN,) * 4,
        scratch_shapes=vmem(
            x_kind, near_kind, state, state, state, state, edge_kind, ct_kind, product_kind, product_kind
        )
        + picked
        + [pltpu.SMEM((row_blocks, 2 * REACH + 1), jnp.int32), SEMS(())]
        + [SEMS((row_blocks,))] * 5
        + [SEMS((2,)), SEMS(())],
        cost_estimate=cost(near_flops, near_blocks.size * 2),
        name="local_one",
    )(near_columns, *hbm(x, near_blocks, p, s), coupling, vectors)

    p2, x, slots, side_a, side_b = pl.pallas_call(
        middle_kernel,
        out_shape=in_hbm(state, x_kind, slots_kind, side_kind, side_kind),
        in_specs=[WHOLE] * 3 + [PLAIN] * 5,
        out_specs=(PLAIN,) * 5,
        scratch_shapes=vmem(
            halo_kind, edge_kind, ct_kind, basis_kind, state, state, state, x_kind, slots_kind, coupled_kind
        )
        + [SEMS((3,)), SEMS((chunks,)), SEMS((chunks,)), SEMS((chunks,)), SEMS(()), SEMS((3,))],
        compiler_params=small,
        name="middle",
    )(got_a, got_b, got, *hbm(edge, coupling_t, basis, known, factor))

    got_a, got_b, got = exchange(side_a, side_b, slots)
    change, factor, new_s, parts = pl.pallas_call(
        second_local_kernel,
        out_shape=in_hbm(state, state, state) + like(((2, 8, cols), F32)),
        in_specs=[SCALARS] + [PLAIN] * 5 + [WHOLE],
        out_specs=(PLAIN,) * 3 + (WHOLE,),
        scratch_shapes=vmem(
            x_kind, near_kind, state, state, state, state, state, state, product_kind, product_kind
        )
        + picked
        + [SEMS(())]
        + [SEMS((row_blocks,))] * 7,
        cost_estimate=cost(near_flops, near_blocks.size * 2),
        name="local_two",
    )(near_columns, *hbm(x, near_blocks, p, s, p2), vectors)

    new_p, parts = pl.pallas_call(
        close_kernel,
        out_shape=in_hbm(state) + like(((devices, 2, cols), F32)),
        in_specs=[WHOLE] * 3 + [PLAIN] * 5 + [WHOLE] * 2,
        out_specs=(PLAIN, WHOLE),
        scratch_shapes=vmem(halo_kind, edge_kind, ct_kind, state, state, state, state, coupled_kind)
        + [SEMS((2,))]
        + [SEMS((chunks,))] * 4,
        compiler_params=small,
        name="close",
    )(got_a, got_b, got, *hbm(edge, coupling_t, p2, change, factor), vectors, parts)

    totals = lax.all_to_all(parts, AXIS, 0, 0).sum(axis=0)
    error_norm = jnp.sqrt(totals[0] / totals[1] + 1e-06)
    return new_p.reshape(rows, cols), new_s.reshape(rows, cols), error_norm


def solution(mesh):
    split = P(("member", "patch"))
    in_specs = (
        P(("member", "patch"), None),
        P(("member", "patch"), None),
        P(("member", "patch"), None, None, None),
        P(("member", "patch"), None),
        P("member", None, "patch"),
        P("member", None, "patch"),
        split,
        split,
        split,
        split,
        split,
    )
    out_specs = (P(("member", "patch"), None), P(("member", "patch"), None), P("member"))
    return jax.shard_map(
        on_device, mesh=mesh, in_specs=in_specs, out_specs=out_specs, check_vma=False
    )
```

```python
import jax
import jax.numpy as jnp
from jax import lax
from jax.experimental import pallas as pl
from jax.experimental.pallas import tpu as pltpu
from jax.sharding import PartitionSpec as P


REACH = 6

step_size = 0.1
damping = 0.5
error_scale = 0.01
half_step = 0.5 * step_size

AXIS = "patch"
F32 = jnp.float32
BF16 = jnp.bfloat16
PLAIN = pl.BlockSpec(memory_space=pltpu.HBM)
WHOLE = pl.BlockSpec(memory_space=pltpu.VMEM)
SCALARS = pl.BlockSpec(memory_space=pltpu.SMEM)
SEMS = pltpu.SemaphoreType.DMA


def cost(flops, moved, exps=0):
    return pl.CostEstimate(flops=flops, bytes_accessed=moved, transcendentals=exps)


def in_hbm(*shapes):
    return tuple(pltpu.HBM(shape, dtype) for shape, dtype in shapes)


def hbm(*arrays):
    return tuple(pltpu.with_memory_space_constraint(v, pltpu.HBM) for v in arrays)


def like(*shapes):
    return tuple(jax.ShapeDtypeStruct(shape, dtype) for shape, dtype in shapes)


def part(src, dst, sems, c, group):
    at = pl.ds(c * group, group)
    return pltpu.make_async_copy(src.at[at], dst.at[at], sems.at[c])


def pair_columns(row_blocks, pair):
    reached = range((2 * pair - REACH) // 2, (2 * pair + 1 + REACH) // 2 + 1)
    count = row_blocks // 2
    return (
        [c for c in reached if c < 0],
        [c for c in reached if 0 <= c < count],
        [c for c in reached if c >= count],
    )


def edge_tiles(row_blocks):
    tiles = []
    for pair in range(row_blocks // 2):
        left, _, right = pair_columns(row_blocks, pair)
        tiles += [(pair, c) for c in left + right]
    return tiles


def project(basis, x):
    row_blocks, size, cols = x.shape
    return jnp.dot(basis[...], x[...].reshape(row_blocks * size, cols), preferred_element_type=F32)


def fill_slots(me, projected, slots):
    devices, rank, _ = slots.shape
    for m in range(devices):
        level = max(m.bit_length() - 1, 0)
        slots[me ^ m] = projected[level * rank : (level + 1) * rank].astype(slots.dtype)


def send_copies(me, x, slots, slots_out, a_out, b_out, sems):
    row_blocks = x.shape[0]
    odd = lax.rem(me, 2)
    start_a = (1 - odd) * (row_blocks - REACH)
    start_b = odd * (row_blocks - REACH)
    return [
        pltpu.make_async_copy(slots, slots_out, sems.at[0]),
        pltpu.make_async_copy(x.at[pl.ds(start_a, REACH)], a_out, sems.at[1]),
        pltpu.make_async_copy(x.at[pl.ds(start_b, REACH)], b_out, sems.at[2]),
    ]


def open_kernel(
    p_in, basis_in, x_out, slots_out, a_out, b_out,
    p, basis, x, slots, p_sems, x_sem, basis_sem, send_sems,
):
    row_blocks, _, _ = p.shape
    chunks = p_sems.shape[0]
    group = row_blocks // chunks
    me = lax.axis_index(AXIS)
    load_basis = pltpu.make_async_copy(basis_in, basis, basis_sem)
    for c in range(chunks):
        part(p_in, p, p_sems, c, group).start()
    load_basis.start()
    for c in range(chunks):
        part(p_in, p, p_sems, c, group).wait()
        rows = slice(c * group, (c + 1) * group)
        x[rows] = jnp.exp(p[rows]).astype(BF16)
    send = send_copies(me, x, slots, slots_out, a_out, b_out, send_sems)
    send.append(pltpu.make_async_copy(x, x_out, x_sem))
    for copy in send[1:]:
        copy.start()
    load_basis.wait()
    fill_slots(me, project(basis, x), slots)
    send[0].start()
    for copy in send:
        copy.wait()


def find_blocks(columns, where):
    row_blocks, near_count = columns.shape
    total = row_blocks * lax.axis_size(AXIS)
    first = row_blocks * lax.axis_index(AXIS)

    def row(r, carry):
        for o in range(2 * REACH + 1):
            where[r, o] = row_blocks * near_count
        for k in range(near_count):
            offset = columns[r, k] - first - r
            offset = jnp.where(offset > REACH, offset - total, offset)
            offset = jnp.where(offset < -REACH, offset + total, offset)
            where[r, offset + REACH] = r * near_count + k
        return carry

    lax.fori_loop(0, row_blocks, row, 0)


def near_block(near, where, r, c):
    if abs(c - r) > REACH:
        return jnp.zeros(near.shape[1:], near.dtype)
    return near[where[r, c - r + REACH]]


def near_product(near, x, where, pair):
    row_blocks, _, cols = x.shape
    own = pair_columns(row_blocks, pair)[1]
    lhs = [
        jnp.concatenate([near_block(near, where, r, c) for c in range(2 * own[0], 2 * own[-1] + 2)], axis=1)
        for r in (2 * pair, 2 * pair + 1)
    ]
    rhs = x[2 * own[0] : 2 * own[-1] + 2].reshape(-1, cols)
    return jnp.dot(jnp.concatenate(lhs, axis=0), rhs, preferred_element_type=F32)


def strips(size):
    step = 32 if size % 32 == 0 else size
    return [slice(i, i + step) for i in range(0, size, step)]


def columns_of(table, r, at):
    return [table[at, 8 * r + q : 8 * r + q + 1] for q in range(5)]


def known_rates(velocity, state, near_term, rows):
    stiff, plate, direct, evolve, _ = rows
    factor = 1.0 / (direct + damping * velocity)
    return (stiff * (plate - velocity) - near_term - evolve * state) * factor, factor


def in_pairs(pairs, wait, product, finish, store):
    wait(0)
    product(0)
    for pair in range(pairs):
        if pair + 1 < pairs:
            wait(pair + 1)
            product(pair + 1)
        finish(pair)
        store(pair)


def first_local_kernel(
    columns, x_in, near_in, p_in, s_in, coupling_in, stiff_in, plate_in, direct_in, evolve_in, area_in,
    known_out, factor_out, edge_out, coupling_t_out, table_out,
    x, near, p, s, coupling, stiff, plate, direct, evolve, area, known, factor, edge, coupling_t, table, products,
    where, x_sem, near_sems, p_sems, s_sems, coupling_sem, vector_sems, known_sems, factor_sems, rest_sems,
):
    row_blocks, size, _ = x.shape
    pairs = row_blocks // 2
    span = (near.shape[0] - 1) // pairs
    vectors = (stiff, plate, direct, evolve, area)
    load_x = pltpu.make_async_copy(x_in, x, x_sem)
    load_coupling = pltpu.make_async_copy(coupling_in, coupling, coupling_sem)
    load_vectors = [
        pltpu.make_async_copy(src, dst, vector_sems.at[q])
        for q, (src, dst) in enumerate(zip((stiff_in, plate_in, direct_in, evolve_in, area_in), vectors))
    ]

    def loads(c):
        return [part(near_in, near, near_sems, c, span), part(p_in, p, p_sems, c, 2), part(s_in, s, s_sems, c, 2)]

    def stores(c):
        return [part(known, known_out, known_sems, c, 2), part(factor, factor_out, factor_sems, c, 2)]

    for copy in load_vectors + [load_x] + loads(0) + [load_coupling]:
        copy.start()
    for c in range(1, pairs):
        for copy in loads(c):
            copy.start()
    near[near.shape[0] - 1] = jnp.zeros(near.shape[1:], near.dtype)
    find_blocks(columns, where)
    for copy in load_vectors:
        copy.wait()
    tiles = [
        jnp.concatenate([v[r : r + 1] for v in vectors + (area, area, area)], axis=0) for r in range(row_blocks)
    ]
    table[...] = jnp.concatenate(tiles, axis=0).T
    load_x.wait()

    def product(pair):
        products[pair] = near_product(near, x, where, pair)

    def finish(pair):
        for i in range(2):
            r = 2 * pair + i
            for at in strips(size):
                now = p[r, at]
                velocity = jnp.exp(now)
                state = jnp.exp(-s[r, at]) - velocity
                near_term = products[pair, i * size + at.start : i * size + at.stop]
                rate, scale = known_rates(velocity, state, near_term, columns_of(table, r, at))
                known[r, at] = now + step_size * rate
                factor[r, at] = step_size * scale

    in_pairs(
        pairs,
        lambda c: [copy.wait() for copy in loads(c)],
        product,
        finish,
        lambda c: [copy.start() for copy in stores(c)],
    )
    for n, (pair, c) in enumerate(edge_tiles(row_blocks)):
        for i in range(2):
            for j in range(2):
                edge[n, i * size : (i + 1) * size, j * size : (j + 1) * size] = near_block(
                    near, where, 2 * pair + i, 2 * c + j
                )
    load_coupling.wait()
    for r in range(row_blocks):
        coupling_t[r] = coupling[:, r * size : (r + 1) * size].T
    last = [
        pltpu.make_async_copy(edge, edge_out, rest_sems.at[0]),
        pltpu.make_async_copy(coupling_t, coupling_t_out, rest_sems.at[1]),
        pltpu.make_async_copy(table, table_out, rest_sems.at[2]),
    ]
    for copy in last:
        copy.start()
    for c in range(pairs):
        for copy in stores(c):
            copy.wait()
    for copy in last:
        copy.wait()


def second_local_kernel(
    columns, x_in, near_in, p_in, s_in, p2_in, table_in,
    change_out, factor_out, new_s_out, parts_out,
    x, near, p, s, p2, table, change, factor, new_s, parts, products,
    where, x_sem, near_sems, p_sems, s_sems, p2_sems, change_sems, factor_sems, new_s_sems, rest_sems,
):
    row_blocks, size, cols = x.shape
    pairs = row_blocks // 2
    span = (near.shape[0] - 1) // pairs
    load_x = pltpu.make_async_copy(x_in, x, x_sem)
    load_table = pltpu.make_async_copy(table_in, table, rest_sems.at[0])

    def loads(c):
        return [
            part(near_in, near, near_sems, c, span),
            part(p_in, p, p_sems, c, 2),
            part(s_in, s, s_sems, c, 2),
            part(p2_in, p2, p2_sems, c, 2),
        ]

    def stores(c):
        return [
            part(change, change_out, change_sems, c, 2),
            part(factor, factor_out, factor_sems, c, 2),
            part(new_s, new_s_out, new_s_sems, c, 2),
        ]

    load_x.start()
    load_table.start()
    for c in range(pairs):
        for copy in loads(c):
            copy.start()
    near[near.shape[0] - 1] = jnp.zeros(near.shape[1:], near.dtype)
    find_blocks(columns, where)
    load_x.wait()
    load_table.wait()
    errors = [jnp.zeros((8, cols), F32)]

    def product(pair):
        products[pair] = near_product(near, x, where, pair)

    def finish(pair):
        for i in range(2):
            r = 2 * pair + i
            for at in strips(size):
                rows = columns_of(table, r, at)
                before, now, start = p[r, at], p2[r, at], s[r, at]
                state_a = jnp.exp(-start) - jnp.exp(before)
                velocity = jnp.exp(now)
                state_b = jnp.exp(-(start + step_size * state_a)) - velocity
                near_term = products[pair, i * size + at.start : i * size + at.stop]
                rate, scale = known_rates(velocity, state_b, near_term, rows)
                change[r, at] = half_step * rate - (half_step / step_size) * (now - before)
                factor[r, at] = half_step * scale
                new_s[r, at] = start + half_step * (state_a + state_b)
                state_error = (half_step / error_scale) * (state_b - state_a)
                weighted = rows[4] * (state_error * state_error)
                errors[0] += jnp.sum(weighted.reshape(-1, 8, cols), axis=0)

    in_pairs(
        pairs,
        lambda c: [copy.wait() for copy in loads(c)],
        product,
        finish,
        lambda c: [copy.start() for copy in stores(c)],
    )
    parts[0] = errors[0]
    areas = jnp.zeros((size, 1), F32)
    for r in range(row_blocks):
        areas += table[:, 8 * r + 4 : 8 * r + 5]
    parts[1] = jnp.sum(jnp.broadcast_to(areas, (size, cols)).reshape(-1, 8, cols), axis=0)
    store_parts = pltpu.make_async_copy(parts, parts_out, rest_sems.at[1])
    store_parts.start()
    for c in range(pairs):
        for copy in stores(c):
            copy.wait()
    store_parts.wait()


def couple(me, got, levels):
    devices = got.shape[0]
    sums = []
    for level in range(levels):
        total = got[me ^ (1 << level)].astype(F32)
        for m in range((1 << level) + 1, min(2 << level, devices)):
            total += got[me ^ m].astype(F32)
        sums.append(total.astype(BF16))
    return jnp.concatenate(sums, axis=0)


def pair_order(row_blocks):
    edged = {pair for pair, _ in edge_tiles(row_blocks)}
    pairs = range(row_blocks // 2)
    return [c for c in pairs if c not in edged] + [c for c in pairs if c in edged]


def outer_terms(coupled, coupling_t, halo, edge, pair):
    row_blocks, size, rank = coupling_t.shape
    cols = halo.shape[2]
    lhs, rhs = [], []
    for n, (row_pair, c) in enumerate(edge_tiles(row_blocks)):
        if row_pair == pair:
            at = REACH + 2 * c if c < 0 else REACH + 2 * c - row_blocks
            lhs.append(edge[n])
            rhs.append(halo[at : at + 2].reshape(2 * size, cols))
    lhs.append(coupling_t[2 * pair : 2 * pair + 2].reshape(2 * size, rank))
    rhs.append(coupled)
    return jnp.dot(
        jnp.concatenate(lhs, axis=1), jnp.concatenate(rhs, axis=0), preferred_element_type=F32
    )


def place_halo(me, got_a, got_b, halo):
    odd = lax.rem(me, 2)
    at_a = (1 - odd) * REACH
    at_b = odd * REACH
    for t in range(REACH):
        halo[at_a + t] = got_a[t]
        halo[at_b + t] = got_b[t]


def run_rows(order, first_edged, loads, outer, row, done, start):
    ahead = 4
    for copy in outer[:1]:
        copy.start()
    for c in order[:ahead]:
        for copy in loads(c):
            copy.start()
        if c == order[0]:
            for copy in outer[1:]:
                copy.start()
    start()
    for n, c in enumerate(order):
        if n == 0:
            outer[0].wait()
        if n == first_edged:
            for copy in outer[1:]:
                copy.wait()
        for copy in loads(c):
            copy.wait()
        if n + ahead < len(order):
            for copy in loads(order[n + ahead]):
                copy.start()
        row(c)
        done(c)


def middle_kernel(
    got_a, got_b, got, edge_in, ct_in, basis_in, known_in, factor_in,
    p2_out, x_out, slots_out, a_out, b_out,
    halo, edge, coupling_t, basis, known, factor, p2, x, slots, coupled,
    outer_sems, known_sems, factor_sems, p2_sems, x_sem, send_sems,
):
    row_blocks, size, _ = known.shape
    chunks, group = row_blocks // 2, 2
    me = lax.axis_index(AXIS)
    order = pair_order(row_blocks)
    first_edged = order.index(0)
    outer = [
        pltpu.make_async_copy(ct_in, coupling_t, outer_sems.at[0]),
        pltpu.make_async_copy(edge_in, edge, outer_sems.at[1]),
        pltpu.make_async_copy(basis_in, basis, outer_sems.at[2]),
    ]

    def loads(c):
        return [part(known_in, known, known_sems, c, group), part(factor_in, factor, factor_sems, c, group)]

    def start():
        coupled[...] = couple(me, got, basis.shape[0] // got.shape[1])
        place_halo(me, got_a, got_b, halo)

    def row(c):
        terms = outer_terms(coupled[...], coupling_t, halo, edge, c)
        for i in range(2):
            r = 2 * c + i
            value = known[r] - factor[r] * terms[i * size : (i + 1) * size]
            p2[r] = value
            x[r] = jnp.exp(value).astype(BF16)

    def done(c):
        part(p2, p2_out, p2_sems, c, group).start()

    run_rows(order, first_edged, loads, outer, row, done, start)
    send = send_copies(me, x, slots, slots_out, a_out, b_out, send_sems)
    send.append(pltpu.make_async_copy(x, x_out, x_sem))
    for copy in send[1:]:
        copy.start()
    fill_slots(me, project(basis, x), slots)
    send[0].start()
    for copy in send + [part(p2, p2_out, p2_sems, c, group) for c in range(chunks)]:
        copy.wait()


def close_kernel(
    got_a, got_b, got, edge_in, ct_in, p2_in, change_in, factor_in, table_in, parts_in,
    new_p_out, parts_out,
    halo, edge, coupling_t, p2, change, factor, new_p, coupled, table, parts,
    outer_sems, p2_sems, change_sems, factor_sems, new_p_sems,
):
    row_blocks, size, cols = change.shape
    chunks, group = row_blocks // 2, 2
    me = lax.axis_index(AXIS)
    order = pair_order(row_blocks)
    first_edged = order.index(0)
    outer = [
        pltpu.make_async_copy(ct_in, coupling_t, outer_sems.at[0]),
        pltpu.make_async_copy(edge_in, edge, outer_sems.at[1]),
    ]
    small = [
        pltpu.make_async_copy(table_in, table, outer_sems.at[2]),
        pltpu.make_async_copy(parts_in, parts, outer_sems.at[3]),
    ]
    for copy in small:
        copy.start()

    def loads(c):
        return [
            part(change_in, change, change_sems, c, group),
            part(factor_in, factor, factor_sems, c, group),
            part(p2_in, p2, p2_sems, c, group),
        ]

    def start():
        coupled[...] = couple(me, got, coupling_t.shape[2] // got.shape[1])
        place_halo(me, got_a, got_b, halo)
        for copy in small:
            copy.wait()

    errors = [jnp.zeros((8, cols), F32)]

    def row(c):
        terms = outer_terms(coupled[...], coupling_t, halo, edge, c)
        for i in range(2):
            r = 2 * c + i
            move = change[r] - factor[r] * terms[i * size : (i + 1) * size]
            new_p[r] = p2[r] + move
            rate_error = (1.0 / error_scale) * move
            weighted = table[:, 8 * r + 4 : 8 * r + 5] * (rate_error * rate_error)
            errors[0] += jnp.sum(weighted.reshape(size // 8, 8, cols), axis=0)

    def done(c):
        part(new_p, new_p_out, new_p_sems, c, group).start()

    run_rows(order, first_edged, loads, outer, row, done, start)
    both = jnp.concatenate(
        [jnp.sum(errors[0] + parts[0], axis=0, keepdims=True), jnp.sum(parts[1], axis=0, keepdims=True)], axis=0
    )
    for j in range(parts_out.shape[0]):
        parts_out[j] = both
    for c in range(chunks):
        part(new_p, new_p_out, new_p_sems, c, group).wait()


def exchange(side_a, side_b, slots):
    count = lax.axis_size(AXIS)
    got_a = lax.ppermute(side_a, AXIS, [(i, i ^ 1) for i in range(count)])
    pairs = [(i, (i - 1) % count if i % 2 == 0 else (i + 1) % count) for i in range(count)]
    got_b = lax.ppermute(side_b, AXIS, pairs)
    got = lax.all_to_all(slots, AXIS, 0, 0)
    return got_a, got_b, got


def on_device(
    log_rate,
    log_state,
    near_blocks,
    near_columns,
    far_basis,
    far_coupling,
    self_stiffness,
    plate_rate,
    direct_effect,
    evolution_effect,
    triangle_area,
):
    rows, cols = log_rate.shape
    row_blocks, near_count, size, _ = near_blocks.shape
    levels, rank, _ = far_basis.shape
    devices = lax.axis_size(AXIS)
    p = log_rate.reshape(row_blocks, size, cols)
    s = log_state.reshape(row_blocks, size, cols)
    basis = far_basis.reshape(levels * rank, rows)
    coupling = far_coupling.reshape(levels * rank, rows)
    stiff, plate, direct, evolve, area = (
        v.reshape(row_blocks, size)
        for v in (self_stiffness, plate_rate, direct_effect, evolution_effect, triangle_area)
    )
    pairs = row_blocks // 2
    flat_near = near_blocks.reshape(row_blocks * near_count, size, size)
    state = ((row_blocks, size, cols), F32)
    x_kind = ((row_blocks, size, cols), BF16)
    slots_kind = ((devices, rank, cols), BF16)
    side_kind = ((REACH, size, cols), BF16)
    edge_kind = ((len(edge_tiles(row_blocks)), 2 * size, 2 * size), BF16)
    ct_kind = ((row_blocks, size, levels * rank), BF16)
    basis_kind = ((levels * rank, rows), BF16)
    near_kind = ((row_blocks * near_count + 1, size, size), BF16)
    halo_kind = ((2 * REACH, size, cols), BF16)
    vector_kind = ((row_blocks, size), F32)
    table_kind = ((size, 8 * row_blocks), F32)
    parts_kind = ((2, 8, cols), F32)
    products_kind = ((pairs, 2 * size, cols), F32)
    coupled_kind = ((levels * rank, cols), BF16)
    where_kind = pltpu.SMEM((row_blocks, 2 * REACH + 1), jnp.int32)
    loads = 4 if row_blocks % 4 == 0 else row_blocks
    near_flops = 2 * rows * near_count * size * cols

    def vmem(*kinds):
        return [pltpu.VMEM(shape, dtype) for shape, dtype in kinds]

    small = pltpu.CompilerParams(vmem_limit_bytes=40 * 1024 * 1024)
    x, slots, side_a, side_b = pl.pallas_call(
        open_kernel,
        out_shape=in_hbm(x_kind, slots_kind, side_kind, side_kind),
        in_specs=[PLAIN] * 2,
        out_specs=(PLAIN,) * 4,
        scratch_shapes=vmem(state, basis_kind, x_kind, slots_kind)
        + [SEMS((loads,)), SEMS(()), SEMS(()), SEMS((3,))],
        name="open",
    )(*hbm(p, basis))

    got_a, got_b, got = exchange(side_a, side_b, slots)
    known, factor, edge, coupling_t, table = pl.pallas_call(
        first_local_kernel,
        out_shape=in_hbm(state, state, edge_kind, ct_kind, table_kind),
        in_specs=[SCALARS] + [PLAIN] * 10,
        out_specs=(PLAIN,) * 5,
        scratch_shapes=vmem(
            x_kind, near_kind, state, state, basis_kind, *[vector_kind] * 5, state, state, edge_kind, ct_kind,
            table_kind, products_kind,
        )
        + [where_kind, SEMS(())]
        + [SEMS((pairs,))] * 3
        + [SEMS(()), SEMS((5,)), SEMS((pairs,)), SEMS((pairs,)), SEMS((3,))],
        cost_estimate=cost(near_flops, near_blocks.size * 2),
        name="local_one",
    )(near_columns, *hbm(x, flat_near, p, s, coupling, stiff, plate, direct, evolve, area))

    p2, x, slots, side_a, side_b = pl.pallas_call(
        middle_kernel,
        out_shape=in_hbm(state, x_kind, slots_kind, side_kind, side_kind),
        in_specs=[WHOLE] * 3 + [PLAIN] * 5,
        out_specs=(PLAIN,) * 5,
        scratch_shapes=vmem(
            halo_kind, edge_kind, ct_kind, basis_kind, state, state, state, x_kind, slots_kind, coupled_kind
        )
        + [SEMS((3,)), SEMS((pairs,)), SEMS((pairs,)), SEMS((pairs,)), SEMS(()), SEMS((3,))],
        compiler_params=small,
        name="middle",
    )(got_a, got_b, got, *hbm(edge, coupling_t, basis, known, factor))

    got_a, got_b, got = exchange(side_a, side_b, slots)
    change, factor, new_s, parts = pl.pallas_call(
        second_local_kernel,
        out_shape=in_hbm(state, state, state, parts_kind),
        in_specs=[SCALARS] + [PLAIN] * 6,
        out_specs=(PLAIN,) * 4,
        scratch_shapes=vmem(
            x_kind, near_kind, state, state, state, table_kind, state, state, state, parts_kind, products_kind
        )
        + [where_kind, SEMS(())]
        + [SEMS((pairs,))] * 7
        + [SEMS((2,))],
        cost_estimate=cost(near_flops, near_blocks.size * 2),
        name="local_two",
    )(near_columns, *hbm(x, flat_near, p, s, p2, table))

    new_p, parts = pl.pallas_call(
        close_kernel,
        out_shape=in_hbm(state) + like(((devices, 2, cols), F32)),
        in_specs=[WHOLE] * 3 + [PLAIN] * 7,
        out_specs=(PLAIN, WHOLE),
        scratch_shapes=vmem(
            halo_kind, edge_kind, ct_kind, state, state, state, state, coupled_kind, table_kind, parts_kind
        )
        + [SEMS((4,))]
        + [SEMS((pairs,))] * 4,
        compiler_params=small,
        name="close",
    )(got_a, got_b, got, *hbm(edge, coupling_t, p2, change, factor, table, parts))

    totals = lax.all_to_all(parts, AXIS, 0, 0).sum(axis=0)
    error_norm = jnp.sqrt(totals[0] / totals[1] + 1e-06)
    return new_p.reshape(rows, cols), new_s.reshape(rows, cols), error_norm


def solution(mesh):
    split = P(("member", "patch"))
    in_specs = (
        P(("member", "patch"), None),
        P(("member", "patch"), None),
        P(("member", "patch"), None, None, None),
        P(("member", "patch"), None),
        P("member", None, "patch"),
        P("member", None, "patch"),
        split,
        split,
        split,
        split,
        split,
    )
    out_specs = (P(("member", "patch"), None), P(("member", "patch"), None), P("member"))
    return jax.shard_map(
        on_device, mesh=mesh, in_specs=in_specs, out_specs=out_specs, check_vma=False
    )
```

```python
import jax
import jax.numpy as jnp
from jax import lax
from jax.experimental import pallas as pl
from jax.experimental.pallas import tpu as pltpu
from jax.sharding import PartitionSpec as P


REACH = 6
PAD = REACH + REACH % 2

step_size = 0.1
damping = 0.5
error_scale = 0.01
half_step = 0.5 * step_size

AXIS = "patch"
F32 = jnp.float32
BF16 = jnp.bfloat16
PLAIN = pl.BlockSpec(memory_space=pltpu.HBM)
WHOLE = pl.BlockSpec(memory_space=pltpu.VMEM)
SCALARS = pl.BlockSpec(memory_space=pltpu.SMEM)
SEMS = pltpu.SemaphoreType.DMA


def cost(flops, moved, exps=0):
    return pl.CostEstimate(flops=flops, bytes_accessed=moved, transcendentals=exps)


def in_hbm(*shapes):
    return tuple(pltpu.HBM(shape, dtype) for shape, dtype in shapes)


def hbm(*arrays):
    return tuple(pltpu.with_memory_space_constraint(v, pltpu.HBM) for v in arrays)


def like(*shapes):
    return tuple(jax.ShapeDtypeStruct(shape, dtype) for shape, dtype in shapes)


def part(src, dst, sems, c, group):
    at = pl.ds(c * group, group)
    return pltpu.make_async_copy(src.at[at], dst.at[at], sems.at[c])


def edged_pairs(row_blocks):
    count = (REACH + 1) // 2
    pairs = row_blocks // 2
    return list(range(count)), list(range(pairs - count, pairs))


def pick(n, values):
    result = jnp.int32(values[0])
    for i, value in enumerate(values[1:], 1):
        result = jnp.where(n == i, jnp.int32(value), result)
    return result


def project(basis, x):
    row_blocks, size, cols = x.shape
    return jnp.dot(basis[...], x[...].reshape(row_blocks * size, cols), preferred_element_type=F32)


def fill_slots(me, projected, slots):
    devices, rank, _ = slots.shape
    for m in range(devices):
        level = max(m.bit_length() - 1, 0)
        slots[me ^ m] = projected[level * rank : (level + 1) * rank].astype(slots.dtype)


def send_copies(me, x, slots, slots_out, a_out, b_out, sems):
    row_blocks = x.shape[0]
    odd = lax.rem(me, 2)
    start_a = (1 - odd) * (row_blocks - REACH)
    start_b = odd * (row_blocks - REACH)
    return [
        pltpu.make_async_copy(slots, slots_out, sems.at[0]),
        pltpu.make_async_copy(x.at[pl.ds(start_a, REACH)], a_out, sems.at[1]),
        pltpu.make_async_copy(x.at[pl.ds(start_b, REACH)], b_out, sems.at[2]),
    ]


def open_kernel(
    p_in, basis_in, x_out, slots_out, a_out, b_out,
    p, basis, x, slots, p_sems, x_sem, basis_sem, send_sems,
):
    row_blocks, _, _ = p.shape
    chunks = p_sems.shape[0]
    group = row_blocks // chunks
    me = lax.axis_index(AXIS)
    load_basis = pltpu.make_async_copy(basis_in, basis, basis_sem)
    for c in range(chunks):
        part(p_in, p, p_sems, c, group).start()
    load_basis.start()
    for c in range(chunks):
        part(p_in, p, p_sems, c, group).wait()
        rows = slice(c * group, (c + 1) * group)
        x[rows] = jnp.exp(p[rows]).astype(BF16)
    send = send_copies(me, x, slots, slots_out, a_out, b_out, send_sems)
    send.append(pltpu.make_async_copy(x, x_out, x_sem))
    for copy in send[1:]:
        copy.start()
    load_basis.wait()
    fill_slots(me, project(basis, x), slots)
    send[0].start()
    for copy in send:
        copy.wait()


def find_blocks(columns, where):
    row_blocks, near_count = columns.shape
    total = row_blocks * lax.axis_size(AXIS)
    first = row_blocks * lax.axis_index(AXIS)

    def row(r, carry):
        for o in range(2 * REACH + 1):
            where[r, o] = row_blocks * near_count
        for k in range(near_count):
            offset = columns[r, k] - first - r
            offset = jnp.where(offset > REACH, offset - total, offset)
            offset = jnp.where(offset < -REACH, offset + total, offset)
            where[r, offset + REACH] = r * near_count + k
        return carry

    lax.fori_loop(0, row_blocks, row, 0)


def near_product(near, x, where, pair):
    size, cols = x.shape[1:]
    width = 2 * PAD + 2
    lhs = []
    for i in range(2):
        offsets = [j - PAD - i for j in range(width)]
        lhs.append(
            jnp.concatenate(
                [
                    near[where[2 * pair + i, o + REACH]] if abs(o) <= REACH else jnp.zeros((size, size), near.dtype)
                    for o in offsets
                ],
                axis=1,
            )
        )
    rhs = x[pl.ds(2 * pair, width)].reshape(width * size, cols)
    return jnp.dot(jnp.concatenate(lhs, axis=0), rhs, preferred_element_type=F32)


def strips(size):
    step = 32 if size % 32 == 0 else size
    return [slice(i, i + step) for i in range(0, size, step)]


def columns_of(table, pair, i, at):
    lanes = table.shape[1]
    turned = pltpu.roll(table[at], lax.rem(lanes - 16 * pair, lanes), axis=1)
    return [turned[:, 8 * i + q : 8 * i + q + 1] for q in range(5)]


def known_rates(velocity, state, near_term, rows):
    stiff, plate, direct, evolve, _ = rows
    factor = 1.0 / (direct + damping * velocity)
    return (stiff * (plate - velocity) - near_term - evolve * state) * factor, factor


def in_pairs(order, wait_product, wait_finish, product, finish, store, terms, carry):
    count = len(order)
    plain = order == list(range(count))

    def at(n):
        return n if plain else pick(n, order)

    def body(n, carry):
        now, before = at(jnp.minimum(n, count - 1)), at(jnp.maximum(n - 1, 0))
        pl.when(n < count)(lambda: wait_product(n, now))
        pl.when(n != 1)(lambda: wait_finish(before))
        new = product(now)
        carry = finish(before, n > 0, n <= 1, carry)
        terms[...] = new
        pl.when(n > 0)(lambda: store(before))
        return carry

    return lax.fori_loop(0, count + 1, body, carry)


def each(count, action):
    def body(n, carry):
        action(n)
        return carry

    lax.fori_loop(0, count, body, 0)


def start_all(copies):
    for copy in copies:
        copy.start()


def wait_all(copies):
    for copy in copies:
        copy.wait()


def inner(x, size_blocks):
    return x.at[pl.ds(PAD, size_blocks)]


def clear_pads(x, row_blocks):
    zeros = jnp.zeros((PAD,) + x.shape[1:], x.dtype)
    x[:PAD] = zeros
    x[PAD + row_blocks :] = zeros


def first_local_kernel(
    columns, x_in, near_in, p_in, s_in, coupling_in, stiff_in, plate_in, direct_in, evolve_in, area_in,
    known_out, factor_out, edge_out, coupling_t_out, table_out,
    x, near, p, s, coupling, stiff, plate, direct, evolve, area, known, factor, edge, coupling_t, table, terms,
    where, x_sem, near_sems, p_sems, s_sems, coupling_sem, vector_sems, known_sems, factor_sems, rest_sems,
):
    row_blocks, size, _ = p.shape
    pairs = row_blocks // 2
    span = (near.shape[0] - 1) // pairs
    vectors = (stiff, plate, direct, evolve, area)
    load_x = pltpu.make_async_copy(x_in, inner(x, row_blocks), x_sem)
    load_coupling = pltpu.make_async_copy(coupling_in, coupling, coupling_sem)
    load_vectors = [
        pltpu.make_async_copy(src, dst, vector_sems.at[q])
        for q, (src, dst) in enumerate(zip((stiff_in, plate_in, direct_in, evolve_in, area_in), vectors))
    ]

    def near_load(c):
        return part(near_in, near, near_sems, c, span)

    def loads(c):
        return [part(p_in, p, p_sems, c, 2), part(s_in, s, s_sems, c, 2)]

    def stores(c):
        return [part(known, known_out, known_sems, c, 2), part(factor, factor_out, factor_sems, c, 2)]

    start_all(load_vectors + [load_x])
    each(pairs, lambda c: start_all([near_load(c)] + loads(c)))
    load_coupling.start()
    near[near.shape[0] - 1] = jnp.zeros(near.shape[1:], near.dtype)
    clear_pads(x, row_blocks)
    find_blocks(columns, where)
    wait_all(load_vectors)
    tiles = [
        jnp.concatenate([v[r : r + 1] for v in vectors + (area, area, area)], axis=0) for r in range(row_blocks)
    ]
    table[...] = jnp.concatenate(tiles, axis=0).T
    load_x.wait()

    def finish(pair, counts, fresh, carry):
        for i in range(2):
            r = 2 * pair + i
            for at in strips(size):
                now = p[r, at]
                velocity = jnp.exp(now)
                state = jnp.exp(-s[r, at]) - velocity
                near_term = terms[i * size + at.start : i * size + at.stop]
                rate, scale = known_rates(velocity, state, near_term, columns_of(table, pair, i, at))
                known[r, at] = now + step_size * rate
                factor[r, at] = step_size * scale
        return carry

    in_pairs(
        list(range(pairs)),
        lambda n, c: near_load(c).wait(),
        lambda c: wait_all(loads(c)),
        lambda c: near_product(near, x, where, c),
        finish,
        lambda c: start_all(stores(c)),
        terms,
        0,
    )
    left, right = edged_pairs(row_blocks)
    width = edge.shape[2] // size
    for side, first in ((left, -width), (right, row_blocks)):

        def edge_pair(n, side=side, first=first):
            pair = side[0] + n
            slot = n if first < 0 else n + len(left)
            for i in range(2):
                for j in range(width):
                    offset = first + j - 2 * pair - i
                    inside = jnp.abs(offset) <= REACH
                    block = near[
                        jnp.where(inside, where[2 * pair + i, jnp.where(inside, offset, 0) + REACH], near.shape[0] - 1)
                    ]
                    edge[slot, i * size : (i + 1) * size, j * size : (j + 1) * size] = block

        each(len(side), edge_pair)
    store_edge = pltpu.make_async_copy(edge, edge_out, rest_sems.at[0])
    store_edge.start()
    load_coupling.wait()

    def turn(r):
        coupling_t[r] = coupling[:, pl.ds(pl.multiple_of(r * size, size), size)].T

    each(row_blocks, turn)
    last = [
        pltpu.make_async_copy(coupling_t, coupling_t_out, rest_sems.at[1]),
        pltpu.make_async_copy(table, table_out, rest_sems.at[2]),
    ]
    start_all(last)
    each(pairs, lambda c: wait_all(stores(c)))
    wait_all(last + [store_edge])


def second_local_kernel(
    columns, x_in, near_in, p_in, s_in, p2_in, table_in,
    change_out, factor_out, new_s_out, parts_out,
    x, near, p, s, p2, table, change, factor, new_s, parts, terms,
    where, x_sem, near_sems, p_sems, s_sems, p2_sems, change_sems, factor_sems, new_s_sems, rest_sems,
):
    row_blocks, size, cols = p.shape
    pairs = row_blocks // 2
    span = (near.shape[0] - 1) // pairs
    load_x = pltpu.make_async_copy(x_in, inner(x, row_blocks), x_sem)
    load_table = pltpu.make_async_copy(table_in, table, rest_sems.at[0])

    def near_load(c):
        return part(near_in, near, near_sems, c, span)

    def loads(c):
        return [part(p_in, p, p_sems, c, 2), part(s_in, s, s_sems, c, 2), part(p2_in, p2, p2_sems, c, 2)]

    def stores(c):
        return [
            part(change, change_out, change_sems, c, 2),
            part(factor, factor_out, factor_sems, c, 2),
            part(new_s, new_s_out, new_s_sems, c, 2),
        ]

    start_all([load_x, load_table])
    each(pairs, lambda c: start_all([near_load(c)] + loads(c)))
    near[near.shape[0] - 1] = jnp.zeros(near.shape[1:], near.dtype)
    clear_pads(x, row_blocks)
    find_blocks(columns, where)
    load_x.wait()
    load_table.wait()

    def finish(pair, counts, fresh, errors):
        more = jnp.zeros((8, cols), F32)
        for i in range(2):
            r = 2 * pair + i
            for at in strips(size):
                rows = columns_of(table, pair, i, at)
                before, now, start = p[r, at], p2[r, at], s[r, at]
                state_a = jnp.exp(-start) - jnp.exp(before)
                velocity = jnp.exp(now)
                state_b = jnp.exp(-(start + step_size * state_a)) - velocity
                near_term = terms[i * size + at.start : i * size + at.stop]
                rate, scale = known_rates(velocity, state_b, near_term, rows)
                change[r, at] = half_step * rate - (half_step / step_size) * (now - before)
                factor[r, at] = half_step * scale
                new_s[r, at] = start + half_step * (state_a + state_b)
                state_error = (half_step / error_scale) * (state_b - state_a)
                weighted = rows[4] * (state_error * state_error)
                more += jnp.sum(weighted.reshape(-1, 8, cols), axis=0)
        return errors + jnp.where(counts, more, jnp.zeros_like(more))

    parts[0] = in_pairs(
        list(range(pairs)),
        lambda n, c: near_load(c).wait(),
        lambda c: wait_all(loads(c)),
        lambda c: near_product(near, x, where, c),
        finish,
        lambda c: start_all(stores(c)),
        terms,
        jnp.zeros((8, cols), F32),
    )
    lane = lax.broadcasted_iota(jnp.int32, table.shape, 1)
    areas = jnp.where(lane % 8 == 4, table[...], jnp.zeros(table.shape, F32))
    areas = jnp.sum(areas.reshape(-1, 8, table.shape[1]), axis=0)
    parts[1] = jnp.broadcast_to(jnp.sum(areas, axis=1, keepdims=True), (8, cols))
    store_parts = pltpu.make_async_copy(parts, parts_out, rest_sems.at[1])
    store_parts.start()
    each(pairs, lambda c: wait_all(stores(c)))
    store_parts.wait()


def couple(me, got, levels):
    devices = got.shape[0]
    sums = []
    for level in range(levels):
        total = got[me ^ (1 << level)].astype(F32)
        for m in range((1 << level) + 1, min(2 << level, devices)):
            total += got[me ^ m].astype(F32)
        sums.append(total.astype(BF16))
    return jnp.concatenate(sums, axis=0)


def pair_order(row_blocks):
    edged = sum(edged_pairs(row_blocks), [])
    free = [c for c in range(row_blocks // 2) if c not in edged]
    return free + edged, len(free)


def outer_terms(coupled, coupling_t, halo, edge, pair):
    row_blocks, size, rank = coupling_t.shape
    cols = halo.shape[2]
    width = edge.shape[2] // size
    left, right = edged_pairs(row_blocks)
    in_left, in_right = pair <= left[-1], pair >= right[0]
    slot = jnp.where(in_left, pair, jnp.where(in_right, pair - right[0] + len(left), 0))
    at = jnp.where(in_left, 0, jnp.where(in_right, width, 2 * width))
    lhs = jnp.concatenate([edge[slot], coupling_t[pl.ds(2 * pair, 2)].reshape(2 * size, rank)], axis=1)
    rhs = jnp.concatenate([halo[pl.ds(at, width)].reshape(width * size, cols), coupled[...]], axis=0)
    return jnp.dot(lhs, rhs, preferred_element_type=F32)


def place_halo(me, got_a, got_b, halo):
    odd = lax.rem(me, 2)
    halo[pl.ds((1 - odd) * REACH, REACH)] = got_a[...]
    halo[pl.ds(odd * REACH, REACH)] = got_b[...]
    halo[2 * REACH :] = jnp.zeros(got_a.shape, got_a.dtype)


def middle_kernel(
    got_a, got_b, got, edge_in, ct_in, basis_in, known_in, factor_in,
    p2_out, x_out, slots_out, a_out, b_out,
    halo, edge, coupling_t, basis, known, factor, p2, x, slots, coupled, projected, terms,
    outer_sems, known_sems, factor_sems, p2_sems, x_sem, send_sems,
):
    row_blocks, size, cols = known.shape
    pairs = row_blocks // 2
    me = lax.axis_index(AXIS)
    order, _ = pair_order(row_blocks)
    load_ct = pltpu.make_async_copy(ct_in, coupling_t, outer_sems.at[0])
    load_edge = pltpu.make_async_copy(edge_in, edge, outer_sems.at[1])
    load_basis = pltpu.make_async_copy(basis_in, basis, outer_sems.at[2])

    def loads(c):
        return [part(known_in, known, known_sems, c, 2), part(factor_in, factor, factor_sems, c, 2)]

    def store(c):
        return part(p2, p2_out, p2_sems, c, 2)

    load_ct.start()
    for n, c in enumerate(order):
        start_all(loads(c))
        if n == 0:
            load_edge.start()
            load_basis.start()
    coupled[...] = couple(me, got, basis.shape[0] // got.shape[1])
    place_halo(me, got_a, got_b, halo)
    load_ct.wait()
    load_edge.wait()
    load_basis.wait()

    def finish(pair, counts, fresh, carry):
        for i in range(2):
            r = 2 * pair + i
            for at in strips(size):
                value = known[r, at] - factor[r, at] * terms[i * size + at.start : i * size + at.stop]
                p2[r, at] = value
                x[r, at] = jnp.exp(value).astype(BF16)
        more = jnp.dot(
            basis[:, pl.ds(pl.multiple_of(2 * pair * size, 2 * size), 2 * size)],
            x[pl.ds(2 * pair, 2)].reshape(2 * size, cols),
            preferred_element_type=F32,
        )
        projected[...] = more + jnp.where(fresh, jnp.zeros_like(more), projected[...])
        return carry

    in_pairs(
        order,
        lambda n, c: None,
        lambda c: wait_all(loads(c)),
        lambda c: outer_terms(coupled, coupling_t, halo, edge, c),
        finish,
        lambda c: store(c).start(),
        terms,
        0,
    )
    send = send_copies(me, x, slots, slots_out, a_out, b_out, send_sems)
    send.append(pltpu.make_async_copy(x, x_out, x_sem))
    start_all(send[1:])
    fill_slots(me, projected, slots)
    send[0].start()
    wait_all(send)
    each(pairs, lambda c: store(c).wait())


def close_kernel(
    got_a, got_b, got, edge_in, ct_in, p2_in, change_in, factor_in, table_in, parts_in,
    new_p_out, parts_out,
    halo, edge, coupling_t, p2, change, factor, new_p, coupled, table, parts, terms,
    outer_sems, p2_sems, change_sems, factor_sems, new_p_sems,
):
    row_blocks, size, cols = change.shape
    pairs = row_blocks // 2
    me = lax.axis_index(AXIS)
    order, _ = pair_order(row_blocks)
    load_ct = pltpu.make_async_copy(ct_in, coupling_t, outer_sems.at[0])
    load_edge = pltpu.make_async_copy(edge_in, edge, outer_sems.at[1])
    small = [
        pltpu.make_async_copy(table_in, table, outer_sems.at[2]),
        pltpu.make_async_copy(parts_in, parts, outer_sems.at[3]),
    ]

    def loads(c):
        return [
            part(change_in, change, change_sems, c, 2),
            part(factor_in, factor, factor_sems, c, 2),
            part(p2_in, p2, p2_sems, c, 2),
        ]

    def store(c):
        return part(new_p, new_p_out, new_p_sems, c, 2)

    start_all(small + [load_ct])
    for n, c in enumerate(order):
        start_all(loads(c))
        if n == 0:
            load_edge.start()
    coupled[...] = couple(me, got, coupling_t.shape[2] // got.shape[1])
    place_halo(me, got_a, got_b, halo)
    wait_all(small + [load_ct, load_edge])

    def finish(pair, counts, fresh, errors):
        more = jnp.zeros((8, cols), F32)
        for i in range(2):
            r = 2 * pair + i
            for at in strips(size):
                move = change[r, at] - factor[r, at] * terms[i * size + at.start : i * size + at.stop]
                new_p[r, at] = p2[r, at] + move
                rate_error = (1.0 / error_scale) * move
                weighted = columns_of(table, pair, i, at)[4] * (rate_error * rate_error)
                more += jnp.sum(weighted.reshape(-1, 8, cols), axis=0)
        return errors + jnp.where(counts, more, jnp.zeros_like(more))

    errors = in_pairs(
        order,
        lambda n, c: None,
        lambda c: wait_all(loads(c)),
        lambda c: outer_terms(coupled, coupling_t, halo, edge, c),
        finish,
        lambda c: store(c).start(),
        terms,
        parts[0],
    )
    both = jnp.concatenate(
        [jnp.sum(errors, axis=0, keepdims=True), jnp.sum(parts[1], axis=0, keepdims=True)], axis=0
    )
    for j in range(parts_out.shape[0]):
        parts_out[j] = both
    each(pairs, lambda c: store(c).wait())


def exchange(side_a, side_b, slots):
    count = lax.axis_size(AXIS)
    got_a = lax.ppermute(side_a, AXIS, [(i, i ^ 1) for i in range(count)])
    pairs = [(i, (i - 1) % count if i % 2 == 0 else (i + 1) % count) for i in range(count)]
    got_b = lax.ppermute(side_b, AXIS, pairs)
    got = lax.all_to_all(slots, AXIS, 0, 0)
    return got_a, got_b, got


def on_device(
    log_rate,
    log_state,
    near_blocks,
    near_columns,
    far_basis,
    far_coupling,
    self_stiffness,
    plate_rate,
    direct_effect,
    evolution_effect,
    triangle_area,
):
    rows, cols = log_rate.shape
    row_blocks, near_count, size, _ = near_blocks.shape
    levels, rank, _ = far_basis.shape
    devices = lax.axis_size(AXIS)
    p = log_rate.reshape(row_blocks, size, cols)
    s = log_state.reshape(row_blocks, size, cols)
    basis = far_basis.reshape(levels * rank, rows)
    coupling = far_coupling.reshape(levels * rank, rows)
    stiff, plate, direct, evolve, area = (
        v.reshape(row_blocks, size)
        for v in (self_stiffness, plate_rate, direct_effect, evolution_effect, triangle_area)
    )
    pairs = row_blocks // 2
    flat_near = near_blocks.reshape(row_blocks * near_count, size, size)
    state = ((row_blocks, size, cols), F32)
    x_kind = ((row_blocks, size, cols), BF16)
    slots_kind = ((devices, rank, cols), BF16)
    side_kind = ((REACH, size, cols), BF16)
    edge_kind = ((sum(map(len, edged_pairs(row_blocks))), 2 * size, REACH * size), BF16)
    ct_kind = ((row_blocks, size, levels * rank), BF16)
    basis_kind = ((levels * rank, rows), BF16)
    near_kind = ((row_blocks * near_count + 1, size, size), BF16)
    halo_kind = ((3 * REACH, size, cols), BF16)
    padded_kind = ((row_blocks + 2 * PAD, size, cols), BF16)
    vector_kind = ((row_blocks, size), F32)
    table_kind = ((size, 8 * row_blocks), F32)
    parts_kind = ((2, 8, cols), F32)
    terms_kind = ((2 * size, cols), F32)
    projected_kind = ((levels * rank, cols), F32)
    coupled_kind = ((levels * rank, cols), BF16)
    where_kind = pltpu.SMEM((row_blocks, 2 * REACH + 1), jnp.int32)
    loads = 4 if row_blocks % 4 == 0 else row_blocks
    near_flops = 2 * rows * near_count * size * cols

    def vmem(*kinds):
        return [pltpu.VMEM(shape, dtype) for shape, dtype in kinds]

    small = pltpu.CompilerParams(vmem_limit_bytes=40 * 1024 * 1024)
    x, slots, side_a, side_b = pl.pallas_call(
        open_kernel,
        out_shape=in_hbm(x_kind, slots_kind, side_kind, side_kind),
        in_specs=[PLAIN] * 2,
        out_specs=(PLAIN,) * 4,
        scratch_shapes=vmem(state, basis_kind, x_kind, slots_kind)
        + [SEMS((loads,)), SEMS(()), SEMS(()), SEMS((3,))],
        name="open",
    )(*hbm(p, basis))

    got_a, got_b, got = exchange(side_a, side_b, slots)
    known, factor, edge, coupling_t, table = pl.pallas_call(
        first_local_kernel,
        out_shape=in_hbm(state, state, edge_kind, ct_kind, table_kind),
        in_specs=[SCALARS] + [PLAIN] * 10,
        out_specs=(PLAIN,) * 5,
        scratch_shapes=vmem(
            padded_kind, near_kind, state, state, basis_kind, *[vector_kind] * 5, state, state, edge_kind, ct_kind,
            table_kind, terms_kind,
        )
        + [where_kind, SEMS(())]
        + [SEMS((pairs,))] * 3
        + [SEMS(()), SEMS((5,)), SEMS((pairs,)), SEMS((pairs,)), SEMS((3,))],
        cost_estimate=cost(near_flops, near_blocks.size * 2),
        name="local_one",
    )(near_columns, *hbm(x, flat_near, p, s, coupling, stiff, plate, direct, evolve, area))

    p2, x, slots, side_a, side_b = pl.pallas_call(
        middle_kernel,
        out_shape=in_hbm(state, x_kind, slots_kind, side_kind, side_kind),
        in_specs=[WHOLE] * 3 + [PLAIN] * 5,
        out_specs=(PLAIN,) * 5,
        scratch_shapes=vmem(
            halo_kind, edge_kind, ct_kind, basis_kind, state, state, state, x_kind, slots_kind, coupled_kind,
            projected_kind, terms_kind,
        )
        + [SEMS((3,)), SEMS((pairs,)), SEMS((pairs,)), SEMS((pairs,)), SEMS(()), SEMS((3,))],
        compiler_params=small,
        name="middle",
    )(got_a, got_b, got, *hbm(edge, coupling_t, basis, known, factor))

    got_a, got_b, got = exchange(side_a, side_b, slots)
    change, factor, new_s, parts = pl.pallas_call(
        second_local_kernel,
        out_shape=in_hbm(state, state, state, parts_kind),
        in_specs=[SCALARS] + [PLAIN] * 6,
        out_specs=(PLAIN,) * 4,
        scratch_shapes=vmem(
            padded_kind, near_kind, state, state, state, table_kind, state, state, state, parts_kind, terms_kind
        )
        + [where_kind, SEMS(())]
        + [SEMS((pairs,))] * 7
        + [SEMS((2,))],
        cost_estimate=cost(near_flops, near_blocks.size * 2),
        name="local_two",
    )(near_columns, *hbm(x, flat_near, p, s, p2, table))

    new_p, parts = pl.pallas_call(
        close_kernel,
        out_shape=in_hbm(state) + like(((devices, 2, cols), F32)),
        in_specs=[WHOLE] * 3 + [PLAIN] * 7,
        out_specs=(PLAIN, WHOLE),
        scratch_shapes=vmem(
            halo_kind, edge_kind, ct_kind, state, state, state, state, coupled_kind, table_kind, parts_kind,
            terms_kind,
        )
        + [SEMS((4,))]
        + [SEMS((pairs,))] * 4,
        compiler_params=small,
        name="close",
    )(got_a, got_b, got, *hbm(edge, coupling_t, p2, change, factor, table, parts))

    totals = lax.all_to_all(parts, AXIS, 0, 0).sum(axis=0)
    error_norm = jnp.sqrt(totals[0] / totals[1] + 1e-06)
    return new_p.reshape(rows, cols), new_s.reshape(rows, cols), error_norm


def solution(mesh):
    split = P(("member", "patch"))
    in_specs = (
        P(("member", "patch"), None),
        P(("member", "patch"), None),
        P(("member", "patch"), None, None, None),
        P(("member", "patch"), None),
        P("member", None, "patch"),
        P("member", None, "patch"),
        split,
        split,
        split,
        split,
        split,
    )
    out_specs = (P(("member", "patch"), None), P(("member", "patch"), None), P("member"))
    return jax.shard_map(
        on_device, mesh=mesh, in_specs=in_specs, out_specs=out_specs, check_vma=False
    )
```

```python
import jax
import jax.numpy as jnp
from jax import lax
from jax.experimental import pallas as pl
from jax.experimental.pallas import tpu as pltpu
from jax.sharding import PartitionSpec as P


REACH = 6
STRIP = 32

step_size = 0.1
damping = 0.5
error_scale = 0.01
half_step = 0.5 * step_size

AXIS = "patch"
F32 = jnp.float32
BF16 = jnp.bfloat16
PLAIN = pl.BlockSpec(memory_space=pltpu.HBM)
WHOLE = pl.BlockSpec(memory_space=pltpu.VMEM)
SCALARS = pl.BlockSpec(memory_space=pltpu.SMEM)
SEMS = pltpu.SemaphoreType.DMA


def cost(flops, moved, exps=0):
    return pl.CostEstimate(flops=flops, bytes_accessed=moved, transcendentals=exps)


def in_hbm(*shapes):
    return tuple(pltpu.HBM(shape, dtype) for shape, dtype in shapes)


def hbm(*arrays):
    return tuple(pltpu.with_memory_space_constraint(v, pltpu.HBM) for v in arrays)


def like(*shapes):
    return tuple(jax.ShapeDtypeStruct(shape, dtype) for shape, dtype in shapes)


def part(src, dst, sems, c, group):
    at = pl.ds(c * group, group)
    return pltpu.make_async_copy(src.at[at], dst.at[at], sems.at[c])


def pair_columns(row_blocks, pair):
    reached = range((2 * pair - REACH) // 2, (2 * pair + 1 + REACH) // 2 + 1)
    count = row_blocks // 2
    return (
        [c for c in reached if c < 0],
        [c for c in reached if 0 <= c < count],
        [c for c in reached if c >= count],
    )


def edge_tiles(row_blocks):
    tiles = []
    for pair in range(row_blocks // 2):
        left, _, right = pair_columns(row_blocks, pair)
        tiles += [(pair, c) for c in left + right]
    return tiles


NT = (((1,), (1,)), ((), ()))


def side_by_side(blocks):
    return jnp.concatenate(blocks, axis=1)


def project(basis, x):
    rates = side_by_side([x[r] for r in range(x.shape[0])])
    return lax.dot_general(rates, basis[...], NT, preferred_element_type=F32).T


def fill_slots(me, projected, slots):
    devices, rank, _ = slots.shape
    for m in range(devices):
        level = max(m.bit_length() - 1, 0)
        slots[me ^ m] = projected[level * rank : (level + 1) * rank].astype(slots.dtype)


def send_copies(me, x, slots, slots_out, a_out, b_out, sems):
    row_blocks = x.shape[0]
    odd = lax.rem(me, 2)
    start_a = (1 - odd) * (row_blocks - REACH)
    start_b = odd * (row_blocks - REACH)
    return [
        pltpu.make_async_copy(slots, slots_out, sems.at[0]),
        pltpu.make_async_copy(x.at[pl.ds(start_a, REACH)], a_out, sems.at[1]),
        pltpu.make_async_copy(x.at[pl.ds(start_b, REACH)], b_out, sems.at[2]),
    ]


def open_kernel(
    p_in, basis_in, x_out, slots_out, a_out, b_out,
    p, basis, x, slots, p_sems, x_sem, basis_sem, send_sems,
):
    row_blocks, _, _ = p.shape
    chunks = p_sems.shape[0]
    group = row_blocks // chunks
    me = lax.axis_index(AXIS)
    load_basis = pltpu.make_async_copy(basis_in, basis, basis_sem)
    for c in range(chunks):
        part(p_in, p, p_sems, c, group).start()
    load_basis.start()
    for c in range(chunks):
        part(p_in, p, p_sems, c, group).wait()
        for r in range(c * group, (c + 1) * group):
            x[r] = jnp.exp(p[r]).astype(BF16).T
    send = send_copies(me, x, slots, slots_out, a_out, b_out, send_sems)
    send.append(pltpu.make_async_copy(x, x_out, x_sem))
    for copy in send[1:]:
        copy.start()
    load_basis.wait()
    fill_slots(me, project(basis, x), slots)
    send[0].start()
    for copy in send:
        copy.wait()


def find_blocks(columns, where):
    row_blocks, near_count = columns.shape
    total = row_blocks * lax.axis_size(AXIS)
    first = row_blocks * lax.axis_index(AXIS)

    def row(r, carry):
        for o in range(2 * REACH + 1):
            where[r, o] = row_blocks * near_count
        for k in range(near_count):
            offset = columns[r, k] - first - r
            offset = jnp.where(offset > REACH, offset - total, offset)
            offset = jnp.where(offset < -REACH, offset + total, offset)
            where[r, offset + REACH] = r * near_count + k
        return carry

    lax.fori_loop(0, row_blocks, row, 0)


def near_block(near, where, r, c):
    if abs(c - r) > REACH:
        return jnp.zeros(near.shape[1:], near.dtype)
    return near[where[r, c - r + REACH]]


def near_product(near, x, where, pair):
    own = pair_columns(x.shape[0], pair)[1]
    reached = range(2 * own[0], 2 * own[-1] + 2)
    tiles = [side_by_side([near_block(near, where, r, c) for c in reached]) for r in (2 * pair, 2 * pair + 1)]
    rates = side_by_side([x[c] for c in reached])
    return lax.dot_general(rates, jnp.concatenate(tiles, axis=0), NT, preferred_element_type=F32)


def strips(size):
    step = STRIP if size % STRIP == 0 else size
    return [slice(i, i + step) for i in range(0, size, step)]


def known_rates(velocity, state, near_term, rows):
    stiff, plate, direct, evolve = rows
    factor = 1.0 / (direct + damping * velocity)
    return (stiff * (plate - velocity) - near_term - evolve * state) * factor, factor


def in_pairs(pairs, wait, product, finish, store):
    wait(0)
    product(0)
    for pair in range(pairs):
        if pair + 1 < pairs:
            wait(pair + 1)
            product(pair + 1)
        finish(pair)
        store(pair)


def vector_loads(sources, targets, sems):
    return [
        pltpu.make_async_copy(src, dst, sems.at[q]) for q, (src, dst) in enumerate(zip(sources, targets))
    ]


def start_all(copies):
    for copy in copies:
        copy.start()


def wait_all(copies):
    for copy in copies:
        copy.wait()


def first_local_kernel(
    columns, x_in, near_in, p_in, s_in, stiff_in, plate_in, direct_in, evolve_in,
    known_out, factor_out, edge_out,
    x, near, p, s, stiff, plate, direct, evolve, known, factor, edge, products, turned_p, turned_s,
    where, x_sem, near_sems, p_sems, s_sems, vector_sems, known_sems, factor_sems, rest_sems,
):
    row_blocks, size, _ = x.shape
    pairs = row_blocks // 2
    span = (near.shape[0] - 1) // pairs
    vectors = (stiff, plate, direct, evolve)
    load_x = pltpu.make_async_copy(x_in, x, x_sem)
    load_vectors = vector_loads((stiff_in, plate_in, direct_in, evolve_in), vectors, vector_sems)

    def loads(c):
        return [part(near_in, near, near_sems, c, span), part(p_in, p, p_sems, c, 2), part(s_in, s, s_sems, c, 2)]

    def stores(c):
        return [part(known, known_out, known_sems, c, 2), part(factor, factor_out, factor_sems, c, 2)]

    start_all([load_x] + loads(0) + load_vectors)
    for c in range(1, pairs):
        start_all(loads(c))
    near[near.shape[0] - 1] = jnp.zeros(near.shape[1:], near.dtype)
    find_blocks(columns, where)
    wait_all(load_vectors + [load_x])

    def product(pair):
        products[pair] = near_product(near, x, where, pair)

    def finish(pair):
        for i in range(2):
            r = 2 * pair + i
            rows = [v[r : r + 1] for v in vectors]
            turned_p[i] = p[r].T
            turned_s[i] = s[r].T
            for at in strips(size):
                now = turned_p[i, at]
                velocity = jnp.exp(now)
                state = jnp.exp(-turned_s[i, at]) - velocity
                near_term = products[pair, at, i * size : (i + 1) * size]
                rate, scale = known_rates(velocity, state, near_term, rows)
                known[r, at] = now + step_size * rate
                factor[r, at] = step_size * scale

    in_pairs(
        pairs,
        lambda c: wait_all(loads(c)),
        product,
        finish,
        lambda c: start_all(stores(c)),
    )
    for n, (pair, c) in enumerate(edge_tiles(row_blocks)):
        for i in range(2):
            for j in range(2):
                edge[n, i * size : (i + 1) * size, j * size : (j + 1) * size] = near_block(
                    near, where, 2 * pair + i, 2 * c + j
                )
    store_edge = pltpu.make_async_copy(edge, edge_out, rest_sems.at[0])
    store_edge.start()
    for c in range(pairs):
        wait_all(stores(c))
    store_edge.wait()


def second_local_kernel(
    columns, x_in, near_in, p_in, s_in, p2_in, stiff_in, plate_in, direct_in, evolve_in, area_in,
    change_out, factor_out, new_s_out, errors_out,
    x, near, p, s, p2, stiff, plate, direct, evolve, area, change, factor, new_s, errors, products,
    turned_p, turned_s, ended_s,
    where, x_sem, near_sems, p_sems, s_sems, p2_sems, vector_sems, change_sems, factor_sems, new_s_sems, rest_sems,
):
    row_blocks, size, _ = x.shape
    pairs = row_blocks // 2
    span = (near.shape[0] - 1) // pairs
    vectors = (stiff, plate, direct, evolve, area)
    load_x = pltpu.make_async_copy(x_in, x, x_sem)
    load_vectors = vector_loads((stiff_in, plate_in, direct_in, evolve_in, area_in), vectors, vector_sems)

    def loads(c):
        return [
            part(near_in, near, near_sems, c, span),
            part(p_in, p, p_sems, c, 2),
            part(s_in, s, s_sems, c, 2),
            part(p2_in, p2, p2_sems, c, 2),
        ]

    def stores(c):
        return [
            part(change, change_out, change_sems, c, 2),
            part(factor, factor_out, factor_sems, c, 2),
            part(new_s, new_s_out, new_s_sems, c, 2),
        ]

    start_all([load_x] + loads(0) + load_vectors)
    for c in range(1, pairs):
        start_all(loads(c))
    near[near.shape[0] - 1] = jnp.zeros(near.shape[1:], near.dtype)
    find_blocks(columns, where)
    wait_all(load_vectors + [load_x])

    def product(pair):
        products[pair] = near_product(near, x, where, pair)

    def finish(pair):
        for i in range(2):
            r = 2 * pair + i
            rows = [v[r : r + 1] for v in vectors]
            turned_p[i] = p[r].T
            turned_s[i] = s[r].T
            for at in strips(size):
                before, now, start = turned_p[i, at], p2[r, at], turned_s[i, at]
                state_a = jnp.exp(-start) - jnp.exp(before)
                velocity = jnp.exp(now)
                state_b = jnp.exp(-(start + step_size * state_a)) - velocity
                near_term = products[pair, at, i * size : (i + 1) * size]
                rate, scale = known_rates(velocity, state_b, near_term, rows[:4])
                change[r, at] = half_step * rate - (half_step / step_size) * (now - before)
                factor[r, at] = half_step * scale
                ended_s[i, at] = start + half_step * (state_a + state_b)
                state_error = (half_step / error_scale) * (state_b - state_a)
                weighted = rows[4] * (state_error * state_error)
                errors[at] = weighted + errors[at] if r else weighted
            new_s[r] = ended_s[i].T

    in_pairs(
        pairs,
        lambda c: wait_all(loads(c)),
        product,
        finish,
        lambda c: start_all(stores(c)),
    )
    store_errors = pltpu.make_async_copy(errors, errors_out, rest_sems.at[0])
    store_errors.start()
    for c in range(pairs):
        wait_all(stores(c))
    store_errors.wait()


def couple(me, got, levels):
    devices = got.shape[0]
    sums = []
    for level in range(levels):
        total = got[me ^ (1 << level)].astype(F32)
        for m in range((1 << level) + 1, min(2 << level, devices)):
            total += got[me ^ m].astype(F32)
        sums.append(total)
    return jnp.concatenate(sums, axis=0).T.astype(BF16)


def pair_order(row_blocks):
    edged = {pair for pair, _ in edge_tiles(row_blocks)}
    pairs = range(row_blocks // 2)
    return [c for c in pairs if c not in edged] + [c for c in pairs if c in edged]


def outer_terms(coupled, coupling, halo, edge, pair, row_blocks):
    size = halo.shape[2]
    terms = jnp.dot(
        coupled, coupling[:, 2 * pair * size : 2 * (pair + 1) * size], preferred_element_type=F32
    )
    rates, tiles = [], []
    for n, (row_pair, c) in enumerate(edge_tiles(row_blocks)):
        if row_pair == pair:
            at = REACH + 2 * c if c < 0 else REACH + 2 * c - row_blocks
            tiles.append(edge[n])
            rates += [halo[at], halo[at + 1]]
    if tiles:
        terms += lax.dot_general(side_by_side(rates), side_by_side(tiles), NT, preferred_element_type=F32)
    return terms


def place_halo(me, got_a, got_b, halo):
    odd = lax.rem(me, 2)
    at_a = (1 - odd) * REACH
    at_b = odd * REACH
    for t in range(REACH):
        halo[at_a + t] = got_a[t]
        halo[at_b + t] = got_b[t]


def run_rows(order, first_edged, loads, outer, row, done, start):
    ahead = 4
    for copy in outer[:1]:
        copy.start()
    for c in order[:ahead]:
        for copy in loads(c):
            copy.start()
        if c == order[0]:
            for copy in outer[1:]:
                copy.start()
    start()
    for n, c in enumerate(order):
        if n == 0:
            outer[0].wait()
        if n == first_edged:
            for copy in outer[1:]:
                copy.wait()
        for copy in loads(c):
            copy.wait()
        if n + ahead < len(order):
            for copy in loads(order[n + ahead]):
                copy.start()
        row(c)
        done(c)


def middle_kernel(
    got_a, got_b, got, edge_in, coupling_in, basis_in, known_in, factor_in,
    p2_out, x_out, slots_out, a_out, b_out,
    halo, edge, coupling, basis, known, factor, p2, x, slots, coupled,
    outer_sems, known_sems, factor_sems, p2_sems, x_sem, send_sems,
):
    row_blocks, size, _ = known.shape
    me = lax.axis_index(AXIS)
    order = pair_order(row_blocks)
    outer = [
        pltpu.make_async_copy(coupling_in, coupling, outer_sems.at[0]),
        pltpu.make_async_copy(edge_in, edge, outer_sems.at[1]),
        pltpu.make_async_copy(basis_in, basis, outer_sems.at[2]),
    ]

    def loads(c):
        return [part(known_in, known, known_sems, c, 2), part(factor_in, factor, factor_sems, c, 2)]

    def start():
        coupled[...] = couple(me, got, basis.shape[0] // got.shape[1])
        place_halo(me, got_a, got_b, halo)

    def row(c):
        terms = outer_terms(coupled[...], coupling, halo, edge, c, row_blocks)
        for i in range(2):
            r = 2 * c + i
            value = known[r] - factor[r] * terms[:, i * size : (i + 1) * size]
            p2[r] = value
            x[r] = jnp.exp(value).astype(BF16)

    def done(c):
        part(p2, p2_out, p2_sems, c, 2).start()

    run_rows(order, order.index(0), loads, outer, row, done, start)
    send = send_copies(me, x, slots, slots_out, a_out, b_out, send_sems)
    send.append(pltpu.make_async_copy(x, x_out, x_sem))
    start_all(send[1:])
    fill_slots(me, project(basis, x), slots)
    send[0].start()
    wait_all(send + [part(p2, p2_out, p2_sems, c, 2) for c in order])


def close_kernel(
    got_a, got_b, got, edge_in, coupling_in, p2_in, change_in, factor_in, area_in, errors_in,
    new_p_out, parts_out,
    halo, edge, coupling, p2, change, factor, new_p, coupled, area, errors,
    outer_sems, p2_sems, change_sems, factor_sems, new_p_sems,
):
    row_blocks, size, _ = change.shape
    me = lax.axis_index(AXIS)
    order = pair_order(row_blocks)
    outer = [
        pltpu.make_async_copy(coupling_in, coupling, outer_sems.at[0]),
        pltpu.make_async_copy(edge_in, edge, outer_sems.at[1]),
    ]
    extra = [
        pltpu.make_async_copy(area_in, area, outer_sems.at[2]),
        pltpu.make_async_copy(errors_in, errors, outer_sems.at[3]),
    ]

    def loads(c):
        return [
            part(change_in, change, change_sems, c, 2),
            part(factor_in, factor, factor_sems, c, 2),
            part(p2_in, p2, p2_sems, c, 2),
        ]

    def start():
        start_all(extra)
        coupled[...] = couple(me, got, coupling.shape[0] // got.shape[1])
        place_halo(me, got_a, got_b, halo)
        wait_all(extra)

    def row(c):
        terms = outer_terms(coupled[...], coupling, halo, edge, c, row_blocks)
        for i in range(2):
            r = 2 * c + i
            move = change[r] - factor[r] * terms[:, i * size : (i + 1) * size]
            new_p[r] = (p2[r] + move).T
            rate_error = (1.0 / error_scale) * move
            errors[...] += area[r : r + 1] * (rate_error * rate_error)

    def done(c):
        part(new_p, new_p_out, new_p_sems, c, 2).start()

    run_rows(order, order.index(0), loads, outer, row, done, start)
    total = jnp.sum(errors[...].T, axis=0, keepdims=True)
    areas = jnp.sum(jnp.sum(area[...], axis=0, keepdims=True), axis=1, keepdims=True)
    both = jnp.concatenate([total, jnp.broadcast_to(areas, total.shape)], axis=0)
    for j in range(parts_out.shape[0]):
        parts_out[j] = both
    wait_all([part(new_p, new_p_out, new_p_sems, c, 2) for c in order])


def exchange(side_a, side_b, slots):
    count = lax.axis_size(AXIS)
    got_a = lax.ppermute(side_a, AXIS, [(i, i ^ 1) for i in range(count)])
    pairs = [(i, (i - 1) % count if i % 2 == 0 else (i + 1) % count) for i in range(count)]
    got_b = lax.ppermute(side_b, AXIS, pairs)
    got = lax.all_to_all(slots, AXIS, 0, 0)
    return got_a, got_b, got


def on_device(
    log_rate,
    log_state,
    near_blocks,
    near_columns,
    far_basis,
    far_coupling,
    self_stiffness,
    plate_rate,
    direct_effect,
    evolution_effect,
    triangle_area,
):
    rows, cols = log_rate.shape
    row_blocks, near_count, size, _ = near_blocks.shape
    levels, rank, _ = far_basis.shape
    devices = lax.axis_size(AXIS)
    p = log_rate.reshape(row_blocks, size, cols)
    s = log_state.reshape(row_blocks, size, cols)
    basis = far_basis.reshape(levels * rank, rows)
    coupling = far_coupling.reshape(levels * rank, rows)
    stiff, plate, direct, evolve, area = (
        v.reshape(row_blocks, size)
        for v in (self_stiffness, plate_rate, direct_effect, evolution_effect, triangle_area)
    )
    pairs = row_blocks // 2
    flat_near = near_blocks.reshape(row_blocks * near_count, size, size)
    state = ((row_blocks, size, cols), F32)
    x_kind = ((row_blocks, size, cols), BF16)
    slots_kind = ((devices, rank, cols), BF16)
    side_kind = ((REACH, size, cols), BF16)
    edge_kind = ((len(edge_tiles(row_blocks)), 2 * size, 2 * size), BF16)
    basis_kind = ((levels * rank, rows), BF16)
    near_kind = ((row_blocks * near_count + 1, size, size), BF16)
    halo_kind = ((2 * REACH, size, cols), BF16)
    vector_kind = ((row_blocks, size), F32)
    errors_kind = ((cols, size), F32)
    products_kind = ((pairs, cols, 2 * size), F32)
    coupled_kind = ((cols, levels * rank), BF16)
    turned_kind = ((2, cols, size), F32)
    where_kind = pltpu.SMEM((row_blocks, 2 * REACH + 1), jnp.int32)
    loads = 4 if row_blocks % 4 == 0 else row_blocks
    near_flops = 2 * rows * near_count * size * cols

    def vmem(*kinds):
        return [pltpu.VMEM(shape, dtype) for shape, dtype in kinds]

    small = pltpu.CompilerParams(vmem_limit_bytes=40 * 1024 * 1024)
    x, slots, side_a, side_b = pl.pallas_call(
        open_kernel,
        out_shape=in_hbm(x_kind, slots_kind, side_kind, side_kind),
        in_specs=[PLAIN] * 2,
        out_specs=(PLAIN,) * 4,
        scratch_shapes=vmem(state, basis_kind, x_kind, slots_kind)
        + [SEMS((loads,)), SEMS(()), SEMS(()), SEMS((3,))],
        name="open",
    )(*hbm(p, basis))

    got_a, got_b, got = exchange(side_a, side_b, slots)
    known, factor, edge = pl.pallas_call(
        first_local_kernel,
        out_shape=in_hbm(state, state, edge_kind),
        in_specs=[SCALARS] + [PLAIN] * 8,
        out_specs=(PLAIN,) * 3,
        scratch_shapes=vmem(
            x_kind, near_kind, state, state, *[vector_kind] * 4, state, state, edge_kind, products_kind,
            turned_kind, turned_kind,
        )
        + [where_kind, SEMS(())]
        + [SEMS((pairs,))] * 3
        + [SEMS((4,)), SEMS((pairs,)), SEMS((pairs,)), SEMS((1,))],
        cost_estimate=cost(near_flops, near_blocks.size * 2),
        name="local_one",
    )(near_columns, *hbm(x, flat_near, p, s, stiff, plate, direct, evolve))

    p2, x, slots, side_a, side_b = pl.pallas_call(
        middle_kernel,
        out_shape=in_hbm(state, x_kind, slots_kind, side_kind, side_kind),
        in_specs=[WHOLE] * 3 + [PLAIN] * 5,
        out_specs=(PLAIN,) * 5,
        scratch_shapes=vmem(
            halo_kind, edge_kind, basis_kind, basis_kind, state, state, state, x_kind, slots_kind, coupled_kind
        )
        + [SEMS((3,)), SEMS((pairs,)), SEMS((pairs,)), SEMS((pairs,)), SEMS(()), SEMS((3,))],
        compiler_params=small,
        name="middle",
    )(got_a, got_b, got, *hbm(edge, coupling, basis, known, factor))

    got_a, got_b, got = exchange(side_a, side_b, slots)
    change, factor, new_s, errors = pl.pallas_call(
        second_local_kernel,
        out_shape=in_hbm(state, state, state, errors_kind),
        in_specs=[SCALARS] + [PLAIN] * 10,
        out_specs=(PLAIN,) * 4,
        scratch_shapes=vmem(
            x_kind, near_kind, state, state, state, *[vector_kind] * 5, state, state, state, errors_kind,
            products_kind, turned_kind, turned_kind, turned_kind,
        )
        + [where_kind, SEMS(())]
        + [SEMS((pairs,))] * 4
        + [SEMS((5,))]
        + [SEMS((pairs,))] * 3
        + [SEMS((1,))],
        cost_estimate=cost(near_flops, near_blocks.size * 2),
        name="local_two",
    )(near_columns, *hbm(x, flat_near, p, s, p2, stiff, plate, direct, evolve, area))

    new_p, parts = pl.pallas_call(
        close_kernel,
        out_shape=in_hbm(state) + like(((devices, 2, cols), F32)),
        in_specs=[WHOLE] * 3 + [PLAIN] * 7,
        out_specs=(PLAIN, WHOLE),
        scratch_shapes=vmem(
            halo_kind, edge_kind, basis_kind, state, state, state, state, coupled_kind, vector_kind, errors_kind
        )
        + [SEMS((4,))]
        + [SEMS((pairs,))] * 4,
        compiler_params=small,
        name="close",
    )(got_a, got_b, got, *hbm(edge, coupling, p2, change, factor, area, errors))

    totals = lax.all_to_all(parts, AXIS, 0, 0).sum(axis=0)
    error_norm = jnp.sqrt(totals[0] / totals[1] + 1e-06)
    return new_p.reshape(rows, cols), new_s.reshape(rows, cols), error_norm


def solution(mesh):
    split = P(("member", "patch"))
    in_specs = (
        P(("member", "patch"), None),
        P(("member", "patch"), None),
        P(("member", "patch"), None, None, None),
        P(("member", "patch"), None),
        P("member", None, "patch"),
        P("member", None, "patch"),
        split,
        split,
        split,
        split,
        split,
    )
    out_specs = (P(("member", "patch"), None), P(("member", "patch"), None), P("member"))
    return jax.shard_map(
        on_device, mesh=mesh, in_specs=in_specs, out_specs=out_specs, check_vma=False
    )
```

```python
import jax
import jax.numpy as jnp
from jax import lax
from jax.experimental import pallas as pl
from jax.experimental.pallas import tpu as pltpu
from jax.sharding import PartitionSpec as P


REACH = 6
STRIP = 32
AHEAD = 3
BUSY = 10**10

step_size = 0.1
damping = 0.5
error_scale = 0.01
half_step = 0.5 * step_size

AXIS = "patch"
F32 = jnp.float32
BF16 = jnp.bfloat16
PLAIN = pl.BlockSpec(memory_space=pltpu.HBM)
WHOLE = pl.BlockSpec(memory_space=pltpu.VMEM)
SCALARS = pl.BlockSpec(memory_space=pltpu.SMEM)
SEMS = pltpu.SemaphoreType.DMA


def cost(flops, moved, exps=0):
    return pl.CostEstimate(flops=flops, bytes_accessed=moved, transcendentals=exps)


def in_hbm(*shapes):
    return tuple(pltpu.HBM(shape, dtype) for shape, dtype in shapes)


def hbm(*arrays):
    return tuple(pltpu.with_memory_space_constraint(v, pltpu.HBM) for v in arrays)


def resident(*arrays):
    return tuple(pltpu.with_memory_space_constraint(v, pltpu.VMEM) for v in arrays)


def like(*shapes):
    return tuple(jax.ShapeDtypeStruct(shape, dtype) for shape, dtype in shapes)


def part(src, dst, sems, c, group):
    at = pl.ds(c * group, group)
    return pltpu.make_async_copy(src.at[at], dst.at[at], sems.at[c])


def pair_columns(row_blocks, pair):
    reached = range((2 * pair - REACH) // 2, (2 * pair + 1 + REACH) // 2 + 1)
    count = row_blocks // 2
    return (
        [c for c in reached if c < 0],
        [c for c in reached if 0 <= c < count],
        [c for c in reached if c >= count],
    )


def edge_tiles(row_blocks):
    tiles = []
    for pair in range(row_blocks // 2):
        left, _, right = pair_columns(row_blocks, pair)
        tiles += [(pair, c) for c in left + right]
    return tiles


NT = (((1,), (1,)), ((), ()))


def side_by_side(blocks):
    return jnp.concatenate(blocks, axis=1)


def project(basis, x):
    rates = side_by_side([x[r] for r in range(x.shape[0])])
    return lax.dot_general(rates, basis[...], NT, preferred_element_type=F32).T


def fill_slots(me, projected, slots):
    devices, rank, _ = slots.shape
    for m in range(devices):
        level = max(m.bit_length() - 1, 0)
        slots[me ^ m] = projected[level * rank : (level + 1) * rank].astype(slots.dtype)


def send_copies(me, x, slots, slots_out, a_out, b_out, sems):
    row_blocks = x.shape[0]
    odd = lax.rem(me, 2)
    start_a = (1 - odd) * (row_blocks - REACH)
    start_b = odd * (row_blocks - REACH)
    return [
        pltpu.make_async_copy(slots, slots_out, sems.at[0]),
        pltpu.make_async_copy(x.at[pl.ds(start_a, REACH)], a_out, sems.at[1]),
        pltpu.make_async_copy(x.at[pl.ds(start_b, REACH)], b_out, sems.at[2]),
    ]


def open_kernel(
    p_in, basis_in, x_out, slots_out, a_out, b_out,
    p, basis, x, slots, p_sems, x_sem, basis_sem, send_sems,
):
    row_blocks, _, _ = p.shape
    chunks = p_sems.shape[0]
    group = row_blocks // chunks
    me = lax.axis_index(AXIS)
    load_basis = pltpu.make_async_copy(basis_in, basis, basis_sem)
    for c in range(chunks):
        part(p_in, p, p_sems, c, group).start()
    load_basis.start()
    for c in range(chunks):
        part(p_in, p, p_sems, c, group).wait()
        for r in range(c * group, (c + 1) * group):
            x[r] = jnp.exp(p[r]).astype(BF16).T
    send = send_copies(me, x, slots, slots_out, a_out, b_out, send_sems)
    send.append(pltpu.make_async_copy(x, x_out, x_sem))
    for copy in send[1:]:
        copy.start()
    load_basis.wait()
    fill_slots(me, project(basis, x), slots)
    send[0].start()
    for copy in send:
        copy.wait()


def find_blocks(columns, where):
    row_blocks, near_count = columns.shape
    total = row_blocks * lax.axis_size(AXIS)
    first = row_blocks * lax.axis_index(AXIS)

    def row(r, carry):
        for o in range(2 * REACH + 1):
            where[r, o] = -1
        for k in range(near_count):
            offset = columns[r, k] - first - r
            offset = jnp.where(offset > REACH, offset - total, offset)
            offset = jnp.where(offset < -REACH, offset + total, offset)
            where[r, offset + REACH] = r * near_count + k
        return carry

    lax.fori_loop(0, row_blocks, row, 0)


def near_block(near, where, r, c):
    offset = c - r
    if abs(offset) > REACH:
        return jnp.zeros(near.shape[1:], near.dtype)
    at = where[r, offset + REACH]
    block = near[jnp.maximum(at, 0)]
    if offset == 0 or abs(offset) == REACH:
        return block
    return jnp.where(at >= 0, block, jnp.zeros_like(block))


def near_product(near, x, where, pair):
    own = pair_columns(x.shape[0], pair)[1]
    reached = range(2 * own[0], 2 * own[-1] + 2)
    tiles = [side_by_side([near_block(near, where, r, c) for c in reached]) for r in (2 * pair, 2 * pair + 1)]
    rates = side_by_side([x[c] for c in reached])
    return lax.dot_general(rates, jnp.concatenate(tiles, axis=0), NT, preferred_element_type=F32)


def strips(size):
    step = STRIP if size % STRIP == 0 else size
    return [slice(i, i + step) for i in range(0, size, step)]


def known_rates(velocity, state, near_term, rows):
    stiff, plate, direct, evolve = rows
    factor = 1.0 / (direct + damping * velocity)
    return (stiff * (plate - velocity) - near_term - evolve * state) * factor, factor


def in_pairs(pairs, wait, product, finish, store):
    wait(0)
    product(0)
    for pair in range(pairs):
        if pair + 1 < pairs:
            wait(pair + 1)
            product(pair + 1)
        finish(pair)
        store(pair)


def start_all(copies):
    for copy in copies:
        copy.start()


def wait_all(copies):
    for copy in copies:
        copy.wait()


def first_local_kernel(
    columns, x_in, near_in, p, s, stiff, plate, direct, evolve,
    known_out, factor_out, edge_out,
    x, near, known, factor, edge, products, turned_p, turned_s,
    where, x_sem, near_sems, known_sems, factor_sems, rest_sems,
):
    row_blocks, size, _ = x.shape
    pairs = row_blocks // 2
    vectors = (stiff, plate, direct, evolve)
    span = near.shape[0] // pairs
    load_x = pltpu.make_async_copy(x_in, x, x_sem)

    def loads(c):
        return [part(near_in, near, near_sems, c, span)]

    def stores(c):
        return [part(known, known_out, known_sems, c, 2), part(factor, factor_out, factor_sems, c, 2)]

    load_x.start()
    for c in range(AHEAD):
        start_all(loads(c))
    find_blocks(columns, where)
    load_x.wait()

    def product(pair):
        if pair + AHEAD < pairs:
            start_all(loads(pair + AHEAD))
        products[pair] = near_product(near, x, where, pair)

    def finish(pair):
        for i in range(2):
            r = 2 * pair + i
            rows = [v[r : r + 1] for v in vectors]
            turned_p[i] = p[r].T
            turned_s[i] = s[r].T
            for at in strips(size):
                now = turned_p[i, at]
                velocity = jnp.exp(now)
                state = jnp.exp(-turned_s[i, at]) - velocity
                near_term = products[pair, at, i * size : (i + 1) * size]
                rate, scale = known_rates(velocity, state, near_term, rows)
                known[r, at] = now + step_size * rate
                factor[r, at] = step_size * scale

    in_pairs(
        pairs,
        lambda c: wait_all(loads(c)),
        product,
        finish,
        lambda c: start_all(stores(c)),
    )
    for n, (pair, c) in enumerate(edge_tiles(row_blocks)):
        for i in range(2):
            for j in range(2):
                edge[n, i * size : (i + 1) * size, j * size : (j + 1) * size] = near_block(
                    near, where, 2 * pair + i, 2 * c + j
                )
    store_edge = pltpu.make_async_copy(edge, edge_out, rest_sems.at[0])
    store_edge.start()
    for c in range(pairs):
        wait_all(stores(c))
    store_edge.wait()


def second_local_kernel(
    columns, x_in, near_in, p, s, p2_in, stiff, plate, direct, evolve, area,
    change_out, factor_out, new_s_out, errors_out,
    x, near, p2, change, factor, new_s, errors, products,
    turned_p, turned_s, ended_s,
    where, x_sem, near_sems, p2_sems, change_sems, factor_sems, new_s_sems, rest_sems,
):
    row_blocks, size, _ = x.shape
    pairs = row_blocks // 2
    vectors = (stiff, plate, direct, evolve, area)
    span = near.shape[0] // pairs
    load_x = pltpu.make_async_copy(x_in, x, x_sem)

    def loads(c):
        return [part(near_in, near, near_sems, c, span), part(p2_in, p2, p2_sems, c, 2)]

    def stores(c):
        return [
            part(change, change_out, change_sems, c, 2),
            part(factor, factor_out, factor_sems, c, 2),
            part(new_s, new_s_out, new_s_sems, c, 2),
        ]

    load_x.start()
    for c in range(AHEAD):
        start_all(loads(c))
    find_blocks(columns, where)
    load_x.wait()

    def product(pair):
        if pair + AHEAD < pairs:
            start_all(loads(pair + AHEAD))
        products[pair] = near_product(near, x, where, pair)

    def finish(pair):
        for i in range(2):
            r = 2 * pair + i
            rows = [v[r : r + 1] for v in vectors]
            turned_p[i] = p[r].T
            turned_s[i] = s[r].T
            for at in strips(size):
                before, now, start = turned_p[i, at], p2[r, at], turned_s[i, at]
                state_a = jnp.exp(-start) - jnp.exp(before)
                velocity = jnp.exp(now)
                state_b = jnp.exp(-(start + step_size * state_a)) - velocity
                near_term = products[pair, at, i * size : (i + 1) * size]
                rate, scale = known_rates(velocity, state_b, near_term, rows[:4])
                change[r, at] = half_step * rate - (half_step / step_size) * (now - before)
                factor[r, at] = half_step * scale
                ended_s[i, at] = start + half_step * (state_a + state_b)
                state_error = (half_step / error_scale) * (state_b - state_a)
                weighted = rows[4] * (state_error * state_error)
                errors[at] = weighted + errors[at] if r else weighted
            new_s[r] = ended_s[i].T

    in_pairs(
        pairs,
        lambda c: wait_all(loads(c)),
        product,
        finish,
        lambda c: start_all(stores(c)),
    )
    store_errors = pltpu.make_async_copy(errors, errors_out, rest_sems.at[0])
    store_errors.start()
    for c in range(pairs):
        wait_all(stores(c))
    store_errors.wait()


def couple(me, got, levels):
    devices = got.shape[0]
    sums = []
    for level in range(levels):
        total = got[me ^ (1 << level)].astype(F32)
        for m in range((1 << level) + 1, min(2 << level, devices)):
            total += got[me ^ m].astype(F32)
        sums.append(total)
    return jnp.concatenate(sums, axis=0).T.astype(BF16)


def pair_order(row_blocks):
    edged = {pair for pair, _ in edge_tiles(row_blocks)}
    pairs = range(row_blocks // 2)
    return [c for c in pairs if c not in edged] + [c for c in pairs if c in edged]


def outer_terms(coupled, coupling, halo, edge, pair, row_blocks):
    size = halo.shape[2]
    terms = jnp.dot(
        coupled, coupling[:, 2 * pair * size : 2 * (pair + 1) * size], preferred_element_type=F32
    )
    rates, tiles = [], []
    for n, (row_pair, c) in enumerate(edge_tiles(row_blocks)):
        if row_pair == pair:
            at = REACH + 2 * c if c < 0 else REACH + 2 * c - row_blocks
            tiles.append(edge[n])
            rates += [halo[at], halo[at + 1]]
    if tiles:
        terms += lax.dot_general(side_by_side(rates), side_by_side(tiles), NT, preferred_element_type=F32)
    return terms


def place_halo(me, got_a, got_b, halo):
    odd = lax.rem(me, 2)
    at_a = (1 - odd) * REACH
    at_b = odd * REACH
    for t in range(REACH):
        halo[at_a + t] = got_a[t]
        halo[at_b + t] = got_b[t]


def run_rows(order, first_edged, loads, outer, row, done, start):
    ahead = 4
    for c in order[:ahead]:
        start_all(loads(c))
        if c == order[0]:
            start_all(outer)
    start()
    for n, c in enumerate(order):
        if n == first_edged:
            wait_all(outer)
        wait_all(loads(c))
        if n + ahead < len(order):
            start_all(loads(order[n + ahead]))
        row(c)
        done(c)


def middle_kernel(
    got_a, got_b, got, edge_in, coupling, basis_in, known_in, factor_in,
    p2_out, x_out, slots_out, a_out, b_out,
    halo, edge, basis, known, factor, p2, x, slots, coupled,
    outer_sems, known_sems, factor_sems, p2_sems, x_sem, send_sems,
):
    row_blocks, size, _ = known.shape
    me = lax.axis_index(AXIS)
    order = pair_order(row_blocks)
    outer = [
        pltpu.make_async_copy(edge_in, edge, outer_sems.at[0]),
        pltpu.make_async_copy(basis_in, basis, outer_sems.at[1]),
    ]

    def loads(c):
        return [part(known_in, known, known_sems, c, 2), part(factor_in, factor, factor_sems, c, 2)]

    def start():
        coupled[...] = couple(me, got, basis.shape[0] // got.shape[1])
        place_halo(me, got_a, got_b, halo)

    def row(c):
        terms = outer_terms(coupled[...], coupling, halo, edge, c, row_blocks)
        for i in range(2):
            r = 2 * c + i
            value = known[r] - factor[r] * terms[:, i * size : (i + 1) * size]
            p2[r] = value
            x[r] = jnp.exp(value).astype(BF16)

    def done(c):
        part(p2, p2_out, p2_sems, c, 2).start()

    run_rows(order, order.index(0), loads, outer, row, done, start)
    send = send_copies(me, x, slots, slots_out, a_out, b_out, send_sems)
    send.append(pltpu.make_async_copy(x, x_out, x_sem))
    start_all(send[1:])
    fill_slots(me, project(basis, x), slots)
    send[0].start()
    wait_all(send + [part(p2, p2_out, p2_sems, c, 2) for c in order])


def close_kernel(
    got_a, got_b, got, edge_in, coupling, p2_in, change_in, factor_in, area_in, errors_in,
    new_p_out, parts_out,
    halo, edge, p2, change, factor, new_p, coupled, area, errors,
    outer_sems, p2_sems, change_sems, factor_sems, new_p_sems,
):
    row_blocks, size, _ = change.shape
    me = lax.axis_index(AXIS)
    order = pair_order(row_blocks)
    outer = [pltpu.make_async_copy(edge_in, edge, outer_sems.at[0])]
    extra = [
        pltpu.make_async_copy(area_in, area, outer_sems.at[1]),
        pltpu.make_async_copy(errors_in, errors, outer_sems.at[2]),
    ]

    def loads(c):
        return [
            part(change_in, change, change_sems, c, 2),
            part(factor_in, factor, factor_sems, c, 2),
            part(p2_in, p2, p2_sems, c, 2),
        ]

    def start():
        start_all(extra)
        coupled[...] = couple(me, got, coupling.shape[0] // got.shape[1])
        place_halo(me, got_a, got_b, halo)
        wait_all(extra)

    def row(c):
        terms = outer_terms(coupled[...], coupling, halo, edge, c, row_blocks)
        for i in range(2):
            r = 2 * c + i
            move = change[r] - factor[r] * terms[:, i * size : (i + 1) * size]
            new_p[r] = (p2[r] + move).T
            rate_error = (1.0 / error_scale) * move
            errors[...] += area[r : r + 1] * (rate_error * rate_error)

    def done(c):
        part(new_p, new_p_out, new_p_sems, c, 2).start()

    run_rows(order, order.index(0), loads, outer, row, done, start)
    total = jnp.sum(errors[...].T, axis=0, keepdims=True)
    areas = jnp.sum(jnp.sum(area[...], axis=0, keepdims=True), axis=1, keepdims=True)
    both = jnp.concatenate([total, jnp.broadcast_to(areas, total.shape)], axis=0)
    for j in range(parts_out.shape[0]):
        parts_out[j] = both
    wait_all([part(new_p, new_p_out, new_p_sems, c, 2) for c in order])


def exchange(side_a, side_b, slots):
    count = lax.axis_size(AXIS)
    got_a = lax.ppermute(side_a, AXIS, [(i, i ^ 1) for i in range(count)])
    pairs = [(i, (i - 1) % count if i % 2 == 0 else (i + 1) % count) for i in range(count)]
    got_b = lax.ppermute(side_b, AXIS, pairs)
    got = lax.all_to_all(slots, AXIS, 0, 0)
    return got_a, got_b, got


def on_device(
    log_rate,
    log_state,
    near_blocks,
    near_columns,
    far_basis,
    far_coupling,
    self_stiffness,
    plate_rate,
    direct_effect,
    evolution_effect,
    triangle_area,
):
    rows, cols = log_rate.shape
    row_blocks, near_count, size, _ = near_blocks.shape
    levels, rank, _ = far_basis.shape
    devices = lax.axis_size(AXIS)
    p = log_rate.reshape(row_blocks, size, cols)
    s = log_state.reshape(row_blocks, size, cols)
    basis = far_basis.reshape(levels * rank, rows)
    coupling = far_coupling.reshape(levels * rank, rows)
    stiff, plate, direct, evolve, area = (
        v.reshape(row_blocks, size)
        for v in (self_stiffness, plate_rate, direct_effect, evolution_effect, triangle_area)
    )
    pairs = row_blocks // 2
    flat_near = near_blocks.reshape(row_blocks * near_count, size, size)
    state = ((row_blocks, size, cols), F32)
    x_kind = ((row_blocks, size, cols), BF16)
    slots_kind = ((devices, rank, cols), BF16)
    side_kind = ((REACH, size, cols), BF16)
    edge_kind = ((len(edge_tiles(row_blocks)), 2 * size, 2 * size), BF16)
    basis_kind = ((levels * rank, rows), BF16)
    near_kind = ((row_blocks * near_count, size, size), BF16)
    halo_kind = ((2 * REACH, size, cols), BF16)
    vector_kind = ((row_blocks, size), F32)
    errors_kind = ((cols, size), F32)
    products_kind = ((pairs, cols, 2 * size), F32)
    coupled_kind = ((cols, levels * rank), BF16)
    turned_kind = ((2, cols, size), F32)
    where_kind = pltpu.SMEM((row_blocks, 2 * REACH + 1), jnp.int32)
    loads = 4 if row_blocks % 4 == 0 else row_blocks
    small = pltpu.CompilerParams(vmem_limit_bytes=32 * 1024 * 1024)
    near_flops = 2 * rows * near_count * size * cols

    def vmem(*kinds):
        return [pltpu.VMEM(shape, dtype) for shape, dtype in kinds]

    x, slots, side_a, side_b = pl.pallas_call(
        open_kernel,
        out_shape=in_hbm(x_kind, slots_kind, side_kind, side_kind),
        in_specs=[PLAIN] * 2,
        out_specs=(PLAIN,) * 4,
        scratch_shapes=vmem(state, basis_kind, x_kind, slots_kind)
        + [SEMS((loads,)), SEMS(()), SEMS(()), SEMS((3,))],
        compiler_params=small,
        cost_estimate=cost(BUSY, 0),
        name="open",
    )(*hbm(p, basis))

    got_a, got_b, got = exchange(side_a, side_b, slots)
    known, factor, edge = pl.pallas_call(
        first_local_kernel,
        out_shape=in_hbm(state, state, edge_kind),
        in_specs=[SCALARS, PLAIN, PLAIN] + [WHOLE] * 6,
        out_specs=(PLAIN,) * 3,
        scratch_shapes=vmem(x_kind, near_kind, state, state, edge_kind, products_kind, turned_kind, turned_kind)
        + [where_kind, SEMS(()), SEMS((pairs,)), SEMS((pairs,)), SEMS((pairs,)), SEMS((1,))],
        compiler_params=small,
        cost_estimate=cost(near_flops, near_blocks.size * 2),
        name="local_one",
    )(near_columns, *hbm(x, flat_near), *resident(p, s), stiff, plate, direct, evolve)

    p2, x, slots, side_a, side_b = pl.pallas_call(
        middle_kernel,
        out_shape=in_hbm(state, x_kind, slots_kind, side_kind, side_kind),
        in_specs=[WHOLE] * 3 + [PLAIN] + [WHOLE] + [PLAIN] * 3,
        out_specs=(PLAIN,) * 5,
        scratch_shapes=vmem(halo_kind, edge_kind, basis_kind, state, state, state, x_kind, slots_kind, coupled_kind)
        + [SEMS((2,)), SEMS((pairs,)), SEMS((pairs,)), SEMS((pairs,)), SEMS(()), SEMS((3,))],
        compiler_params=small,
        cost_estimate=cost(BUSY, 0),
        name="middle",
    )(got_a, got_b, got, *hbm(edge), *resident(coupling), *hbm(basis, known, factor))

    got_a, got_b, got = exchange(side_a, side_b, slots)
    change, factor, new_s, errors = pl.pallas_call(
        second_local_kernel,
        out_shape=in_hbm(state, state, state, errors_kind),
        in_specs=[SCALARS, PLAIN, PLAIN] + [WHOLE] * 2 + [PLAIN] + [WHOLE] * 5,
        out_specs=(PLAIN,) * 4,
        scratch_shapes=vmem(
            x_kind, near_kind, state, state, state, state, errors_kind, products_kind, turned_kind, turned_kind,
            turned_kind,
        )
        + [where_kind, SEMS(())]
        + [SEMS((pairs,))] * 5
        + [SEMS((1,))],
        compiler_params=small,
        cost_estimate=cost(near_flops, near_blocks.size * 2),
        name="local_two",
    )(near_columns, *hbm(x, flat_near), *resident(p, s), *hbm(p2), stiff, plate, direct, evolve, area)

    new_p, parts = pl.pallas_call(
        close_kernel,
        out_shape=in_hbm(state) + like(((devices, 2, cols), F32)),
        in_specs=[WHOLE] * 3 + [PLAIN] + [WHOLE] + [PLAIN] * 5,
        out_specs=(PLAIN, WHOLE),
        scratch_shapes=vmem(
            halo_kind, edge_kind, state, state, state, state, coupled_kind, vector_kind, errors_kind
        )
        + [SEMS((3,))]
        + [SEMS((pairs,))] * 4,
        compiler_params=small,
        name="close",
    )(got_a, got_b, got, *hbm(edge), *resident(coupling), *hbm(p2, change, factor, area, errors))

    totals = lax.all_to_all(parts, AXIS, 0, 0).sum(axis=0)
    error_norm = jnp.sqrt(totals[0] / totals[1] + 1e-06)
    return new_p.reshape(rows, cols), new_s.reshape(rows, cols), error_norm


def solution(mesh):
    split = P(("member", "patch"))
    in_specs = (
        P(("member", "patch"), None),
        P(("member", "patch"), None),
        P(("member", "patch"), None, None, None),
        P(("member", "patch"), None),
        P("member", None, "patch"),
        P("member", None, "patch"),
        split,
        split,
        split,
        split,
        split,
    )
    out_specs = (P(("member", "patch"), None), P(("member", "patch"), None), P("member"))
    return jax.shard_map(
        on_device, mesh=mesh, in_specs=in_specs, out_specs=out_specs, check_vma=False
    )
```

```python
import jax
import jax.numpy as jnp
from jax import lax
from jax.experimental import pallas as pl
from jax.experimental.pallas import tpu as pltpu
from jax.sharding import PartitionSpec as P


REACH = 6
PAD = REACH + REACH % 2
STRIP = 32
AHEAD = 3
BUSY = 10**10

step_size = 0.1
damping = 0.5
error_scale = 0.01
half_step = 0.5 * step_size

AXIS = "patch"
F32 = jnp.float32
BF16 = jnp.bfloat16
PLAIN = pl.BlockSpec(memory_space=pltpu.HBM)
WHOLE = pl.BlockSpec(memory_space=pltpu.VMEM)
SCALARS = pl.BlockSpec(memory_space=pltpu.SMEM)
SEMS = pltpu.SemaphoreType.DMA


def cost(flops, moved, exps=0):
    return pl.CostEstimate(flops=flops, bytes_accessed=moved, transcendentals=exps)


def in_hbm(*shapes):
    return tuple(pltpu.HBM(shape, dtype) for shape, dtype in shapes)


def hbm(*arrays):
    return tuple(pltpu.with_memory_space_constraint(v, pltpu.HBM) for v in arrays)


def resident(*arrays):
    return tuple(pltpu.with_memory_space_constraint(v, pltpu.VMEM) for v in arrays)


def like(*shapes):
    return tuple(jax.ShapeDtypeStruct(shape, dtype) for shape, dtype in shapes)


def part(src, dst, sems, c, group):
    at = pl.ds(c * group, group)
    return pltpu.make_async_copy(src.at[at], dst.at[at], sems.at[c])


def pair_columns(row_blocks, pair):
    reached = range((2 * pair - REACH) // 2, (2 * pair + 1 + REACH) // 2 + 1)
    count = row_blocks // 2
    return (
        [c for c in reached if c < 0],
        [c for c in reached if 0 <= c < count],
        [c for c in reached if c >= count],
    )


def edge_tiles(row_blocks):
    tiles = []
    for pair in range(row_blocks // 2):
        left, _, right = pair_columns(row_blocks, pair)
        tiles += [(pair, c) for c in left + right]
    return tiles


NT = (((1,), (1,)), ((), ()))


def side_by_side(blocks):
    return jnp.concatenate(blocks, axis=1)


def project(basis, x):
    rates = side_by_side([x[r] for r in range(x.shape[0])])
    return lax.dot_general(rates, basis[...], NT, preferred_element_type=F32).T


def fill_slots(me, projected, slots):
    devices, rank, _ = slots.shape
    for m in range(devices):
        level = max(m.bit_length() - 1, 0)
        slots[me ^ m] = projected[level * rank : (level + 1) * rank].astype(slots.dtype)


def send_copies(me, x, slots, slots_out, a_out, b_out, sems):
    row_blocks = x.shape[0]
    odd = lax.rem(me, 2)
    start_a = (1 - odd) * (row_blocks - REACH)
    start_b = odd * (row_blocks - REACH)
    return [
        pltpu.make_async_copy(slots, slots_out, sems.at[0]),
        pltpu.make_async_copy(x.at[pl.ds(start_a, REACH)], a_out, sems.at[1]),
        pltpu.make_async_copy(x.at[pl.ds(start_b, REACH)], b_out, sems.at[2]),
    ]


def open_kernel(
    p_in, basis_in, x_out, slots_out, a_out, b_out,
    p, basis, x, slots, p_sems, x_sem, basis_sem, send_sems,
):
    row_blocks, _, _ = p.shape
    chunks = p_sems.shape[0]
    group = row_blocks // chunks
    me = lax.axis_index(AXIS)
    load_basis = pltpu.make_async_copy(basis_in, basis, basis_sem)
    for c in range(chunks):
        part(p_in, p, p_sems, c, group).start()
    load_basis.start()
    for c in range(chunks):
        part(p_in, p, p_sems, c, group).wait()
        for r in range(c * group, (c + 1) * group):
            x[r] = jnp.exp(p[r]).astype(BF16).T
    send = send_copies(me, x, slots, slots_out, a_out, b_out, send_sems)
    send.append(pltpu.make_async_copy(x, x_out, x_sem))
    for copy in send[1:]:
        copy.start()
    load_basis.wait()
    fill_slots(me, project(basis, x), slots)
    send[0].start()
    for copy in send:
        copy.wait()


def find_blocks(columns, where):
    row_blocks, near_count = columns.shape
    total = row_blocks * lax.axis_size(AXIS)
    first = row_blocks * lax.axis_index(AXIS)

    def row(r, carry):
        for o in range(2 * REACH + 1):
            where[r, o] = -1
        for k in range(near_count):
            offset = columns[r, k] - first - r
            offset = jnp.where(offset > REACH, offset - total, offset)
            offset = jnp.where(offset < -REACH, offset + total, offset)
            where[r, offset + REACH] = r * near_count + k
        return carry

    lax.fori_loop(0, row_blocks, row, 0)


def near_block(near, where, r, offset):
    if abs(offset) > REACH:
        return jnp.zeros(near.shape[1:], near.dtype)
    at = where[r, offset + REACH]
    block = near[jnp.maximum(at, 0)]
    if offset == 0 or abs(offset) == REACH:
        return block
    return jnp.where(at >= 0, block, jnp.zeros_like(block))


def near_product(near, x, where, pair):
    reached = range(2 * PAD + 2)
    tiles = [side_by_side([near_block(near, where, 2 * pair + i, j - PAD - i) for j in reached]) for i in range(2)]
    rates = side_by_side([x[2 * pair + j] for j in reached])
    return lax.dot_general(rates, jnp.concatenate(tiles, axis=0), NT, preferred_element_type=F32)


def strips(size):
    step = STRIP if size % STRIP == 0 else size
    return [slice(i, i + step) for i in range(0, size, step)]


def known_rates(velocity, state, near_term, rows):
    stiff, plate, direct, evolve = rows
    factor = 1.0 / (direct + damping * velocity)
    return (stiff * (plate - velocity) - near_term - evolve * state) * factor, factor


def in_pairs(pairs, loads, product, finish, stores):
    def body(pair, carry):
        pl.when(pair + AHEAD < pairs)(lambda: start_all(loads(pair + AHEAD)))
        wait_all(loads(pair))
        product(pair)
        finish(pair)
        start_all(stores(pair))
        return carry

    lax.fori_loop(0, pairs, body, 0)


def clear_pads(x, row_blocks):
    zeros = jnp.zeros((PAD,) + x.shape[1:], x.dtype)
    x[:PAD] = zeros
    x[PAD + row_blocks :] = zeros


def start_all(copies):
    for copy in copies:
        copy.start()


def wait_all(copies):
    for copy in copies:
        copy.wait()


def first_local_kernel(
    columns, x_in, near_in, p, s, stiff, plate, direct, evolve,
    known_out, factor_out, edge_out,
    x, near, known, factor, edge, products, turned_p, turned_s,
    where, x_sem, near_sems, known_sems, factor_sems, rest_sems,
):
    row_blocks, size, _ = p.shape
    pairs = row_blocks // 2
    vectors = (stiff, plate, direct, evolve)
    span = near.shape[0] // pairs
    load_x = pltpu.make_async_copy(x_in, x.at[pl.ds(PAD, row_blocks)], x_sem)

    def loads(c):
        return [part(near_in, near, near_sems, c, span)]

    def stores(c):
        return [part(known, known_out, known_sems, c, 2), part(factor, factor_out, factor_sems, c, 2)]

    load_x.start()
    for c in range(AHEAD):
        start_all(loads(c))
    clear_pads(x, row_blocks)
    find_blocks(columns, where)
    load_x.wait()

    def product(pair):
        products[...] = near_product(near, x, where, pair)

    def finish(pair):
        for i in range(2):
            r = 2 * pair + i
            rows = [v[pl.ds(r, 1), :] for v in vectors]
            turned_p[i] = p[r].T
            turned_s[i] = s[r].T
            for at in strips(size):
                now = turned_p[i, at]
                velocity = jnp.exp(now)
                state = jnp.exp(-turned_s[i, at]) - velocity
                near_term = products[at, i * size : (i + 1) * size]
                rate, scale = known_rates(velocity, state, near_term, rows)
                known[r, at] = now + step_size * rate
                factor[r, at] = step_size * scale

    in_pairs(
        pairs,
        loads,
        product,
        finish,
        stores,
    )
    for n, (pair, c) in enumerate(edge_tiles(row_blocks)):
        for i in range(2):
            for j in range(2):
                edge[n, i * size : (i + 1) * size, j * size : (j + 1) * size] = near_block(
                    near, where, 2 * pair + i, 2 * c + j - 2 * pair - i
                )
    store_edge = pltpu.make_async_copy(edge, edge_out, rest_sems.at[0])
    store_edge.start()
    for c in range(pairs):
        wait_all(stores(c))
    store_edge.wait()


def second_local_kernel(
    columns, x_in, near_in, p, s, p2_in, stiff, plate, direct, evolve, area,
    change_out, factor_out, new_s_out, errors_out,
    x, near, p2, change, factor, new_s, errors, products,
    turned_p, turned_s, ended_s,
    where, x_sem, near_sems, p2_sems, change_sems, factor_sems, new_s_sems, rest_sems,
):
    row_blocks, size, _ = p.shape
    pairs = row_blocks // 2
    vectors = (stiff, plate, direct, evolve, area)
    span = near.shape[0] // pairs
    load_x = pltpu.make_async_copy(x_in, x.at[pl.ds(PAD, row_blocks)], x_sem)

    def loads(c):
        return [part(near_in, near, near_sems, c, span), part(p2_in, p2, p2_sems, c, 2)]

    def stores(c):
        return [
            part(change, change_out, change_sems, c, 2),
            part(factor, factor_out, factor_sems, c, 2),
            part(new_s, new_s_out, new_s_sems, c, 2),
        ]

    load_x.start()
    for c in range(AHEAD):
        start_all(loads(c))
    clear_pads(x, row_blocks)
    errors[...] = jnp.zeros(errors.shape, F32)
    find_blocks(columns, where)
    load_x.wait()

    def product(pair):
        products[...] = near_product(near, x, where, pair)

    def finish(pair):
        for i in range(2):
            r = 2 * pair + i
            rows = [v[pl.ds(r, 1), :] for v in vectors]
            turned_p[i] = p[r].T
            turned_s[i] = s[r].T
            for at in strips(size):
                before, now, start = turned_p[i, at], p2[r, at], turned_s[i, at]
                state_a = jnp.exp(-start) - jnp.exp(before)
                velocity = jnp.exp(now)
                state_b = jnp.exp(-(start + step_size * state_a)) - velocity
                near_term = products[at, i * size : (i + 1) * size]
                rate, scale = known_rates(velocity, state_b, near_term, rows[:4])
                change[r, at] = half_step * rate - (half_step / step_size) * (now - before)
                factor[r, at] = half_step * scale
                ended_s[i, at] = start + half_step * (state_a + state_b)
                state_error = (half_step / error_scale) * (state_b - state_a)
                weighted = rows[4] * (state_error * state_error)
                errors[at] += weighted
            new_s[r] = ended_s[i].T

    in_pairs(
        pairs,
        loads,
        product,
        finish,
        stores,
    )
    store_errors = pltpu.make_async_copy(errors, errors_out, rest_sems.at[0])
    store_errors.start()
    for c in range(pairs):
        wait_all(stores(c))
    store_errors.wait()


def couple(me, got, levels):
    devices = got.shape[0]
    sums = []
    for level in range(levels):
        total = got[me ^ (1 << level)].astype(F32)
        for m in range((1 << level) + 1, min(2 << level, devices)):
            total += got[me ^ m].astype(F32)
        sums.append(total)
    return jnp.concatenate(sums, axis=0).T.astype(BF16)


def pair_order(row_blocks):
    edged = {pair for pair, _ in edge_tiles(row_blocks)}
    pairs = range(row_blocks // 2)
    return [c for c in pairs if c not in edged] + [c for c in pairs if c in edged]


def outer_terms(coupled, coupling, halo, edge, pair, row_blocks):
    size = halo.shape[2]
    terms = jnp.dot(
        coupled, coupling[:, 2 * pair * size : 2 * (pair + 1) * size], preferred_element_type=F32
    )
    rates, tiles = [], []
    for n, (row_pair, c) in enumerate(edge_tiles(row_blocks)):
        if row_pair == pair:
            at = REACH + 2 * c if c < 0 else REACH + 2 * c - row_blocks
            tiles.append(edge[n])
            rates += [halo[at], halo[at + 1]]
    if tiles:
        terms += lax.dot_general(side_by_side(rates), side_by_side(tiles), NT, preferred_element_type=F32)
    return terms


def place_halo(me, got_a, got_b, halo):
    odd = lax.rem(me, 2)
    at_a = (1 - odd) * REACH
    at_b = odd * REACH
    for t in range(REACH):
        halo[at_a + t] = got_a[t]
        halo[at_b + t] = got_b[t]


def run_rows(order, first_edged, loads, outer, row, done, start):
    ahead = 4
    for c in order[:ahead]:
        start_all(loads(c))
        if c == order[0]:
            start_all(outer)
    start()
    for n, c in enumerate(order):
        if n == first_edged:
            wait_all(outer)
        wait_all(loads(c))
        if n + ahead < len(order):
            start_all(loads(order[n + ahead]))
        row(c)
        done(c)


def middle_kernel(
    got_a, got_b, got, edge_in, coupling, basis_in, known_in, factor_in,
    p2_out, x_out, slots_out, a_out, b_out,
    halo, edge, basis, known, factor, p2, x, slots, coupled,
    outer_sems, known_sems, factor_sems, p2_sems, x_sem, send_sems,
):
    row_blocks, size, _ = known.shape
    me = lax.axis_index(AXIS)
    order = pair_order(row_blocks)
    outer = [
        pltpu.make_async_copy(edge_in, edge, outer_sems.at[0]),
        pltpu.make_async_copy(basis_in, basis, outer_sems.at[1]),
    ]

    def loads(c):
        return [part(known_in, known, known_sems, c, 2), part(factor_in, factor, factor_sems, c, 2)]

    def start():
        coupled[...] = couple(me, got, basis.shape[0] // got.shape[1])
        place_halo(me, got_a, got_b, halo)

    def row(c):
        terms = outer_terms(coupled[...], coupling, halo, edge, c, row_blocks)
        for i in range(2):
            r = 2 * c + i
            value = known[r] - factor[r] * terms[:, i * size : (i + 1) * size]
            p2[r] = value
            x[r] = jnp.exp(value).astype(BF16)

    def done(c):
        part(p2, p2_out, p2_sems, c, 2).start()

    run_rows(order, order.index(0), loads, outer, row, done, start)
    send = send_copies(me, x, slots, slots_out, a_out, b_out, send_sems)
    send.append(pltpu.make_async_copy(x, x_out, x_sem))
    start_all(send[1:])
    fill_slots(me, project(basis, x), slots)
    send[0].start()
    wait_all(send + [part(p2, p2_out, p2_sems, c, 2) for c in order])


def close_kernel(
    got_a, got_b, got, edge_in, coupling, p2_in, change_in, factor_in, area_in, errors_in,
    new_p_out, parts_out,
    halo, edge, p2, change, factor, new_p, coupled, area, errors,
    outer_sems, p2_sems, change_sems, factor_sems, new_p_sems,
):
    row_blocks, size, _ = change.shape
    me = lax.axis_index(AXIS)
    order = pair_order(row_blocks)
    outer = [pltpu.make_async_copy(edge_in, edge, outer_sems.at[0])]
    extra = [
        pltpu.make_async_copy(area_in, area, outer_sems.at[1]),
        pltpu.make_async_copy(errors_in, errors, outer_sems.at[2]),
    ]

    def loads(c):
        return [
            part(change_in, change, change_sems, c, 2),
            part(factor_in, factor, factor_sems, c, 2),
            part(p2_in, p2, p2_sems, c, 2),
        ]

    def start():
        start_all(extra)
        coupled[...] = couple(me, got, coupling.shape[0] // got.shape[1])
        place_halo(me, got_a, got_b, halo)
        wait_all(extra)

    def row(c):
        terms = outer_terms(coupled[...], coupling, halo, edge, c, row_blocks)
        for i in range(2):
            r = 2 * c + i
            move = change[r] - factor[r] * terms[:, i * size : (i + 1) * size]
            new_p[r] = (p2[r] + move).T
            rate_error = (1.0 / error_scale) * move
            errors[...] += area[r : r + 1] * (rate_error * rate_error)

    def done(c):
        part(new_p, new_p_out, new_p_sems, c, 2).start()

    run_rows(order, order.index(0), loads, outer, row, done, start)
    total = jnp.sum(errors[...].T, axis=0, keepdims=True)
    areas = jnp.sum(jnp.sum(area[...], axis=0, keepdims=True), axis=1, keepdims=True)
    both = jnp.concatenate([total, jnp.broadcast_to(areas, total.shape)], axis=0)
    for j in range(parts_out.shape[0]):
        parts_out[j] = both
    wait_all([part(new_p, new_p_out, new_p_sems, c, 2) for c in order])


def exchange(side_a, side_b, slots):
    count = lax.axis_size(AXIS)
    got_a = lax.ppermute(side_a, AXIS, [(i, i ^ 1) for i in range(count)])
    pairs = [(i, (i - 1) % count if i % 2 == 0 else (i + 1) % count) for i in range(count)]
    got_b = lax.ppermute(side_b, AXIS, pairs)
    got = lax.all_to_all(slots, AXIS, 0, 0)
    return got_a, got_b, got


def on_device(
    log_rate,
    log_state,
    near_blocks,
    near_columns,
    far_basis,
    far_coupling,
    self_stiffness,
    plate_rate,
    direct_effect,
    evolution_effect,
    triangle_area,
):
    rows, cols = log_rate.shape
    row_blocks, near_count, size, _ = near_blocks.shape
    levels, rank, _ = far_basis.shape
    devices = lax.axis_size(AXIS)
    p = log_rate.reshape(row_blocks, size, cols)
    s = log_state.reshape(row_blocks, size, cols)
    basis = far_basis.reshape(levels * rank, rows)
    coupling = far_coupling.reshape(levels * rank, rows)
    stiff, plate, direct, evolve, area = (
        v.reshape(row_blocks, size)
        for v in (self_stiffness, plate_rate, direct_effect, evolution_effect, triangle_area)
    )
    pairs = row_blocks // 2
    flat_near = near_blocks.reshape(row_blocks * near_count, size, size)
    state = ((row_blocks, size, cols), F32)
    x_kind = ((row_blocks, size, cols), BF16)
    slots_kind = ((devices, rank, cols), BF16)
    side_kind = ((REACH, size, cols), BF16)
    edge_kind = ((len(edge_tiles(row_blocks)), 2 * size, 2 * size), BF16)
    basis_kind = ((levels * rank, rows), BF16)
    near_kind = ((row_blocks * near_count, size, size), BF16)
    halo_kind = ((2 * REACH, size, cols), BF16)
    vector_kind = ((row_blocks, size), F32)
    errors_kind = ((cols, size), F32)
    products_kind = ((cols, 2 * size), F32)
    padded_kind = ((row_blocks + 2 * PAD, size, cols), BF16)
    coupled_kind = ((cols, levels * rank), BF16)
    turned_kind = ((2, cols, size), F32)
    where_kind = pltpu.SMEM((row_blocks, 2 * REACH + 1), jnp.int32)
    loads = 4 if row_blocks % 4 == 0 else row_blocks
    small = pltpu.CompilerParams(vmem_limit_bytes=32 * 1024 * 1024)
    near_flops = 2 * rows * near_count * size * cols

    def vmem(*kinds):
        return [pltpu.VMEM(shape, dtype) for shape, dtype in kinds]

    x, slots, side_a, side_b = pl.pallas_call(
        open_kernel,
        out_shape=in_hbm(x_kind, slots_kind, side_kind, side_kind),
        in_specs=[PLAIN] * 2,
        out_specs=(PLAIN,) * 4,
        scratch_shapes=vmem(state, basis_kind, x_kind, slots_kind)
        + [SEMS((loads,)), SEMS(()), SEMS(()), SEMS((3,))],
        compiler_params=small,
        cost_estimate=cost(BUSY, 0),
        name="open",
    )(*hbm(p, basis))

    got_a, got_b, got = exchange(side_a, side_b, slots)
    known, factor, edge = pl.pallas_call(
        first_local_kernel,
        out_shape=in_hbm(state, state, edge_kind),
        in_specs=[SCALARS, PLAIN, PLAIN] + [WHOLE] * 6,
        out_specs=(PLAIN,) * 3,
        scratch_shapes=vmem(padded_kind, near_kind, state, state, edge_kind, products_kind, turned_kind, turned_kind)
        + [where_kind, SEMS(()), SEMS((pairs,)), SEMS((pairs,)), SEMS((pairs,)), SEMS((1,))],
        compiler_params=small,
        cost_estimate=cost(near_flops, near_blocks.size * 2),
        name="local_one",
    )(near_columns, *hbm(x, flat_near), *resident(p, s), stiff, plate, direct, evolve)

    p2, x, slots, side_a, side_b = pl.pallas_call(
        middle_kernel,
        out_shape=in_hbm(state, x_kind, slots_kind, side_kind, side_kind),
        in_specs=[WHOLE] * 3 + [PLAIN] + [WHOLE] + [PLAIN] * 3,
        out_specs=(PLAIN,) * 5,
        scratch_shapes=vmem(halo_kind, edge_kind, basis_kind, state, state, state, x_kind, slots_kind, coupled_kind)
        + [SEMS((2,)), SEMS((pairs,)), SEMS((pairs,)), SEMS((pairs,)), SEMS(()), SEMS((3,))],
        compiler_params=small,
        cost_estimate=cost(BUSY, 0),
        name="middle",
    )(got_a, got_b, got, *hbm(edge), *resident(coupling), *hbm(basis, known, factor))

    got_a, got_b, got = exchange(side_a, side_b, slots)
    change, factor, new_s, errors = pl.pallas_call(
        second_local_kernel,
        out_shape=in_hbm(state, state, state, errors_kind),
        in_specs=[SCALARS, PLAIN, PLAIN] + [WHOLE] * 2 + [PLAIN] + [WHOLE] * 5,
        out_specs=(PLAIN,) * 4,
        scratch_shapes=vmem(
            padded_kind, near_kind, state, state, state, state, errors_kind, products_kind, turned_kind, turned_kind,
            turned_kind,
        )
        + [where_kind, SEMS(())]
        + [SEMS((pairs,))] * 5
        + [SEMS((1,))],
        compiler_params=small,
        cost_estimate=cost(near_flops, near_blocks.size * 2),
        name="local_two",
    )(near_columns, *hbm(x, flat_near), *resident(p, s), *hbm(p2), stiff, plate, direct, evolve, area)

    new_p, parts = pl.pallas_call(
        close_kernel,
        out_shape=in_hbm(state) + like(((devices, 2, cols), F32)),
        in_specs=[WHOLE] * 3 + [PLAIN] + [WHOLE] + [PLAIN] * 5,
        out_specs=(PLAIN, WHOLE),
        scratch_shapes=vmem(
            halo_kind, edge_kind, state, state, state, state, coupled_kind, vector_kind, errors_kind
        )
        + [SEMS((3,))]
        + [SEMS((pairs,))] * 4,
        compiler_params=small,
        name="close",
    )(got_a, got_b, got, *hbm(edge), *resident(coupling), *hbm(p2, change, factor, area, errors))

    totals = lax.all_to_all(parts, AXIS, 0, 0).sum(axis=0)
    error_norm = jnp.sqrt(totals[0] / totals[1] + 1e-06)
    return new_p.reshape(rows, cols), new_s.reshape(rows, cols), error_norm


def solution(mesh):
    split = P(("member", "patch"))
    in_specs = (
        P(("member", "patch"), None),
        P(("member", "patch"), None),
        P(("member", "patch"), None, None, None),
        P(("member", "patch"), None),
        P("member", None, "patch"),
        P("member", None, "patch"),
        split,
        split,
        split,
        split,
        split,
    )
    out_specs = (P(("member", "patch"), None), P(("member", "patch"), None), P("member"))
    return jax.shard_map(
        on_device, mesh=mesh, in_specs=in_specs, out_specs=out_specs, check_vma=False
    )
```

```python
import jax
import jax.numpy as jnp
from jax import lax
from jax.experimental import pallas as pl
from jax.experimental.pallas import tpu as pltpu
from jax.sharding import PartitionSpec as P


REACH = 6
PAD = REACH + REACH % 2
STRIP = 32
AHEAD = 3
BUSY = 10**10

step_size = 0.1
damping = 0.5
error_scale = 0.01
half_step = 0.5 * step_size

AXIS = "patch"
F32 = jnp.float32
BF16 = jnp.bfloat16
PLAIN = pl.BlockSpec(memory_space=pltpu.HBM)
WHOLE = pl.BlockSpec(memory_space=pltpu.VMEM)
SCALARS = pl.BlockSpec(memory_space=pltpu.SMEM)
SEMS = pltpu.SemaphoreType.DMA


def cost(flops, moved, exps=0):
    return pl.CostEstimate(flops=flops, bytes_accessed=moved, transcendentals=exps)


def in_hbm(*shapes):
    return tuple(pltpu.HBM(shape, dtype) for shape, dtype in shapes)


def hbm(*arrays):
    return tuple(pltpu.with_memory_space_constraint(v, pltpu.HBM) for v in arrays)


def resident(*arrays):
    return tuple(pltpu.with_memory_space_constraint(v, pltpu.VMEM) for v in arrays)


def like(*shapes):
    return tuple(jax.ShapeDtypeStruct(shape, dtype) for shape, dtype in shapes)


def part(src, dst, sems, c, group):
    at = pl.ds(c * group, group)
    return pltpu.make_async_copy(src.at[at], dst.at[at], sems.at[c])


def pair_columns(row_blocks, pair):
    reached = range((2 * pair - REACH) // 2, (2 * pair + 1 + REACH) // 2 + 1)
    count = row_blocks // 2
    return (
        [c for c in reached if c < 0],
        [c for c in reached if 0 <= c < count],
        [c for c in reached if c >= count],
    )


def edge_tiles(row_blocks):
    tiles = []
    for pair in range(row_blocks // 2):
        left, _, right = pair_columns(row_blocks, pair)
        tiles += [(pair, c) for c in left + right]
    return tiles


NT = (((1,), (1,)), ((), ()))


def side_by_side(blocks):
    return jnp.concatenate(blocks, axis=1)


def project(basis, x):
    rates = side_by_side([x[r] for r in range(x.shape[0])])
    return lax.dot_general(rates, basis[...], NT, preferred_element_type=F32).T


def fill_slots(me, projected, slots):
    devices, rank, _ = slots.shape
    for m in range(devices):
        level = max(m.bit_length() - 1, 0)
        slots[me ^ m] = projected[level * rank : (level + 1) * rank].astype(slots.dtype)


def send_copies(me, x, slots, slots_out, a_out, b_out, sems):
    row_blocks = x.shape[0]
    odd = lax.rem(me, 2)
    start_a = (1 - odd) * (row_blocks - REACH)
    start_b = odd * (row_blocks - REACH)
    return [
        pltpu.make_async_copy(slots, slots_out, sems.at[0]),
        pltpu.make_async_copy(x.at[pl.ds(start_a, REACH)], a_out, sems.at[1]),
        pltpu.make_async_copy(x.at[pl.ds(start_b, REACH)], b_out, sems.at[2]),
    ]


def open_kernel(
    p_in, basis_in, x_out, slots_out, a_out, b_out,
    p, basis, x, slots, p_sems, x_sem, basis_sem, send_sems,
):
    row_blocks, _, _ = p.shape
    chunks = p_sems.shape[0]
    group = row_blocks // chunks
    me = lax.axis_index(AXIS)
    load_basis = pltpu.make_async_copy(basis_in, basis, basis_sem)
    for c in range(chunks):
        part(p_in, p, p_sems, c, group).start()
    load_basis.start()
    for c in range(chunks):
        part(p_in, p, p_sems, c, group).wait()
        for r in range(c * group, (c + 1) * group):
            x[r] = jnp.exp(p[r]).astype(BF16).T
    send = send_copies(me, x, slots, slots_out, a_out, b_out, send_sems)
    send.append(pltpu.make_async_copy(x, x_out, x_sem))
    for copy in send[1:]:
        copy.start()
    load_basis.wait()
    fill_slots(me, project(basis, x), slots)
    send[0].start()
    for copy in send:
        copy.wait()


def find_blocks(columns, where):
    row_blocks, near_count = columns.shape
    total = row_blocks * lax.axis_size(AXIS)
    first = row_blocks * lax.axis_index(AXIS)

    def row(r, carry):
        for o in range(2 * REACH + 1):
            where[r, o] = -1
        for k in range(near_count):
            offset = columns[r, k] - first - r
            offset = jnp.where(offset > REACH, offset - total, offset)
            offset = jnp.where(offset < -REACH, offset + total, offset)
            where[r, offset + REACH] = r * near_count + k
        return carry

    lax.fori_loop(0, row_blocks, row, 0)


def near_block(near, where, r, offset):
    if abs(offset) > REACH:
        return jnp.zeros(near.shape[1:], near.dtype)
    at = where[r, offset + REACH]
    block = near[jnp.maximum(at, 0)]
    if offset == 0 or abs(offset) == REACH:
        return block
    return jnp.where(at >= 0, block, jnp.zeros_like(block))


def near_product(near, x, where, pair):
    reached = range(2 * PAD + 2)
    tiles = [side_by_side([near_block(near, where, 2 * pair + i, j - PAD - i) for j in reached]) for i in range(2)]
    rates = side_by_side([x[2 * pair + j] for j in reached])
    return lax.dot_general(rates, jnp.concatenate(tiles, axis=0), NT, preferred_element_type=F32)


def strips(size):
    step = STRIP if size % STRIP == 0 else size
    return [slice(i, i + step) for i in range(0, size, step)]


def known_rates(velocity, state, near_term, rows):
    stiff, plate, direct, evolve = rows
    factor = 1.0 / (direct + damping * velocity)
    return (stiff * (plate - velocity) - near_term - evolve * state) * factor, factor


def in_pairs(pairs, loads, product, finish, stores):
    def body(pair, carry):
        pl.when(pair + AHEAD < pairs)(lambda: start_all(loads(pair + AHEAD)))
        wait_all(loads(pair))
        product(pair)
        finish(pair)
        start_all(stores(pair))
        return carry

    lax.fori_loop(0, pairs, body, 0)


def clear_pads(x, row_blocks):
    zeros = jnp.zeros((PAD,) + x.shape[1:], x.dtype)
    x[:PAD] = zeros
    x[PAD + row_blocks :] = zeros


def start_all(copies):
    for copy in copies:
        copy.start()


def wait_all(copies):
    for copy in copies:
        copy.wait()


def first_local_kernel(
    columns, x_in, near_in, p, s, stiff, plate, direct, evolve,
    known_out, factor_out, edge_out,
    x, near, known, factor, edge, products, turned_p, turned_s,
    where, x_sem, near_sems, known_sems, factor_sems, rest_sems,
):
    row_blocks, size, _ = p.shape
    pairs = row_blocks // 2
    vectors = (stiff, plate, direct, evolve)
    span = near.shape[0] // pairs
    load_x = pltpu.make_async_copy(x_in, x.at[pl.ds(PAD, row_blocks)], x_sem)

    def loads(c):
        return [part(near_in, near, near_sems, c, span)]

    def stores(c):
        return [part(known, known_out, known_sems, c, 2), part(factor, factor_out, factor_sems, c, 2)]

    load_x.start()
    for c in range(AHEAD):
        start_all(loads(c))
    clear_pads(x, row_blocks)
    find_blocks(columns, where)
    load_x.wait()

    def product(pair):
        products[...] = near_product(near, x, where, pair)

    def finish(pair):
        for i in range(2):
            r = 2 * pair + i
            rows = [v[pl.ds(r, 1), :] for v in vectors]
            turned_p[i] = p[r].T
            turned_s[i] = s[r].T
            for at in strips(size):
                now = turned_p[i, at]
                velocity = jnp.exp(now)
                state = jnp.exp(-turned_s[i, at]) - velocity
                near_term = products[at, i * size : (i + 1) * size]
                rate, scale = known_rates(velocity, state, near_term, rows)
                known[r, at] = now + step_size * rate
                factor[r, at] = step_size * scale

    in_pairs(
        pairs,
        loads,
        product,
        finish,
        stores,
    )
    tiles = edge_tiles(row_blocks)
    edge_stores = [part(edge, edge_out, rest_sems, n, 1) for n in range(len(tiles))]
    for n, (pair, c) in enumerate(tiles):
        for i in range(2):
            for j in range(2):
                edge[n, i * size : (i + 1) * size, j * size : (j + 1) * size] = near_block(
                    near, where, 2 * pair + i, 2 * c + j - 2 * pair - i
                )
        edge_stores[n].start()
    for c in range(pairs):
        wait_all(stores(c))
    wait_all(edge_stores)


def second_local_kernel(
    columns, x_in, near_in, p, s, p2_in, stiff, plate, direct, evolve, area,
    change_out, factor_out, new_s_out, errors_out,
    x, near, p2, change, factor, new_s, errors, products,
    turned_p, turned_s, ended_s,
    where, x_sem, near_sems, p2_sems, change_sems, factor_sems, new_s_sems, rest_sems,
):
    row_blocks, size, _ = p.shape
    pairs = row_blocks // 2
    vectors = (stiff, plate, direct, evolve, area)
    span = near.shape[0] // pairs
    load_x = pltpu.make_async_copy(x_in, x.at[pl.ds(PAD, row_blocks)], x_sem)

    def loads(c):
        return [part(near_in, near, near_sems, c, span), part(p2_in, p2, p2_sems, c, 2)]

    def stores(c):
        return [
            part(change, change_out, change_sems, c, 2),
            part(factor, factor_out, factor_sems, c, 2),
            part(new_s, new_s_out, new_s_sems, c, 2),
        ]

    load_x.start()
    for c in range(AHEAD):
        start_all(loads(c))
    clear_pads(x, row_blocks)
    errors[...] = jnp.zeros(errors.shape, F32)
    find_blocks(columns, where)
    load_x.wait()

    def product(pair):
        products[...] = near_product(near, x, where, pair)

    def finish(pair):
        for i in range(2):
            r = 2 * pair + i
            rows = [v[pl.ds(r, 1), :] for v in vectors]
            turned_p[i] = p[r].T
            turned_s[i] = s[r].T
            for at in strips(size):
                before, now, start = turned_p[i, at], p2[r, at], turned_s[i, at]
                state_a = jnp.exp(-start) - jnp.exp(before)
                velocity = jnp.exp(now)
                state_b = jnp.exp(-(start + step_size * state_a)) - velocity
                near_term = products[at, i * size : (i + 1) * size]
                rate, scale = known_rates(velocity, state_b, near_term, rows[:4])
                change[r, at] = half_step * rate - (half_step / step_size) * (now - before)
                factor[r, at] = half_step * scale
                ended_s[i, at] = start + half_step * (state_a + state_b)
                state_error = (half_step / error_scale) * (state_b - state_a)
                weighted = rows[4] * (state_error * state_error)
                errors[at] += weighted
            new_s[r] = ended_s[i].T

    in_pairs(
        pairs,
        loads,
        product,
        finish,
        stores,
    )
    store_errors = pltpu.make_async_copy(errors, errors_out, rest_sems.at[0])
    store_errors.start()
    for c in range(pairs):
        wait_all(stores(c))
    store_errors.wait()


def couple(me, got, levels):
    devices = got.shape[0]
    sums = []
    for level in range(levels):
        total = got[me ^ (1 << level)].astype(F32)
        for m in range((1 << level) + 1, min(2 << level, devices)):
            total += got[me ^ m].astype(F32)
        sums.append(total)
    return jnp.concatenate(sums, axis=0).T.astype(BF16)


def pair_order(row_blocks):
    edged = {pair for pair, _ in edge_tiles(row_blocks)}
    pairs = range(row_blocks // 2)
    return [c for c in pairs if c not in edged] + [c for c in pairs if c in edged]


def outer_terms(coupled, coupling, halo, edge, pair, row_blocks):
    size = halo.shape[2]
    terms = jnp.dot(
        coupled, coupling[:, 2 * pair * size : 2 * (pair + 1) * size], preferred_element_type=F32
    )
    rates, tiles = [], []
    for n, (row_pair, c) in enumerate(edge_tiles(row_blocks)):
        if row_pair == pair:
            at = REACH + 2 * c if c < 0 else REACH + 2 * c - row_blocks
            tiles.append(edge[n])
            rates += [halo[at], halo[at + 1]]
    if tiles:
        terms += lax.dot_general(side_by_side(rates), side_by_side(tiles), NT, preferred_element_type=F32)
    return terms


def place_halo(me, got_a, got_b, halo):
    odd = lax.rem(me, 2)
    at_a = (1 - odd) * REACH
    at_b = odd * REACH
    for t in range(REACH):
        halo[at_a + t] = got_a[t]
        halo[at_b + t] = got_b[t]


def run_rows(order, first_edged, loads, outer, row, done, start):
    ahead = 4
    for c in order[:ahead]:
        start_all(loads(c))
        if c == order[max(first_edged - 1, 0)]:
            start_all(outer)
    start()
    for n, c in enumerate(order):
        if n == first_edged:
            wait_all(outer)
        wait_all(loads(c))
        if n + ahead < len(order):
            start_all(loads(order[n + ahead]))
        row(c)
        done(c)


def middle_kernel(
    got_a, got_b, got, edge_in, coupling, basis_in, known_in, factor_in,
    p2_out, x_out, slots_out, a_out, b_out,
    halo, edge, basis, known, factor, p2, x, slots, coupled,
    outer_sems, known_sems, factor_sems, p2_sems, x_sem, send_sems,
):
    row_blocks, size, _ = known.shape
    me = lax.axis_index(AXIS)
    order = pair_order(row_blocks)
    outer = [
        pltpu.make_async_copy(edge_in, edge, outer_sems.at[0]),
        pltpu.make_async_copy(basis_in, basis, outer_sems.at[1]),
    ]

    def loads(c):
        return [part(known_in, known, known_sems, c, 2), part(factor_in, factor, factor_sems, c, 2)]

    def start():
        coupled[...] = couple(me, got, basis.shape[0] // got.shape[1])
        place_halo(me, got_a, got_b, halo)

    def row(c):
        terms = outer_terms(coupled[...], coupling, halo, edge, c, row_blocks)
        for i in range(2):
            r = 2 * c + i
            value = known[r] - factor[r] * terms[:, i * size : (i + 1) * size]
            p2[r] = value
            x[r] = jnp.exp(value).astype(BF16)

    def done(c):
        part(p2, p2_out, p2_sems, c, 2).start()

    run_rows(order, order.index(0), loads, outer, row, done, start)
    send = send_copies(me, x, slots, slots_out, a_out, b_out, send_sems)
    send.append(pltpu.make_async_copy(x, x_out, x_sem))
    start_all(send[1:])
    fill_slots(me, project(basis, x), slots)
    send[0].start()
    wait_all(send + [part(p2, p2_out, p2_sems, c, 2) for c in order])


def close_kernel(
    got_a, got_b, got, edge_in, coupling, p2_in, change_in, factor_in, area_in, errors_in,
    new_p_out, parts_out,
    halo, edge, p2, change, factor, new_p, coupled, area, errors,
    outer_sems, p2_sems, change_sems, factor_sems, new_p_sems,
):
    row_blocks, size, _ = change.shape
    me = lax.axis_index(AXIS)
    order = pair_order(row_blocks)
    outer = [pltpu.make_async_copy(edge_in, edge, outer_sems.at[0])]
    extra = [
        pltpu.make_async_copy(area_in, area, outer_sems.at[1]),
        pltpu.make_async_copy(errors_in, errors, outer_sems.at[2]),
    ]

    def loads(c):
        return [
            part(change_in, change, change_sems, c, 2),
            part(factor_in, factor, factor_sems, c, 2),
            part(p2_in, p2, p2_sems, c, 2),
        ]

    def start():
        start_all(extra)
        coupled[...] = couple(me, got, coupling.shape[0] // got.shape[1])
        place_halo(me, got_a, got_b, halo)
        wait_all(extra)

    def row(c):
        terms = outer_terms(coupled[...], coupling, halo, edge, c, row_blocks)
        for i in range(2):
            r = 2 * c + i
            move = change[r] - factor[r] * terms[:, i * size : (i + 1) * size]
            new_p[r] = (p2[r] + move).T
            rate_error = (1.0 / error_scale) * move
            errors[...] += area[r : r + 1] * (rate_error * rate_error)

    def done(c):
        part(new_p, new_p_out, new_p_sems, c, 2).start()

    run_rows(order, order.index(0), loads, outer, row, done, start)
    total = jnp.sum(errors[...].T, axis=0, keepdims=True)
    areas = jnp.sum(jnp.sum(area[...], axis=0, keepdims=True), axis=1, keepdims=True)
    both = jnp.concatenate([total, jnp.broadcast_to(areas, total.shape)], axis=0)
    for j in range(parts_out.shape[0]):
        parts_out[j] = both
    wait_all([part(new_p, new_p_out, new_p_sems, c, 2) for c in order])


def exchange(side_a, side_b, slots):
    count = lax.axis_size(AXIS)
    got_a = lax.ppermute(side_a, AXIS, [(i, i ^ 1) for i in range(count)])
    pairs = [(i, (i - 1) % count if i % 2 == 0 else (i + 1) % count) for i in range(count)]
    got_b = lax.ppermute(side_b, AXIS, pairs)
    got = lax.all_to_all(slots, AXIS, 0, 0)
    return got_a, got_b, got


def on_device(
    log_rate,
    log_state,
    near_blocks,
    near_columns,
    far_basis,
    far_coupling,
    self_stiffness,
    plate_rate,
    direct_effect,
    evolution_effect,
    triangle_area,
):
    rows, cols = log_rate.shape
    row_blocks, near_count, size, _ = near_blocks.shape
    levels, rank, _ = far_basis.shape
    devices = lax.axis_size(AXIS)
    p = log_rate.reshape(row_blocks, size, cols)
    s = log_state.reshape(row_blocks, size, cols)
    basis = far_basis.reshape(levels * rank, rows)
    coupling = far_coupling.reshape(levels * rank, rows)
    stiff, plate, direct, evolve, area = (
        v.reshape(row_blocks, size)
        for v in (self_stiffness, plate_rate, direct_effect, evolution_effect, triangle_area)
    )
    pairs = row_blocks // 2
    flat_near = near_blocks.reshape(row_blocks * near_count, size, size)
    state = ((row_blocks, size, cols), F32)
    x_kind = ((row_blocks, size, cols), BF16)
    slots_kind = ((devices, rank, cols), BF16)
    side_kind = ((REACH, size, cols), BF16)
    edge_kind = ((len(edge_tiles(row_blocks)), 2 * size, 2 * size), BF16)
    basis_kind = ((levels * rank, rows), BF16)
    near_kind = ((row_blocks * near_count, size, size), BF16)
    halo_kind = ((2 * REACH, size, cols), BF16)
    vector_kind = ((row_blocks, size), F32)
    errors_kind = ((cols, size), F32)
    products_kind = ((cols, 2 * size), F32)
    padded_kind = ((row_blocks + 2 * PAD, size, cols), BF16)
    coupled_kind = ((cols, levels * rank), BF16)
    turned_kind = ((2, cols, size), F32)
    where_kind = pltpu.SMEM((row_blocks, 2 * REACH + 1), jnp.int32)
    loads = 4 if row_blocks % 4 == 0 else row_blocks
    small = pltpu.CompilerParams(vmem_limit_bytes=32 * 1024 * 1024)
    near_flops = 2 * rows * near_count * size * cols

    def vmem(*kinds):
        return [pltpu.VMEM(shape, dtype) for shape, dtype in kinds]

    x, slots, side_a, side_b = pl.pallas_call(
        open_kernel,
        out_shape=in_hbm(x_kind, slots_kind, side_kind, side_kind),
        in_specs=[PLAIN] * 2,
        out_specs=(PLAIN,) * 4,
        scratch_shapes=vmem(state, basis_kind, x_kind, slots_kind)
        + [SEMS((loads,)), SEMS(()), SEMS(()), SEMS((3,))],
        compiler_params=small,
        cost_estimate=cost(BUSY, 0),
        name="open",
    )(*hbm(p, basis))

    got_a, got_b, got = exchange(side_a, side_b, slots)
    known, factor, edge = pl.pallas_call(
        first_local_kernel,
        out_shape=in_hbm(state, state, edge_kind),
        in_specs=[SCALARS, PLAIN, PLAIN] + [WHOLE] * 6,
        out_specs=(PLAIN,) * 3,
        scratch_shapes=vmem(padded_kind, near_kind, state, state, edge_kind, products_kind, turned_kind, turned_kind)
        + [where_kind, SEMS(()), SEMS((pairs,)), SEMS((pairs,)), SEMS((pairs,)), SEMS(edge_kind[0][:1])],
        compiler_params=small,
        cost_estimate=cost(near_flops, near_blocks.size * 2),
        name="local_one",
    )(near_columns, *hbm(x, flat_near), *resident(p, s), stiff, plate, direct, evolve)

    p2, x, slots, side_a, side_b = pl.pallas_call(
        middle_kernel,
        out_shape=in_hbm(state, x_kind, slots_kind, side_kind, side_kind),
        in_specs=[WHOLE] * 3 + [PLAIN] + [WHOLE] + [PLAIN] * 3,
        out_specs=(PLAIN,) * 5,
        scratch_shapes=vmem(halo_kind, edge_kind, basis_kind, state, state, state, x_kind, slots_kind, coupled_kind)
        + [SEMS((2,)), SEMS((pairs,)), SEMS((pairs,)), SEMS((pairs,)), SEMS(()), SEMS((3,))],
        compiler_params=small,
        cost_estimate=cost(BUSY, 0),
        name="middle",
    )(got_a, got_b, got, *hbm(edge), *resident(coupling), *hbm(basis, known, factor))

    got_a, got_b, got = exchange(side_a, side_b, slots)
    change, factor, new_s, errors = pl.pallas_call(
        second_local_kernel,
        out_shape=in_hbm(state, state, state, errors_kind),
        in_specs=[SCALARS, PLAIN, PLAIN] + [WHOLE] * 2 + [PLAIN] + [WHOLE] * 5,
        out_specs=(PLAIN,) * 4,
        scratch_shapes=vmem(
            padded_kind, near_kind, state, state, state, state, errors_kind, products_kind, turned_kind, turned_kind,
            turned_kind,
        )
        + [where_kind, SEMS(())]
        + [SEMS((pairs,))] * 5
        + [SEMS((1,))],
        compiler_params=small,
        cost_estimate=cost(near_flops, near_blocks.size * 2),
        name="local_two",
    )(near_columns, *hbm(x, flat_near), *resident(p, s), *hbm(p2), stiff, plate, direct, evolve, area)

    new_p, parts = pl.pallas_call(
        close_kernel,
        out_shape=in_hbm(state) + like(((devices, 2, cols), F32)),
        in_specs=[WHOLE] * 3 + [PLAIN] + [WHOLE] + [PLAIN] * 5,
        out_specs=(PLAIN, WHOLE),
        scratch_shapes=vmem(
            halo_kind, edge_kind, state, state, state, state, coupled_kind, vector_kind, errors_kind
        )
        + [SEMS((3,))]
        + [SEMS((pairs,))] * 4,
        compiler_params=small,
        name="close",
    )(got_a, got_b, got, *hbm(edge), *resident(coupling), *hbm(p2, change, factor, area, errors))

    totals = lax.all_to_all(parts, AXIS, 0, 0).sum(axis=0)
    error_norm = jnp.sqrt(totals[0] / totals[1] + 1e-06)
    return new_p.reshape(rows, cols), new_s.reshape(rows, cols), error_norm


def solution(mesh):
    split = P(("member", "patch"))
    in_specs = (
        P(("member", "patch"), None),
        P(("member", "patch"), None),
        P(("member", "patch"), None, None, None),
        P(("member", "patch"), None),
        P("member", None, "patch"),
        P("member", None, "patch"),
        split,
        split,
        split,
        split,
        split,
    )
    out_specs = (P(("member", "patch"), None), P(("member", "patch"), None), P("member"))
    return jax.shard_map(
        on_device, mesh=mesh, in_specs=in_specs, out_specs=out_specs, check_vma=False
    )
```
